128 devices in a mesh: dp: 2 (over x_lo), fsdp: 8 (over y, core), tp: 8 (over z, x_hi).
Axes of the slice: x: 4 (x_hi: 2, x_lo: 2; x = x_hi * 2 + x_lo), y: 4, z: 4, core: 2. Of those that a mesh axis runs over, the one named last changes fastest.
Arguments:
- ref_hidden: bfloat16 [2048, 4096], P(('dp', 'fsdp', 'tp')), may hold values from -18 to 18
- proxy_hidden: bfloat16 [2048, 1024], P(('dp', 'fsdp')), may hold values from -91 to 91
- targets: int32 [2048], P(('dp', 'fsdp')), may hold values from 0 to 65535
- languages: int32 [2048], P(('dp', 'fsdp')), may hold values from 0 to 63
- ref_gain: float32 [4096], replicated, may hold values from 0.25 to 1.75
- ref_head: bfloat16 [65536, 4096], P(('fsdp', 'tp')), may hold values from -16 to 16
- proxy_gain_in: float32 [1024], replicated, may hold values from 0.25 to 1.75
- proxy_gain_out: float32 [1024], replicated, may hold values from 0.25 to 1.75
- gate_weight: bfloat16 [1024, 4096], P('fsdp', 'tp'), may hold values from -0.1875 to 0.1875
- up_weight: bfloat16 [1024, 4096], P('fsdp', 'tp'), may hold values from -0.1875 to 0.1875
- down_weight: bfloat16 [4096, 1024], P('tp', 'fsdp'), may hold values from -0.09375 to 0.09375
- proxy_head: bfloat16 [65536, 1024], P(('fsdp', 'tp')), may hold values from -16 to 16
- domain_weights: float32 [64], replicated, may hold values from 0.7 to 1.4
Outputs:
- log_weights: float32 [64], replicated
- grad_gate: float32 [1024, 4096], P('fsdp', 'tp')
- grad_up: float32 [1024, 4096], P('fsdp', 'tp')
- grad_down: float32 [4096, 1024], P('tp', 'fsdp')
- grad_head: float32 [65536, 1024], P(('fsdp', 'tp'))
The draws below stay inside these ranges and needn't reach their ends.
All inputs are finite; a program needn't handle non-finite values.
Results may differ from the reference program's by a relative error of at most 0.011.
Values may be sent and summed in bfloat16 or wider, within the bound.
A program may use at most 128 MiB of HBM per device.

```python
import math
import jax
import jax.numpy as jnp
import numpy as np
from jax import lax

D = 4096
VOCAB = 65536
PD = 1024
PF = 4096
LANGS = 64
TOKENS = 2048


def draw_ref_hidden(key, part):
    return jnp.clip(jax.random.normal(jax.random.fold_in(key, 32), (TOKENS, D), jnp.float32), -6.0, 6.0).astype(jnp.bfloat16)


def draw_proxy_hidden(key, part):
    return jnp.clip(jax.random.normal(jax.random.fold_in(key, 42), (TOKENS, PD), jnp.float32), -6.0, 6.0).astype(jnp.bfloat16)


def draw_ref_head(key, part):
    factor = 3.0 / D ** 0.5
    return (jnp.clip(jax.random.normal(jax.random.fold_in(key, 52), (VOCAB, D), jnp.float32), -6.0, 6.0) * factor).astype(jnp.bfloat16)


def draw_proxy_head(key, part):
    factor = 3.0 / PD ** 0.5
    return (jnp.clip(jax.random.normal(jax.random.fold_in(key, 62), (VOCAB, PD), jnp.float32), -6.0, 6.0) * factor).astype(jnp.bfloat16)


def with_ends(values, own_key, low, high):
    spot = [jax.random.randint(jax.random.fold_in(own_key, axis), (), 0, length) for axis, length in enumerate(values.shape)]
    widest = values.shape.index(max(values.shape))
    beside = spot[:widest] + [(spot[widest] + 1) % values.shape[widest]] + spot[widest + 1:]
    return values.at[tuple(spot)].set(low).at[tuple(beside)].set(high)


def block_scale(rng, extent, cuts, least, high):
    def one(dim, parts):
        steps = jax.random.uniform(jax.random.fold_in(jax.random.fold_in(rng, 6), dim), (parts,), jnp.float32, least / len(cuts), high / len(cuts))
        return jnp.repeat(jnp.exp(steps), extent[dim] // parts).reshape((-1,) + (1,) * (len(extent) - dim - 1))

    level = one(*cuts[0])
    for cut in cuts[1:]:
        level = level * one(*cut)
    return level


def rank_bounds(number_of, skew):
    portions = [(1 << 20) // math.isqrt(standing ** skew) + 1 for standing in range(1, number_of + 1)]
    spread = 1 + sum(portions) // (1 << 30)
    return np.cumsum(np.array([max(1, weight // spread) for weight in portions]))


def skewed_ids(own_key, extent, amount, lean):
    grid = rank_bounds(amount, lean)
    lot = jax.random.randint(jax.random.fold_in(own_key, 1), extent, 0, int(grid[amount - 1]))
    grade = jnp.searchsorted(jnp.asarray(grid, jnp.int32), lot, side="right")
    return jax.random.permutation(jax.random.fold_in(own_key, 2), amount)[grade].astype(jnp.int32)


def gaussian(rng, dims, width, bound, cuts=(), held_as=jnp.bfloat16):
    values = width * jax.random.normal(rng, dims, jnp.float32)
    if cuts:
        values = values * block_scale(rng, dims, cuts, -0.22, 0.18)
    return jnp.clip(values, -bound, bound).astype(held_as)


def setup_inputs(seed: int = 0) -> dict:
    key_list = jax.random.split(jax.random.key(seed), 14)
    ref_hidden = draw_ref_hidden(jax.random.fold_in(key_list[13], 71), 0)
    proxy_hidden = draw_proxy_hidden(jax.random.fold_in(key_list[13], 71), 0)
    targets = with_ends(skewed_ids(key_list[2], (TOKENS,), VOCAB, 2), jax.random.fold_in(key_list[2], 3), 0, VOCAB - 1).astype(jnp.int32)
    languages = with_ends(jax.random.randint(key_list[3], (TOKENS,), 0, LANGS), jax.random.fold_in(key_list[3], 1), 0, LANGS - 1).astype(jnp.int32)
    ref_gain = jnp.clip(1.0 + 0.15 * jax.random.normal(key_list[4], (D,), jnp.float32), 0.25, 1.75)
    ref_head = draw_ref_head(jax.random.fold_in(key_list[13], 71), 0)
    proxy_gain_in = jnp.clip(1.0 + 0.15 * jax.random.normal(key_list[6], (PD,), jnp.float32), 0.25, 1.75)
    proxy_gain_out = jnp.clip(1.0 + 0.15 * jax.random.normal(key_list[7], (PD,), jnp.float32), 0.25, 1.75)
    gate_weight = gaussian(key_list[8], (PD, PF), PD ** -0.5, 0.1875, ((0, 8), (1, 8)))
    up_weight = gaussian(key_list[9], (PD, PF), PD ** -0.5, 0.1875, ((0, 8), (1, 8)))
    down_weight = gaussian(key_list[10], (PF, PD), PF ** -0.5, 0.09375, ((0, 8), (1, 8)))
    proxy_head = draw_proxy_head(jax.random.fold_in(key_list[13], 71), 0)
    domain_weights = jnp.clip(jnp.exp(jax.random.uniform(key_list[12], (LANGS,), jnp.float32, math.log(0.7), math.log(1.4))), 0.7, 1.4)
    return {"ref_hidden": ref_hidden, "proxy_hidden": proxy_hidden, "targets": targets, "languages": languages, "ref_gain": ref_gain, "ref_head": ref_head, "proxy_gain_in": proxy_gain_in, "proxy_gain_out": proxy_gain_out, "gate_weight": gate_weight, "up_weight": up_weight, "down_weight": down_weight, "proxy_head": proxy_head, "domain_weights": domain_weights}


EPSILON = 1e-05
STEP_SIZE = 1.0
SMOOTHING = 0.001

def rms_scale(values, gain_vec):
    values = values.astype(jnp.float32)
    return values * lax.rsqrt(lax.optimization_barrier(jnp.mean(values * values, axis=-1, keepdims=True)) + EPSILON) * gain_vec

def row_logits(row_block, head):
    return lax.dot_general(row_block, head, (((1,), (1,)), ((), ())), preferred_element_type=jnp.float32)

def vocab_stats(normed, head, targets):
    row_count = normed.shape[0]
    block_rows = math.gcd(row_count, 256)
    vocab_ids = jnp.arange(head.shape[0], dtype=jnp.int32)

    def one_block(inputs):
        part_rows, part_targets = inputs
        logits = row_logits(part_rows, head)
        high_val = lax.optimization_barrier(jnp.max(logits, axis=1))
        exp_total = lax.optimization_barrier(jnp.sum(jnp.exp(logits - high_val[:, None]), axis=1))
        picked = lax.optimization_barrier(jnp.sum(jnp.where(vocab_ids[None, :] == part_targets[:, None], logits, 0.0), axis=1))
        return (high_val + jnp.log(exp_total), picked)
    lse_vals, picked = lax.map(one_block, (normed.reshape(row_count // block_rows, block_rows, normed.shape[1]), targets.reshape(row_count // block_rows, block_rows)))
    return (lse_vals.reshape(row_count), picked.reshape(row_count))

def head_backward(final_normed, head, targets, lse_vals, token_weight):
    row_count = final_normed.shape[0]
    block_rows = math.gcd(row_count, 256)
    vocab_ids = jnp.arange(head.shape[0], dtype=jnp.int32)

    def scan_step(grad_acc, inputs):
        part_rows, part_targets, part_lse, part_weight = inputs
        logits = row_logits(part_rows, head)
        onehot = (vocab_ids[None, :] == part_targets[:, None]).astype(logits.dtype)
        dlogits = (part_weight[:, None] * (jnp.exp(logits - part_lse[:, None]) - onehot)).astype(jnp.bfloat16)
        grad_acc = grad_acc + lax.dot_general(dlogits, part_rows, (((0,), (0,)), ((), ())), preferred_element_type=jnp.float32)
        return (grad_acc, jnp.dot(dlogits, head, preferred_element_type=jnp.float32))
    blocks = row_count // block_rows
    init = jnp.zeros((head.shape[0], final_normed.shape[1]), jnp.float32)
    grad_head, d_final = lax.scan(scan_step, init, (final_normed.reshape(blocks, block_rows, final_normed.shape[1]), targets.reshape(blocks, block_rows), lse_vals.reshape(blocks, block_rows), token_weight.reshape(blocks, block_rows)))
    return (grad_head, d_final.reshape(row_count, final_normed.shape[1]))

def norm_backward(mid_sum, gain_vec, d_out):
    inv_rms = lax.rsqrt(lax.optimization_barrier(jnp.mean(mid_sum * mid_sum, axis=1, keepdims=True)) + EPSILON)
    scaled_grad = d_out * gain_vec
    inner_mean = lax.optimization_barrier(jnp.mean(mid_sum * scaled_grad, axis=1, keepdims=True))
    return (inv_rms * scaled_grad - mid_sum * inv_rms * inv_rms * inv_rms * inner_mean).astype(jnp.bfloat16)

def gate_grads(d_act, gate_pre, up_pre):
    sigmoid_g = jax.nn.sigmoid(gate_pre)
    d_gate = (d_act * up_pre * sigmoid_g * (1.0 + gate_pre * (1.0 - sigmoid_g))).astype(jnp.bfloat16)
    d_up = (d_act * gate_pre * sigmoid_g).astype(jnp.bfloat16)
    return (d_gate, d_up)

def domain_update(domain_weights, lang_excess, lang_count):
    excess = lang_excess / jnp.maximum(lang_count, 1.0)
    mixture = jax.nn.softmax(jnp.log(domain_weights) + STEP_SIZE * excess)
    return (1.0 - SMOOTHING) * mixture + SMOOTHING / domain_weights.shape[0]

def reference(ref_hidden, proxy_hidden, targets, languages, ref_gain, ref_head, proxy_gain_in, proxy_gain_out, gate_weight, up_weight, down_weight, proxy_head, domain_weights):
    normed_in = rms_scale(proxy_hidden, proxy_gain_in).astype(jnp.bfloat16)
    gate_pre = jnp.dot(normed_in, gate_weight, preferred_element_type=jnp.float32)
    up_pre = jnp.dot(normed_in, up_weight, preferred_element_type=jnp.float32)
    hidden_act = (gate_pre * jax.nn.sigmoid(gate_pre) * up_pre).astype(jnp.bfloat16)
    mid_sum = proxy_hidden.astype(jnp.float32) + jnp.dot(hidden_act, down_weight, preferred_element_type=jnp.float32)
    final_normed = rms_scale(mid_sum, proxy_gain_out).astype(jnp.bfloat16)
    ref_normed = rms_scale(ref_hidden, ref_gain).astype(jnp.bfloat16)
    ref_lse, ref_pick = vocab_stats(ref_normed, ref_head, targets)
    proxy_lse, proxy_pick = vocab_stats(final_normed, proxy_head, targets)
    excess_tok = jnp.maximum(proxy_lse - proxy_pick - (ref_lse - ref_pick), 0.0)
    lang_ids = jnp.arange(LANGS, dtype=jnp.int32)
    member = (languages[:, None] == lang_ids[None, :]).astype(jnp.float32)
    lang_count = lax.optimization_barrier(jnp.sum(member, axis=0))
    new_weights = domain_update(domain_weights, lax.optimization_barrier(jnp.sum(member * excess_tok[:, None], axis=0)), lang_count)
    token_weight = lax.optimization_barrier(jnp.sum(member * (new_weights / jnp.maximum(lang_count, 1.0))[None, :], axis=1)) * TOKENS
    grad_head, d_final = head_backward(final_normed, proxy_head, targets, proxy_lse, token_weight)
    d_mid = norm_backward(mid_sum, proxy_gain_out, d_final)
    grad_down = lax.dot_general(hidden_act, d_mid, (((0,), (0,)), ((), ())), preferred_element_type=jnp.float32)
    d_act = lax.dot_general(d_mid, down_weight, (((1,), (1,)), ((), ())), preferred_element_type=jnp.float32)
    d_gate, d_up = gate_grads(d_act, gate_pre, up_pre)
    grad_gate = lax.dot_general(normed_in, d_gate, (((0,), (0,)), ((), ())), preferred_element_type=jnp.float32)
    grad_up = lax.dot_general(normed_in, d_up, (((0,), (0,)), ((), ())), preferred_element_type=jnp.float32)
    return (jnp.log(new_weights), grad_gate, grad_up, grad_down, grad_head)
```

```python
import functools

import jax
import jax.numpy as jnp
from jax import lax
from jax.experimental import pallas as pl
from jax.experimental.pallas import tpu as pltpu
from jax.sharding import PartitionSpec as P

EPSILON = 1e-05
STEP_SIZE = 1.0
SMOOTHING = 0.001
LANGS = 64
MESH = pl.DeviceIdType.MESH
F32, BF16 = jnp.float32, jnp.bfloat16


class Place:
    def __init__(self):
        self.dp = lax.axis_index("dp")
        f, t = lax.axis_index("fsdp"), lax.axis_index("tp")
        self.f, self.t = f, t
        self.y, self.c = lax.div(f, 2), lax.rem(f, 2)
        self.z, self.xh = lax.div(t, 2), lax.rem(t, 2)
        self.p = self.xh
        c = self.c
        self.a = (1 - c) * self.y + c * self.z
        self.b = (1 - c) * self.z + c * self.y

    def at(self, dp=None, y=None, z=None, xh=None, c=None):
        pick = lambda new, old: old if new is None else new
        dp, y, z = pick(dp, self.dp), pick(y, self.y), pick(z, self.z)
        xh, c = pick(xh, self.xh), pick(c, self.c)
        return {"dp": dp, "fsdp": y * 2 + c, "tp": z * 2 + xh}

    def on_a(self, a):
        c = self.c
        return self.at(y=(1 - c) * a + c * self.y, z=(1 - c) * self.z + c * a)

    def on_b(self, b):
        c = self.c
        return self.at(y=(1 - c) * self.y + c * b, z=(1 - c) * b + c * self.z)

    def core(self):
        return self.at(c=1 - self.c)

    def partner(self):
        return self.at(dp=1 - self.dp, xh=1 - self.xh)

    def neighbour(self):
        return self.at(dp=1 - self.dp)

    def opposite(self):
        return self.at(xh=1 - self.xh)


class Copies:
    def __init__(self, send, recv):
        self.send, self.recv, self.n, self.all = send, recv, 0, []

    def start(self, src, dst, to):
        copy = pltpu.make_async_remote_copy(
            src_ref=src,
            dst_ref=dst,
            send_sem=self.send.at[self.n],
            recv_sem=self.recv.at[self.n],
            device_id=to,
            device_id_type=MESH,
        )
        copy.start()
        self.n += 1
        self.all.append(copy)
        return copy

    def drain(self):
        for copy in self.all:
            copy.wait_send()


def greet(peers):
    barrier = pltpu.get_barrier_semaphore()
    for peer in peers:
        pl.semaphore_signal(barrier, inc=1, device_id=peer, device_id_type=MESH)
    pl.semaphore_wait(barrier, len(peers))


def ring(i, k):
    return lax.rem(i + k, 4)


def gather_body(wide, weights, *refs):
    n = len(wide)
    m = 2 if weights else 0
    ins, w_ins = refs[:n], refs[n : n + m]
    outs, w_outs = refs[n + m : 2 * n + m], refs[2 * n + m : 2 * n + 2 * m]
    send, recv, local = refs[2 * n + 2 * m :]
    me = Place()
    a, b, c, p = me.a, me.b, me.c, me.p
    go = Copies(send, recv)
    right_a, left_a = me.on_a(ring(a, 1)), me.on_a(ring(a, 3))
    right_b, left_b = me.on_b(ring(b, 1)), me.on_b(ring(b, 3))
    peers = [me.core(), me.partner(), right_a, left_a, right_b, left_b]
    if any(wide):
        peers += [me.neighbour(), me.opposite()]
    if weights:
        others = [lax.rem(me.f + j, 8) for j in range(1, 8)]
        kept = {"dp": me.dp, "tp": me.t}
        peers = peers[1:] + [{**kept, "fsdp": o} for o in others]
    greet(peers)

    def block(i, g, *at):
        return outs[i].at[(g, *at)] if wide[i] else outs[i].at[at]

    sides = [range(2) if w else range(1) for w in wide]
    locals_, first = [], []
    for i in range(n):
        mine = pltpu.make_async_copy(ins[i], block(i, 0, c, b, a, p), local.at[i])
        mine.start()
        locals_.append(mine)
        first.append(go.start(ins[i], block(i, 0, c, b, a, p), me.partner()))
        if wide[i]:
            first.append(go.start(ins[i], block(i, 1, c, b, a, p), me.neighbour()))
            first.append(go.start(ins[i], block(i, 1, c, b, a, p), me.opposite()))
    w_copies = []
    for k in range(m):
        mine = pltpu.make_async_copy(w_ins[k].at[me.f], w_outs[k].at[me.f], local.at[n + k])
        mine.start()
        locals_.append(mine)
        for o in others if weights else ():
            w_copies.append(go.start(w_ins[k].at[o], w_outs[k].at[me.f], {**kept, "fsdp": o}))
    for copy in first:
        copy.wait_recv()
    for copy in locals_:
        copy.wait()
    steps = [(i, g) for i in range(n) for g in sides[i]]
    near = []
    for i, g in steps:
        unit = block(i, g, c, b, a)
        near.append((go.start(unit, unit, right_a), go.start(unit, unit, left_a)))
    last = []
    for (i, g), (to_right, to_left) in zip(steps, near):
        to_right.wait_recv()
        half = block(i, g, c, b, ring(a, 3), 0)
        last.append(go.start(half, half, right_a))
        to_left.wait_recv()
        half = block(i, g, c, b, ring(a, 1), 1)
        last.append(go.start(half, half, left_a))
    for copy in last:
        copy.wait_recv()
    near, across = [], []
    for i, g in steps:
        unit = block(i, g, c, b)
        near.append((go.start(unit, unit, right_b), go.start(unit, unit, left_b)))
        across.append(go.start(unit, unit, me.core()))
    last = []
    for (i, g), (to_right, to_left) in zip(steps, near):
        to_right.wait_recv()
        half = block(i, g, c, ring(b, 3), pl.ds(0, 2))
        last.append(go.start(half, half, right_b))
        to_left.wait_recv()
        half = block(i, g, c, ring(b, 1), pl.ds(2, 2))
        last.append(go.start(half, half, left_b))
        for k in (3, 1):
            unit = block(i, g, c, ring(b, k))
            across.append(go.start(unit, unit, me.core()))
    for copy in last:
        copy.wait_recv()
    for i, g in steps:
        unit = block(i, g, c, ring(b, 2))
        across.append(go.start(unit, unit, me.core()))
    for copy in across + w_copies:
        copy.wait_recv()
    go.drain()


def gather(blocks, wide, weights, collective_id):
    n, m = len(blocks), len(weights)
    shapes = [
        jax.ShapeDtypeStruct(((2,) if w else ()) + (2, 4, 4, 2) + x.shape, x.dtype)
        for x, w in zip(blocks, wide)
    ] + [jax.ShapeDtypeStruct(w.shape, w.dtype) for w in weights]
    count = sum(27 if w else 13 for w in wide) + 7 * m
    vmem = pl.BlockSpec(memory_space=pltpu.VMEM)
    hbm = pl.BlockSpec(memory_space=pl.ANY)
    return pl.pallas_call(
        functools.partial(gather_body, tuple(wide), bool(weights)),
        out_shape=shapes,
        in_specs=[vmem] * (n + m),
        out_specs=[hbm] * (n + m),
        scratch_shapes=[
            pltpu.SemaphoreType.DMA((count,)),
            pltpu.SemaphoreType.DMA((count,)),
            pltpu.SemaphoreType.DMA((n + m,)),
        ],
        compiler_params=pltpu.CompilerParams(
            collective_id=collective_id, has_side_effects=True
        ),
        name="gather%d" % collective_id,
    )(*blocks, *weights)


def scatter_body(x, out, r0, acc, hr, hl, ur, ul, acc1, ra, acc2, give, rp, send, recv):
    me = Place()
    a, b, c, p = me.a, me.b, me.c, me.p
    go = Copies(send, recv)
    right_a, left_a, far_a = (me.on_a(ring(a, k)) for k in (1, 3, 2))
    right_b, left_b = me.on_b(ring(b, 1)), me.on_b(ring(b, 3))
    greet([me.core(), me.partner(), right_a, left_a, far_a, right_b, left_b])
    halves = x.shape[2] // 2
    lo, hi = pl.ds(0, halves), pl.ds(halves, halves)
    order = (2, 1, 3, 0)
    got = []
    for k in order:
        j = ring(a, k)
        got.append(go.start(x.at[1 - c, j], r0.at[j], me.core()))

    def join(k):
        j = ring(b, order[k])
        got[k].wait_recv()
        acc[j] = (x[c, j].astype(F32) + r0[j].astype(F32)).astype(BF16)
        return j

    far = join(0)
    s_r = go.start(acc.at[far, lo], hr, right_b)
    s_l = go.start(acc.at[far, hi], hl, left_b)
    near_r = join(1)
    t_r = go.start(acc.at[near_r, hi], ul.at[hi], right_b)
    near_l = join(2)
    t_l = go.start(acc.at[near_l, lo], ur.at[lo], left_b)
    s_r.wait_recv()
    acc[near_r, lo] = (acc[near_r, lo].astype(F32) + hr[...].astype(F32)).astype(BF16)
    v_r = go.start(acc.at[near_r, lo], ul.at[lo], right_b)
    s_l.wait_recv()
    acc[near_l, hi] = (acc[near_l, hi].astype(F32) + hl[...].astype(F32)).astype(BF16)
    v_l = go.start(acc.at[near_l, hi], ur.at[hi], left_b)
    own = join(3)
    for copy in (t_r, t_l, v_r, v_l):
        copy.wait_recv()
    total = acc[own].astype(F32) + ul[...].astype(F32) + ur[...].astype(F32)
    acc1[...] = total.astype(BF16).reshape(acc1.shape)
    sends = [
        go.start(acc1.at[ring(a, k)], ra.at[i], to)
        for i, (k, to) in enumerate(((2, far_a), (1, right_a), (3, left_a)))
    ]
    for copy in sends:
        copy.wait_recv()
    total = acc1[a].astype(F32)
    for i in range(3):
        total = total + ra[i].astype(F32)
    acc2[...] = total.reshape(acc2.shape)
    give[...] = acc2[1 - p].astype(BF16)
    swap = go.start(give, rp, me.partner())
    swap.wait_recv()
    out[...] = acc2[p] + rp[...].astype(F32)
    go.drain()


def scatter(x, collective_id):
    rows, width = x.shape
    unit = rows // 8
    block = rows // 64
    x = x.reshape(2, 4, unit, width)
    vmem = pl.BlockSpec(memory_space=pltpu.VMEM)
    return pl.pallas_call(
        scatter_body,
        out_shape=jax.ShapeDtypeStruct((block, width), F32),
        in_specs=[vmem],
        out_specs=vmem,
        scratch_shapes=[
            pltpu.VMEM((4, unit, width), BF16),
            pltpu.VMEM((4, unit, width), BF16),
            pltpu.VMEM((unit // 2, width), BF16),
            pltpu.VMEM((unit // 2, width), BF16),
            pltpu.VMEM((unit, width), BF16),
            pltpu.VMEM((unit, width), BF16),
            pltpu.VMEM((4, unit // 4, width), BF16),
            pltpu.VMEM((3, unit // 4, width), BF16),
            pltpu.VMEM((2, block, width), F32),
            pltpu.VMEM((block, width), BF16),
            pltpu.VMEM((block, width), BF16),
            pltpu.SemaphoreType.DMA((14,)),
            pltpu.SemaphoreType.DMA((14,)),
        ],
        compiler_params=pltpu.CompilerParams(
            collective_id=collective_id, has_side_effects=True
        ),
        name="scatter%d" % collective_id,
    )(x)


def join_all(pieces):
    out = []
    for base in (0, 24):
        high = functools.reduce(jnp.maximum, [s[base : base + 8] for s in pieces])
        total = pick = None
        for s in pieces:
            t = s[base + 8 : base + 16] * jnp.exp(s[base : base + 8] - high)
            k = s[base + 16 : base + 24]
            total, pick = (t, k) if total is None else (total + t, pick + k)
        out += [high, total, pick]
    return jnp.concatenate(out, axis=0)


def stats_body(st, lang, dw, lse, tw, logw, slot_c, slot_z, slot_y, slot_p, pack, other, send, recv):
    me = Place()
    go = Copies(send, recv)
    on_z = [me.at(z=ring(me.z, k)) for k in (1, 2, 3)]
    on_y = [me.at(y=ring(me.y, k)) for k in (1, 2, 3)]
    greet([me.core(), me.partner(), me.neighbour(), *on_z, *on_y])
    mine = st[...]
    for slots, at, peers in (
        (slot_c, me.c, [me.core()]),
        (slot_z, me.z, on_z),
        (slot_y, me.y, on_y),
        (slot_p, me.p, [me.partner()]),
    ):
        slots[at] = mine
        sent = [go.start(slots.at[at], slots.at[at], to) for to in peers]
        for copy in sent:
            copy.wait_recv()
        mine = join_all([slots[j] for j in range(slots.shape[0])])
    ref_loss = mine[0:8] + jnp.log(mine[8:16]) - mine[16:24]
    proxy_lse = mine[24:32] + jnp.log(mine[32:40])
    excess = jnp.maximum(proxy_lse - mine[40:48] - ref_loss, 0.0)
    own_lang = lang[0:8]
    for l in range(LANGS):
        here = own_lang == l
        pack[l : l + 1] = jnp.sum(jnp.where(here, excess, 0.0), axis=0, keepdims=True)
        pack[LANGS + l : LANGS + l + 1] = jnp.sum(
            jnp.where(here, 1.0, 0.0), axis=0, keepdims=True
        )
    pack[2 * LANGS : 2 * LANGS + 8] = proxy_lse
    swap = go.start(pack, other, me.neighbour())
    swap.wait_recv()
    lse[0:8] = proxy_lse
    lse[8:16] = other[2 * LANGS : 2 * LANGS + 8]
    sums = jnp.sum(pack[0 : 2 * LANGS] + other[0 : 2 * LANGS], axis=1, keepdims=True)
    sums = jnp.broadcast_to(sums, (2 * LANGS, 128))
    count = jnp.maximum(sums[LANGS:], 1.0)
    score = jnp.log(dw[...]) + STEP_SIZE * (sums[:LANGS] / count)
    score = jnp.exp(score - jnp.max(score, axis=0, keepdims=True))
    mixture = score / jnp.sum(score, axis=0, keepdims=True)
    new = (1.0 - SMOOTHING) * mixture + SMOOTHING / LANGS
    logw[...] = jnp.log(new)
    share = new / count * 2048.0
    every = lang[...]
    weight = jnp.zeros(every.shape, F32)
    for l in range(LANGS):
        weight = jnp.where(every == l, share[l : l + 1], weight)
    tw[...] = weight
    go.drain()


def join_stats(stats, lang, domain_weights, collective_id):
    vmem = pl.BlockSpec(memory_space=pltpu.VMEM)
    shape = stats.shape
    return pl.pallas_call(
        stats_body,
        out_shape=[
            jax.ShapeDtypeStruct((16, 128), F32),
            jax.ShapeDtypeStruct((16, 128), F32),
            jax.ShapeDtypeStruct((LANGS, 128), F32),
        ],
        in_specs=[vmem] * 3,
        out_specs=[vmem] * 3,
        scratch_shapes=[
            pltpu.VMEM((2, *shape), F32),
            pltpu.VMEM((4, *shape), F32),
            pltpu.VMEM((4, *shape), F32),
            pltpu.VMEM((2, *shape), F32),
            pltpu.VMEM((2 * LANGS + 8, 128), F32),
            pltpu.VMEM((2 * LANGS + 8, 128), F32),
            pltpu.SemaphoreType.DMA((9,)),
            pltpu.SemaphoreType.DMA((9,)),
        ],
        compiler_params=pltpu.CompilerParams(
            collective_id=collective_id, has_side_effects=True
        ),
        name="stats",
    )(stats, lang, jnp.broadcast_to(domain_weights[:, None], (LANGS, 128)))


def home_body(gu, dn, gate, up, down, o_gu, o_dn, s_gu, s_dn, r_gu, r_dn, send, recv):
    me = Place()
    go = Copies(send, recv)
    others = [lax.rem(me.f + j, 8) for j in range(1, 8)]
    to = [{"dp": me.dp, "fsdp": o, "tp": me.t} for o in others]
    greet([me.neighbour(), *to])
    first = [go.start(gu, o_gu, me.neighbour()), go.start(dn, o_dn, me.neighbour())]
    for copy in first:
        copy.wait_recv()
    for j in range(8):
        s_gu[j] = (gu[j].astype(F32) + o_gu[j].astype(F32)).astype(BF16)
        s_dn[j] = (dn[j].astype(F32) + o_dn[j].astype(F32)).astype(BF16)
    sent = []
    for o, dev in zip(others, to):
        sent.append(go.start(s_gu.at[o], r_gu.at[me.f], dev))
        sent.append(go.start(s_dn.at[o], r_dn.at[me.f], dev))
    r_gu[me.f] = s_gu[me.f]
    r_dn[me.f] = s_dn[me.f]
    for copy in sent:
        copy.wait_recv()
    for j in range(8):
        both = r_gu[j].astype(F32)
        gate[:, 64 * j : 64 * (j + 1)] = both[:, :64]
        up[:, 64 * j : 64 * (j + 1)] = both[:, 64:]
        down[64 * j : 64 * (j + 1)] = r_dn[j].astype(F32)
    go.drain()


def home(gu, dn, collective_id):
    vmem = pl.BlockSpec(memory_space=pltpu.VMEM)
    return pl.pallas_call(
        home_body,
        out_shape=[
            jax.ShapeDtypeStruct((128, 512), F32),
            jax.ShapeDtypeStruct((128, 512), F32),
            jax.ShapeDtypeStruct((512, 128), F32),
        ],
        in_specs=[vmem] * 2,
        out_specs=[vmem] * 3,
        scratch_shapes=[pltpu.VMEM(gu.shape, BF16), pltpu.VMEM(dn.shape, BF16)] * 3
        + [pltpu.SemaphoreType.DMA((16,)), pltpu.SemaphoreType.DMA((16,))],
        compiler_params=pltpu.CompilerParams(
            collective_id=collective_id, has_side_effects=True
        ),
        name="home",
    )(gu, dn)


def rms_scale(values, gain_vec):
    values = values.astype(F32)
    return (
        values * lax.rsqrt(jnp.mean(values * values, axis=-1, keepdims=True) + EPSILON) * gain_vec
    )


def row_logits(row_block, head):
    return lax.dot_general(row_block, head, (((1,), (1,)), ((), ())), preferred_element_type=F32)


def piece_stats(logits, part_targets, vocab_start):
    vocab_cols = vocab_start + jnp.arange(logits.shape[1], dtype=jnp.int32)
    high_val = jnp.max(logits, axis=1)
    exp_total = jnp.sum(jnp.exp(logits - high_val[:, None]), axis=1)
    picked = jnp.sum(jnp.where(vocab_cols[None, :] == part_targets[:, None], logits, 0.0), axis=1)
    return (high_val, exp_total, picked)


def norm_backward(mid_sum, gain_vec, d_out):
    inv_rms = lax.rsqrt(jnp.mean(mid_sum * mid_sum, axis=1, keepdims=True) + EPSILON)
    scaled_grad = d_out * gain_vec
    inner_mean = jnp.mean(mid_sum * scaled_grad, axis=1, keepdims=True)
    return (inv_rms * scaled_grad - mid_sum * inv_rms * inv_rms * inv_rms * inner_mean).astype(BF16)


def gate_grads(d_act, gate_pre, up_pre):
    sigmoid_g = jax.nn.sigmoid(gate_pre)
    d_gate = (d_act * up_pre * sigmoid_g * (1.0 + gate_pre * (1.0 - sigmoid_g))).astype(BF16)
    d_up = (d_act * gate_pre * sigmoid_g).astype(BF16)
    return (d_gate, d_up)


def local(
    ref_hidden,
    proxy_hidden,
    targets,
    languages,
    ref_gain,
    ref_head,
    proxy_gain_in,
    proxy_gain_out,
    gate_weight,
    up_weight,
    down_weight,
    proxy_head,
    domain_weights,
):
    tp = lax.axis_index("tp")
    vocab_rows = ref_head.shape[0]
    vocab_start = lax.axis_index(("fsdp", "tp")) * vocab_rows
    mine = lambda v: lax.dynamic_slice_in_dim(v, tp * 16, 16, 0)
    hidden = mine(proxy_hidden)
    normed_own = rms_scale(hidden, proxy_gain_in).astype(BF16)
    ref_own = rms_scale(ref_hidden, ref_gain).astype(BF16)
    ids = jnp.stack([mine(targets), mine(languages)])
    ids = jnp.pad(ids, ((0, 6), (0, 112)))
    rows = gate_weight.shape[0]
    gu_own = jnp.concatenate(
        [w.reshape(rows, 8, 64).transpose(1, 0, 2) for w in (gate_weight, up_weight)], axis=2
    )
    dn_own = down_weight.reshape(8, 64, 128)
    ids, normed_in, ref_all, gu_w, dn_w = gather(
        (ids, normed_own, ref_own), (True, False, False), (gu_own, dn_own), 1
    )
    group_targets = ids[..., 0, :16].reshape(2048)
    group_langs = ids[..., 1, :16].reshape(16, 128)
    normed_in = normed_in.reshape(1024, 1024)
    ref_all = ref_all.reshape(1024, 4096)
    gu_w = gu_w.reshape(1024, 128)
    pre = jnp.dot(normed_in, gu_w, preferred_element_type=F32)
    gate_pre, up_pre = pre[:, :64], pre[:, 64:]
    hidden_act = (gate_pre * jax.nn.sigmoid(gate_pre) * up_pre).astype(BF16)
    down_w = dn_w.transpose(1, 0, 2).reshape(64, 1024)
    ffn_part = jnp.dot(hidden_act, down_w, preferred_element_type=F32).astype(BF16)
    mid_sum = hidden.astype(F32) + scatter(ffn_part, 2)
    final_own = rms_scale(mid_sum, proxy_gain_out).astype(BF16)
    (final_all,) = gather((final_own,), (True,), (), 3)
    final_all = final_all.reshape(2048, 1024)
    proxy_logits = row_logits(final_all, proxy_head)
    proxy_stats = piece_stats(proxy_logits[:1024], group_targets[:1024], vocab_start)
    logits = row_logits(ref_all, ref_head)
    ref_stats = piece_stats(logits, group_targets[:1024], vocab_start)
    stats = jnp.stack(ref_stats + proxy_stats).reshape(48, 128)
    lse, token_weight, log_weights = join_stats(stats, group_langs, domain_weights, 4)
    lse, token_weight = lse.reshape(2048), token_weight.reshape(2048)
    vocab_cols = vocab_start + jnp.arange(vocab_rows, dtype=jnp.int32)
    onehot = (vocab_cols[None, :] == group_targets[:, None]).astype(F32)
    dlogits = (token_weight[:, None] * (jnp.exp(proxy_logits - lse[:, None]) - onehot)).astype(BF16)
    d_part = jnp.dot(dlogits[:1024], proxy_head, preferred_element_type=F32).astype(BF16)
    d_final = scatter(d_part, 5)
    grad_head = lax.dot_general(
        dlogits, final_all, (((0,), (0,)), ((), ())), preferred_element_type=F32
    )
    d_own = norm_backward(mid_sum, proxy_gain_out, d_final)
    (d_mid,) = gather((d_own,), (False,), (), 6)
    d_mid = d_mid.reshape(1024, 1024)
    grad_down = lax.dot_general(
        hidden_act, d_mid, (((0,), (0,)), ((), ())), preferred_element_type=F32
    )
    d_act = lax.dot_general(d_mid, down_w, (((1,), (1,)), ((), ())), preferred_element_type=F32)
    d_both = jnp.concatenate(gate_grads(d_act, gate_pre, up_pre), axis=1)
    grad_gu = lax.dot_general(
        normed_in, d_both, (((0,), (0,)), ((), ())), preferred_element_type=F32
    )
    grad_gu = grad_gu.astype(BF16).reshape(8, 128, 128)
    grad_down = grad_down.astype(BF16).reshape(64, 8, 128).transpose(1, 0, 2)
    grad_gate, grad_up, grad_down = home(grad_gu, grad_down, 7)
    return (log_weights[:, 0], grad_gate, grad_up, grad_down, grad_head)


def solution(mesh):
    in_specs = (
        P(("dp", "fsdp", "tp"), None),
        P(("dp", "fsdp"), None),
        P(("dp", "fsdp")),
        P(("dp", "fsdp")),
        P(),
        P(("fsdp", "tp"), None),
        P(),
        P(),
        P("fsdp", "tp"),
        P("fsdp", "tp"),
        P("tp", "fsdp"),
        P(("fsdp", "tp"), None),
        P(),
    )
    out_specs = (P(), P("fsdp", "tp"), P("fsdp", "tp"), P("tp", "fsdp"), P(("fsdp", "tp"), None))
    return jax.shard_map(local, mesh=mesh, in_specs=in_specs, out_specs=out_specs, check_vma=False)
```

```python
import functools

import jax
import jax.numpy as jnp
from jax import lax
from jax.experimental import pallas as pl
from jax.experimental.pallas import tpu as pltpu
from jax.sharding import PartitionSpec as P

EPSILON = 1e-05
STEP_SIZE = 1.0
SMOOTHING = 0.001
LANGS = 64
MESH = pl.DeviceIdType.MESH
F32, BF16 = jnp.float32, jnp.bfloat16


class Place:
    def __init__(self):
        self.dp = lax.axis_index("dp")
        f, t = lax.axis_index("fsdp"), lax.axis_index("tp")
        self.f, self.t = f, t
        self.y, self.c = lax.div(f, 2), lax.rem(f, 2)
        self.z, self.xh = lax.div(t, 2), lax.rem(t, 2)
        self.p = self.xh
        c = self.c
        self.a = (1 - c) * self.y + c * self.z
        self.b = (1 - c) * self.z + c * self.y

    def at(self, dp=None, y=None, z=None, xh=None, c=None):
        pick = lambda new, old: old if new is None else new
        dp, y, z = pick(dp, self.dp), pick(y, self.y), pick(z, self.z)
        xh, c = pick(xh, self.xh), pick(c, self.c)
        return {"dp": dp, "fsdp": y * 2 + c, "tp": z * 2 + xh}

    def on_a(self, a):
        c = self.c
        return self.at(y=(1 - c) * a + c * self.y, z=(1 - c) * self.z + c * a)

    def on_b(self, b):
        c = self.c
        return self.at(y=(1 - c) * self.y + c * b, z=(1 - c) * b + c * self.z)

    def on_ab(self, a, b):
        c = self.c
        return self.at(y=(1 - c) * a + c * b, z=(1 - c) * b + c * a)

    def core(self):
        return self.at(c=1 - self.c)

    def partner(self):
        return self.at(dp=1 - self.dp, xh=1 - self.xh)

    def neighbour(self):
        return self.at(dp=1 - self.dp)

    def opposite(self):
        return self.at(xh=1 - self.xh)


class Copies:
    def __init__(self, send, recv):
        self.send, self.recv, self.n, self.all = send, recv, 0, []

    def start(self, src, dst, to):
        copy = pltpu.make_async_remote_copy(
            src_ref=src,
            dst_ref=dst,
            send_sem=self.send.at[self.n],
            recv_sem=self.recv.at[self.n],
            device_id=to,
            device_id_type=MESH,
        )
        copy.start()
        self.n += 1
        self.all.append(copy)
        return copy

    def drain(self):
        for copy in self.all:
            copy.wait_send()


def greet(peers):
    barrier = pltpu.get_barrier_semaphore()
    for peer in peers:
        pl.semaphore_signal(barrier, inc=1, device_id=peer, device_id_type=MESH)
    pl.semaphore_wait(barrier, len(peers))


def ring(i, k):
    return lax.rem(i + k, 4)


def gather_body(wide, weights, *refs):
    n = len(wide)
    m = 2 if weights else 0
    ins, w_ins = refs[:n], refs[n : n + m]
    outs, w_outs = refs[n + m : 2 * n + m], refs[2 * n + m : 2 * n + 2 * m]
    send, recv, local = refs[2 * n + 2 * m :]
    me = Place()
    a, b, c, p = me.a, me.b, me.c, me.p
    go = Copies(send, recv)
    right_a, left_a = me.on_a(ring(a, 1)), me.on_a(ring(a, 3))
    right_b, left_b = me.on_b(ring(b, 1)), me.on_b(ring(b, 3))
    peers = [me.core(), me.partner(), right_a, left_a, right_b, left_b]
    if any(wide):
        peers += [me.neighbour(), me.opposite()]
    if weights:
        others = [lax.rem(me.f + j, 8) for j in range(1, 8)]
        kept = {"dp": me.dp, "tp": me.t}
        peers = peers[1:] + [{**kept, "fsdp": o} for o in others]
    greet(peers)

    def block(i, g, *at):
        return outs[i].at[(g, *at)] if wide[i] else outs[i].at[at]

    sides = [range(2) if w else range(1) for w in wide]
    locals_, first = [], []
    for i in range(n):
        mine = pltpu.make_async_copy(ins[i], block(i, 0, c, b, a, p), local.at[i])
        mine.start()
        locals_.append(mine)
        first.append(go.start(ins[i], block(i, 0, c, b, a, p), me.partner()))
        if wide[i]:
            first.append(go.start(ins[i], block(i, 1, c, b, a, p), me.neighbour()))
            first.append(go.start(ins[i], block(i, 1, c, b, a, p), me.opposite()))
    w_copies = []
    for k in range(m):
        mine = pltpu.make_async_copy(w_ins[k].at[me.f], w_outs[k].at[me.f], local.at[n + k])
        mine.start()
        locals_.append(mine)
        for o in others if weights else ():
            w_copies.append(go.start(w_ins[k].at[o], w_outs[k].at[me.f], {**kept, "fsdp": o}))
    for copy in first:
        copy.wait_recv()
    for copy in locals_:
        copy.wait()
    steps = [(i, g) for i in range(n) for g in sides[i]]
    near = []
    for i, g in steps:
        unit = block(i, g, c, b, a)
        near.append((go.start(unit, unit, right_a), go.start(unit, unit, left_a)))
    last = []
    for (i, g), (to_right, to_left) in zip(steps, near):
        to_right.wait_recv()
        half = block(i, g, c, b, ring(a, 3), 0)
        last.append(go.start(half, half, right_a))
        to_left.wait_recv()
        half = block(i, g, c, b, ring(a, 1), 1)
        last.append(go.start(half, half, left_a))
    for copy in last:
        copy.wait_recv()
    near, across = [], []
    for i, g in steps:
        unit = block(i, g, c, b)
        near.append((go.start(unit, unit, right_b), go.start(unit, unit, left_b)))
        across.append(go.start(unit, unit, me.core()))
    last = []
    for (i, g), (to_right, to_left) in zip(steps, near):
        to_right.wait_recv()
        half = block(i, g, c, ring(b, 3), pl.ds(0, 2))
        last.append(go.start(half, half, right_b))
        to_left.wait_recv()
        half = block(i, g, c, ring(b, 1), pl.ds(2, 2))
        last.append(go.start(half, half, left_b))
        for k in (3, 1):
            unit = block(i, g, c, ring(b, k))
            across.append(go.start(unit, unit, me.core()))
    for copy in last:
        copy.wait_recv()
    for i, g in steps:
        unit = block(i, g, c, ring(b, 2))
        across.append(go.start(unit, unit, me.core()))
    for copy in across + w_copies:
        copy.wait_recv()
    go.drain()


def gather(blocks, wide, weights, collective_id):
    n, m = len(blocks), len(weights)
    shapes = [
        jax.ShapeDtypeStruct(((2,) if w else ()) + (2, 4, 4, 2) + x.shape, x.dtype)
        for x, w in zip(blocks, wide)
    ] + [jax.ShapeDtypeStruct(w.shape, w.dtype) for w in weights]
    count = sum(27 if w else 13 for w in wide) + 7 * m
    vmem = pl.BlockSpec(memory_space=pltpu.VMEM)
    hbm = pl.BlockSpec(memory_space=pl.ANY)
    return pl.pallas_call(
        functools.partial(gather_body, tuple(wide), bool(weights)),
        out_shape=shapes,
        in_specs=[vmem] * (n + m),
        out_specs=[hbm] * (n + m),
        scratch_shapes=[
            pltpu.SemaphoreType.DMA((count,)),
            pltpu.SemaphoreType.DMA((count,)),
            pltpu.SemaphoreType.DMA((n + m,)),
        ],
        compiler_params=pltpu.CompilerParams(
            collective_id=collective_id, has_side_effects=True
        ),
        name="gather%d" % collective_id,
    )(*blocks, *weights)


def scatter_body(x, out, r0, acc, hr, hl, ur, ul, acc1, ra, acc2, give, rp, send, recv):
    me = Place()
    a, b, c, p = me.a, me.b, me.c, me.p
    go = Copies(send, recv)
    right_a, left_a, far_a = (me.on_a(ring(a, k)) for k in (1, 3, 2))
    right_b, left_b = me.on_b(ring(b, 1)), me.on_b(ring(b, 3))
    greet([me.core(), me.partner(), right_a, left_a, far_a, right_b, left_b])
    halves = x.shape[2] // 2
    lo, hi = pl.ds(0, halves), pl.ds(halves, halves)
    order = (2, 1, 3, 0)
    got = []
    for k in order:
        j = ring(a, k)
        got.append(go.start(x.at[1 - c, j], r0.at[j], me.core()))

    def join(k):
        j = ring(b, order[k])
        got[k].wait_recv()
        acc[j] = (x[c, j].astype(F32) + r0[j].astype(F32)).astype(BF16)
        return j

    far = join(0)
    s_r = go.start(acc.at[far, lo], hr, right_b)
    s_l = go.start(acc.at[far, hi], hl, left_b)
    near_r = join(1)
    t_r = go.start(acc.at[near_r, hi], ul.at[hi], right_b)
    near_l = join(2)
    t_l = go.start(acc.at[near_l, lo], ur.at[lo], left_b)
    s_r.wait_recv()
    acc[near_r, lo] = (acc[near_r, lo].astype(F32) + hr[...].astype(F32)).astype(BF16)
    v_r = go.start(acc.at[near_r, lo], ul.at[lo], right_b)
    s_l.wait_recv()
    acc[near_l, hi] = (acc[near_l, hi].astype(F32) + hl[...].astype(F32)).astype(BF16)
    v_l = go.start(acc.at[near_l, hi], ur.at[hi], left_b)
    own = join(3)
    for copy in (t_r, t_l, v_r, v_l):
        copy.wait_recv()
    total = acc[own].astype(F32) + ul[...].astype(F32) + ur[...].astype(F32)
    acc1[...] = total.astype(BF16).reshape(acc1.shape)
    sends = [
        go.start(acc1.at[ring(a, k)], ra.at[i], to)
        for i, (k, to) in enumerate(((2, far_a), (1, right_a), (3, left_a)))
    ]
    for copy in sends:
        copy.wait_recv()
    total = acc1[a].astype(F32)
    for i in range(3):
        total = total + ra[i].astype(F32)
    acc2[...] = total.reshape(acc2.shape)
    give[...] = acc2[1 - p].astype(BF16)
    swap = go.start(give, rp, me.partner())
    swap.wait_recv()
    out[...] = acc2[p] + rp[...].astype(F32)
    go.drain()


def scatter(x, collective_id):
    rows, width = x.shape
    unit = rows // 8
    block = rows // 64
    x = x.reshape(2, 4, unit, width)
    vmem = pl.BlockSpec(memory_space=pltpu.VMEM)
    return pl.pallas_call(
        scatter_body,
        out_shape=jax.ShapeDtypeStruct((block, width), F32),
        in_specs=[vmem],
        out_specs=vmem,
        scratch_shapes=[
            pltpu.VMEM((4, unit, width), BF16),
            pltpu.VMEM((4, unit, width), BF16),
            pltpu.VMEM((unit // 2, width), BF16),
            pltpu.VMEM((unit // 2, width), BF16),
            pltpu.VMEM((unit, width), BF16),
            pltpu.VMEM((unit, width), BF16),
            pltpu.VMEM((4, unit // 4, width), BF16),
            pltpu.VMEM((3, unit // 4, width), BF16),
            pltpu.VMEM((2, block, width), F32),
            pltpu.VMEM((block, width), BF16),
            pltpu.VMEM((block, width), BF16),
            pltpu.SemaphoreType.DMA((14,)),
            pltpu.SemaphoreType.DMA((14,)),
        ],
        compiler_params=pltpu.CompilerParams(
            collective_id=collective_id, has_side_effects=True
        ),
        name="scatter%d" % collective_id,
    )(x)


OFFSETS = [(k, i) for k in (2, 1, 3, 0) for i in range(4) if k or i]
ROWS = (2, 3, 1, 0)


def rms_rows(values, gain):
    values = values.astype(F32)
    return values * lax.rsqrt(jnp.mean(values * values, axis=-1, keepdims=True) + EPSILON) * gain


def to_plane(go, me, view, slot=None):
    sent = {}
    for k, i in OFFSETS:
        to = me.on_ab(ring(me.a, i), ring(me.b, k))
        sent[k, i] = go.start(view, view if slot is None else slot(k, i), to)
    return sent


def forward_body(
    ids, hid, gain_in, gain_out, refh, ref_gain, gate, up, down, head,
    normed, pre, fin, fin_x, mid, ref_st, tgt, lang, dnw,
    idsg, gus, guw, ref_all, headv, rhs, logit, x, r0, acc, rs, give, rp,
    send, recv, local,
):
    me = Place()
    a, b, c, p, f = me.a, me.b, me.c, me.p, me.f
    go = Copies(send, recv)
    plane = [me.on_ab(ring(a, i), ring(b, k)) for k, i in OFFSETS]
    x_peers = [me.partner(), me.neighbour(), me.opposite()]
    flips = [me.at(y=ring(me.y, k), c=1 - c) for k in range(4)]
    greet(plane + x_peers + flips)
    take_head = pltpu.make_async_copy(head, headv, local.at[0])
    take_head.start()
    normed[c, b, a, p] = rms_rows(hid[...], gain_in[...]).astype(BF16)
    idsg[c, b, a, 0, p] = ids[...]
    s1 = [go.start(normed.at[c, b, a, p], normed.at[c, b, a, p], me.partner())]
    for g, to in zip((0, 1, 1), x_peers):
        s1.append(go.start(ids, idsg.at[c, b, a, g, p], to))
    low = lax.broadcasted_iota(jnp.int32, (128, 128), 1) < 64
    for i in range(4):
        g = gate[:, 128 * i : 128 * (i + 1)].astype(F32)
        u = up[:, 128 * i : 128 * (i + 1)].astype(F32)
        gus[2 * i] = jnp.where(low, g, pltpu.roll(u, 64, 1)).astype(BF16)
        gus[2 * i + 1] = jnp.where(low, pltpu.roll(g, 64, 1), u).astype(BF16)
    here = pl.ds(pl.multiple_of(f * 128, 128), 128)
    w_sent = []
    for j in range(1, 8):
        o = lax.rem(f + j, 8)
        to = {"dp": me.dp, "fsdp": o, "tp": me.t}
        w_sent.append(go.start(gus.at[o], guw.at[f], to))
        w_sent.append(go.start(down.at[o], dnw.at[:, here], to))
    guw[f] = gus[f]
    dnw[:, here] = down[f]
    ref_all[c, b, a, p] = rms_rows(refh[...], ref_gain[...]).astype(BF16)
    r1 = go.start(ref_all.at[c, b, a, p], ref_all.at[c, b, a, p], me.partner())
    for copy in s1:
        copy.wait_recv()
    s2 = to_plane(go, me, normed.at[c, b, a])
    s2_ids = to_plane(go, me, idsg.at[c, b, a])
    r1.wait_recv()
    unit = ref_all.at[c, b, a]
    r2 = [go.start(unit, unit, me.on_a(ring(a, k))) for k in (1, 3, 2)]
    s3 = []
    for k in (2, 1, 3, 0):
        for i in range(4):
            if k or i:
                s2[k, i].wait_recv()
        row = normed.at[c, ring(b, 4 - k)]
        s3.append(go.start(row, row, me.core()))
    for copy in s2_ids.values():
        copy.wait_recv()
    ids_across = go.start(idsg.at[c], idsg.at[c], me.core())
    for copy in w_sent:
        copy.wait_recv()

    def ffn(cc, bb):
        h = jnp.dot(
            normed[cc, bb].reshape(128, 1024), guw[...].reshape(1024, 128),
            preferred_element_type=F32,
        )
        pre[cc, bb] = h
        h = (h * jax.nn.sigmoid(h) * pltpu.roll(h, 64, 1)).astype(BF16)[:, :64]
        x[cc, bb] = jnp.dot(h, dnw[...], preferred_element_type=F32).astype(BF16)

    across = []
    for n, m in enumerate(ROWS):
        s3[n].wait_recv()
        bb = ring(a, m)
        ffn(1 - c, bb)
        across.append(go.start(x.at[1 - c, bb], r0.at[bb], me.core()))
    rs_sent = {}
    for n, m in enumerate(ROWS):
        bb = ring(b, m)
        ffn(c, bb)
        across[n].wait_recv()
        total = x[c, bb].astype(F32) + r0[bb].astype(F32)
        acc[bb] = total.astype(BF16).reshape(acc.shape[1:])
        for i in range(4):
            if m or i:
                to = me.on_ab(ring(a, i), bb)
                rs_sent[m, i] = go.start(acc.at[bb, ring(a, i)], rs.at[4 * m + i], to)
    for copy in r2:
        copy.wait_recv()
    right_b, left_b = me.on_b(ring(b, 1)), me.on_b(ring(b, 3))
    unit = ref_all.at[c, b]
    r3 = [go.start(unit, unit, right_b), go.start(unit, unit, left_b)]
    cross = {0: go.start(unit, unit, me.core())}
    ids_across.wait_recv()
    for g in range(2):
        for cc in range(2):
            for bb in range(4):
                row = idsg[cc, bb, 0, g, 0]
                for j in range(1, 8):
                    row = row + idsg[cc, bb, j // 2, g, j % 2]
                tgt[8 * g + 4 * cc + bb] = row[0:1]
                lang[8 * g + 4 * cc + bb] = row[1:2]
    vocab = lax.broadcasted_iota(jnp.int32, (1024, 256), 0) + (f * 8 + me.t) * 1024

    def ref_rows(m):
        b_own, b_far = ring(b, m), ring(a, m)
        rhs[0:128] = ref_all[c, b_own].reshape(128, 4096)
        rhs[128:256] = ref_all[1 - c, b_far].reshape(128, 4096)

        @pl.loop(0, 4)
        def _(n):
            at = pl.ds(pl.multiple_of(n * 256, 256), 256)
            logit[at] = lax.dot_general(
                headv[at], rhs[...], (((1,), (1,)), ((), ())), preferred_element_type=F32
            )

        value = logit[...]
        high = jnp.max(value, axis=0, keepdims=True)
        want = jnp.concatenate([tgt[4 * c + b_own], tgt[4 * (1 - c) + b_far]], axis=1)
        picked = jnp.sum(jnp.where(vocab == want, value, 0.0), axis=0, keepdims=True)
        total = jnp.sum(jnp.exp(value - high), axis=0, keepdims=True)
        for s, got in enumerate((high, total, picked)):
            ref_st[s, 4 * c + b_own] = got[:, :128]
            ref_st[s, 4 * (1 - c) + b_far] = got[:, 128:]

    take_head.wait()
    cross[0].wait_recv()
    ref_rows(0)
    for copy in rs_sent.values():
        copy.wait_recv()
    total = acc[b, a].astype(F32)
    for m, i in rs_sent:
        total = total + rs[4 * m + i].astype(F32)
    first, second = total[0:16], total[16:32]
    own = jnp.where(p == 0, first, second)
    give[...] = jnp.where(p == 0, second, first).astype(BF16)
    swap = go.start(give, rp, me.partner())
    swap.wait_recv()
    middle = hid[...].astype(F32) + (own + rp[...].astype(F32))
    mid[...] = middle
    fin[c, b, a, p] = rms_rows(middle, gain_out[...]).astype(BF16)
    block = fin.at[c, b, a, p]
    f1 = go.start(block, block, me.partner())
    f_x = [go.start(block, fin_x.at[p], to) for to in x_peers[1:]]
    f1.wait_recv()
    f2 = to_plane(go, me, fin.at[c, b, a])
    r3[0].wait_recv()
    half = ref_all.at[c, ring(b, 3), pl.ds(0, 2)]
    r4 = [go.start(half, half, right_b)]
    r3[1].wait_recv()
    half = ref_all.at[c, ring(b, 1), pl.ds(2, 2)]
    r4.append(go.start(half, half, left_b))
    for m in (3, 1):
        unit = ref_all.at[c, ring(b, m)]
        cross[m] = go.start(unit, unit, me.core())
    cross[3].wait_recv()
    ref_rows(3)
    f3 = []
    for k in (2, 1, 3, 0):
        for i in range(4):
            if k or i:
                f2[k, i].wait_recv()
        row = fin.at[c, ring(b, 4 - k)]
        f3.append(go.start(row, row, me.core()))
    for copy in r4:
        copy.wait_recv()
    unit = ref_all.at[c, ring(b, 2)]
    cross[2] = go.start(unit, unit, me.core())
    cross[1].wait_recv()
    ref_rows(1)
    cross[2].wait_recv()
    ref_rows(2)
    for copy in f3 + f_x:
        copy.wait_recv()
    go.drain()


def forward(ids, hid, gain_in, gain_out, refh, ref_gain, gate, up, down, head):
    vmem = pl.BlockSpec(memory_space=pltpu.VMEM)
    shape = jax.ShapeDtypeStruct
    return pl.pallas_call(
        forward_body,
        out_shape=[
            shape((2, 4, 4, 2, 16, 1024), BF16),
            shape((2, 4, 128, 128), F32),
            shape((2, 4, 4, 2, 16, 1024), BF16),
            shape((2, 16, 1024), BF16),
            shape((16, 1024), F32),
            shape((3, 8, 1, 128), F32),
            shape((16, 1, 128), jnp.int32),
            shape((16, 1, 128), jnp.int32),
            shape((64, 1024), BF16),
        ],
        in_specs=[vmem] * 9 + [pl.BlockSpec(memory_space=pl.ANY)],
        out_specs=[vmem] * 9,
        scratch_shapes=[
            pltpu.VMEM((2, 4, 4, 2, 2, 8, 128), jnp.int32),
            pltpu.VMEM((8, 128, 128), BF16),
            pltpu.VMEM((8, 128, 128), BF16),
            pltpu.VMEM((2, 4, 4, 2, 16, 4096), BF16),
            pltpu.VMEM((1024, 4096), BF16),
            pltpu.VMEM((256, 4096), BF16),
            pltpu.VMEM((1024, 256), F32),
            pltpu.VMEM((2, 4, 128, 1024), BF16),
            pltpu.VMEM((4, 128, 1024), BF16),
            pltpu.VMEM((4, 4, 32, 1024), BF16),
            pltpu.VMEM((16, 32, 1024), BF16),
            pltpu.VMEM((16, 1024), BF16),
            pltpu.VMEM((16, 1024), BF16),
            pltpu.SemaphoreType.DMA((110,)),
            pltpu.SemaphoreType.DMA((110,)),
            pltpu.SemaphoreType.DMA((1,)),
        ],
        compiler_params=pltpu.CompilerParams(
            collective_id=1, has_side_effects=True, vmem_limit_bytes=60 * 2**20
        ),
        name="forward",
    )(ids, hid, gain_in, gain_out, refh, ref_gain, gate, up, down, head)


def join_all(pieces):
    out = []
    for base in (0, 12):
        high = functools.reduce(jnp.maximum, [s[base : base + 4] for s in pieces])
        total = pick = None
        for s in pieces:
            t = s[base + 4 : base + 8] * jnp.exp(s[base : base + 4] - high)
            k = s[base + 8 : base + 12]
            total, pick = (t, k) if total is None else (total + t, pick + k)
        out += [high, total, pick]
    return jnp.concatenate(out, axis=0)


def stats_body(
    st, lang, dw, fin_x, lse, tw, logw, fin, slot_c, slot_yz, slot_x, both, ls, lc, send, recv
):
    me = Place()
    a, b, c, p = me.a, me.b, me.c, me.p
    go = Copies(send, recv)
    plane = [me.on_ab(ring(a, i), ring(b, k)) for k, i in OFFSETS]
    x_peers = [me.partner(), me.neighbour(), me.opposite()]
    greet(plane + x_peers + [me.core()])
    slot_c[c] = st[c]
    half = go.start(st.at[1 - c], slot_c.at[c], me.core())
    fin[c, b, a] = fin_x[...]
    half.wait_recv()
    yz = me.y * 4 + me.z
    slot_c_other = slot_c[1 - c]
    mine = slot_c[c]
    first = jnp.where(c == 0, mine, slot_c_other)
    second = jnp.where(c == 0, slot_c_other, mine)
    slot_yz[yz] = join_all([first, second])
    sent = to_plane(go, me, slot_yz.at[yz])
    beside = to_plane(go, me, fin_x, lambda k, i: fin.at[c, b, a])
    for copy in sent.values():
        copy.wait_recv()
    slot_x[0, p] = join_all([slot_yz[j] for j in range(16)])
    spread = [
        go.start(slot_x.at[0, p], slot_x.at[g, p], to) for g, to in zip((0, 1, 1), x_peers)
    ]
    for copy in spread:
        copy.wait_recv()
    both[c, 0] = join_all([slot_x[0, 0], slot_x[0, 1]])
    both[c, 1] = join_all([slot_x[1, 0], slot_x[1, 1]])
    share = go.start(both.at[c], both.at[c], me.core())
    across = []
    for k in (2, 1, 3, 0):
        for i in range(4):
            if k or i:
                beside[k, i].wait_recv()
        row = fin.at[c, ring(b, 4 - k)]
        across.append(go.start(row, row, me.core()))
    share.wait_recv()
    group = lax.rem(me.dp + me.xh, 2)
    excess = [None, None]
    for g in range(2):
        now = [jnp.concatenate([both[0, g, 4 * i : 4 * i + 4], both[1, g, 4 * i : 4 * i + 4]]) for i in range(6)]
        ref_loss = now[0] + jnp.log(now[1]) - now[2]
        proxy_lse = now[3] + jnp.log(now[4])
        lse[8 * g : 8 * g + 8] = proxy_lse
        excess[g] = jnp.maximum(proxy_lse - now[5] - ref_loss, 0.0)
    every = lang[...]
    for l in range(LANGS):
        here = every == l
        e = jnp.where(here[:8], excess[0], 0.0) + jnp.where(here[8:], excess[1], 0.0)
        n = jnp.where(here[:8], 1.0, 0.0) + jnp.where(here[8:], 1.0, 0.0)
        ls[l : l + 1] = jnp.sum(e, axis=0, keepdims=True)
        lc[l : l + 1] = jnp.sum(n, axis=0, keepdims=True)
    wide = lambda v: jnp.broadcast_to(jnp.sum(v[...], axis=1, keepdims=True), (LANGS, 128))
    count = jnp.maximum(wide(lc), 1.0)
    score = jnp.log(dw[...]) + STEP_SIZE * (wide(ls) / count)
    score = jnp.exp(score - jnp.max(score, axis=0, keepdims=True))
    mixture = score / jnp.sum(score, axis=0, keepdims=True)
    new = (1.0 - SMOOTHING) * mixture + SMOOTHING / LANGS
    logw[...] = jnp.log(new)
    per_token = new / count * 2048.0
    weight = jnp.zeros(every.shape, F32)
    for l in range(LANGS):
        weight = jnp.where(every == l, per_token[l : l + 1], weight)
    tw[...] = weight
    for copy in across:
        copy.wait_recv()
    go.drain()


def join_stats(stats, lang, domain_weights, fin_x):
    vmem = pl.BlockSpec(memory_space=pltpu.VMEM)
    return pl.pallas_call(
        stats_body,
        out_shape=[
            jax.ShapeDtypeStruct((16, 128), F32),
            jax.ShapeDtypeStruct((16, 128), F32),
            jax.ShapeDtypeStruct((LANGS, 128), F32),
            jax.ShapeDtypeStruct((2, 4, 4, 2, 16, 1024), BF16),
        ],
        in_specs=[vmem] * 4,
        out_specs=[vmem] * 4,
        scratch_shapes=[
            pltpu.VMEM((2, 24, 128), F32),
            pltpu.VMEM((16, 24, 128), F32),
            pltpu.VMEM((2, 2, 24, 128), F32),
            pltpu.VMEM((2, 2, 24, 128), F32),
            pltpu.VMEM((LANGS, 128), F32),
            pltpu.VMEM((LANGS, 128), F32),
            pltpu.SemaphoreType.DMA((40,)),
            pltpu.SemaphoreType.DMA((40,)),
        ],
        compiler_params=pltpu.CompilerParams(collective_id=4, has_side_effects=True),
        name="stats",
    )(stats, lang, jnp.broadcast_to(domain_weights[:, None], (LANGS, 128)), fin_x)


def home_body(gu, dn, gate, up, down, o_gu, o_dn, s_gu, s_dn, r_gu, r_dn, send, recv):
    me = Place()
    go = Copies(send, recv)
    others = [lax.rem(me.f + j, 8) for j in range(1, 8)]
    to = [{"dp": me.dp, "fsdp": o, "tp": me.t} for o in others]
    greet([me.neighbour(), *to])
    first = [go.start(gu, o_gu, me.neighbour()), go.start(dn, o_dn, me.neighbour())]
    for copy in first:
        copy.wait_recv()
    for j in range(8):
        s_gu[j] = (gu[j].astype(F32) + o_gu[j].astype(F32)).astype(BF16)
        s_dn[j] = (dn[j].astype(F32) + o_dn[j].astype(F32)).astype(BF16)
    sent = []
    for o, dev in zip(others, to):
        sent.append(go.start(s_gu.at[o], r_gu.at[me.f], dev))
        sent.append(go.start(s_dn.at[o], r_dn.at[me.f], dev))
    r_gu[me.f] = s_gu[me.f]
    r_dn[me.f] = s_dn[me.f]
    for copy in sent:
        copy.wait_recv()
    for j in range(8):
        both = r_gu[j].astype(F32)
        gate[:, 64 * j : 64 * (j + 1)] = both[:, :64]
        up[:, 64 * j : 64 * (j + 1)] = both[:, 64:]
        down[64 * j : 64 * (j + 1)] = r_dn[j].astype(F32)
    go.drain()


def home(gu, dn, collective_id):
    vmem = pl.BlockSpec(memory_space=pltpu.VMEM)
    return pl.pallas_call(
        home_body,
        out_shape=[
            jax.ShapeDtypeStruct((128, 512), F32),
            jax.ShapeDtypeStruct((128, 512), F32),
            jax.ShapeDtypeStruct((512, 128), F32),
        ],
        in_specs=[vmem] * 2,
        out_specs=[vmem] * 3,
        scratch_shapes=[pltpu.VMEM(gu.shape, BF16), pltpu.VMEM(dn.shape, BF16)] * 3
        + [pltpu.SemaphoreType.DMA((16,)), pltpu.SemaphoreType.DMA((16,))],
        compiler_params=pltpu.CompilerParams(
            collective_id=collective_id, has_side_effects=True
        ),
        name="home",
    )(gu, dn)


def rms_scale(values, gain_vec):
    values = values.astype(F32)
    return (
        values * lax.rsqrt(jnp.mean(values * values, axis=-1, keepdims=True) + EPSILON) * gain_vec
    )


def row_logits(row_block, head):
    return lax.dot_general(row_block, head, (((1,), (1,)), ((), ())), preferred_element_type=F32)


def piece_stats(logits, part_targets, vocab_start):
    vocab_cols = vocab_start + jnp.arange(logits.shape[1], dtype=jnp.int32)
    high_val = jnp.max(logits, axis=1)
    exp_total = jnp.sum(jnp.exp(logits - high_val[:, None]), axis=1)
    picked = jnp.sum(jnp.where(vocab_cols[None, :] == part_targets[:, None], logits, 0.0), axis=1)
    return (high_val, exp_total, picked)


def norm_backward(mid_sum, gain_vec, d_out):
    inv_rms = lax.rsqrt(jnp.mean(mid_sum * mid_sum, axis=1, keepdims=True) + EPSILON)
    scaled_grad = d_out * gain_vec
    inner_mean = jnp.mean(mid_sum * scaled_grad, axis=1, keepdims=True)
    return (inv_rms * scaled_grad - mid_sum * inv_rms * inv_rms * inv_rms * inner_mean).astype(BF16)


def gate_grads(d_act, gate_pre, up_pre):
    sigmoid_g = jax.nn.sigmoid(gate_pre)
    d_gate = (d_act * up_pre * sigmoid_g * (1.0 + gate_pre * (1.0 - sigmoid_g))).astype(BF16)
    d_up = (d_act * gate_pre * sigmoid_g).astype(BF16)
    return (d_gate, d_up)


def local(
    ref_hidden,
    proxy_hidden,
    targets,
    languages,
    ref_gain,
    ref_head,
    proxy_gain_in,
    proxy_gain_out,
    gate_weight,
    up_weight,
    down_weight,
    proxy_head,
    domain_weights,
):
    me = Place()
    vocab_rows = ref_head.shape[0]
    vocab_start = lax.axis_index(("fsdp", "tp")) * vocab_rows
    mine = lambda v: lax.dynamic_slice_in_dim(v, me.t * 16, 16, 0)
    hidden = mine(proxy_hidden)
    ids = jnp.tile(jnp.stack([mine(targets), mine(languages)]), (4, 8))
    lanes = lax.broadcasted_iota(jnp.int32, (8, 128), 1)
    ids = jnp.where(lax.div(lanes, 16) == me.a * 2 + me.p, ids, 0)
    normed_in, pre, final_own, fin_x, mid_sum, ref_stats, group_targets, langs, down_w = forward(
        ids,
        hidden,
        proxy_gain_in[None],
        proxy_gain_out[None],
        ref_hidden,
        ref_gain[None],
        gate_weight,
        up_weight,
        down_weight.reshape(8, 64, 128),
        ref_head,
    )
    group_targets = group_targets.reshape(2048)
    normed_in = normed_in.reshape(1024, 1024)
    pre = pre.reshape(1024, 128)
    gate_pre, up_pre = pre[:, :64], pre[:, 64:]
    hidden_act = (gate_pre * jax.nn.sigmoid(gate_pre) * up_pre).astype(BF16)
    final_own = final_own.reshape(1024, 1024)
    logits_own = row_logits(final_own, proxy_head)
    proxy_stats = piece_stats(logits_own, group_targets[:1024], vocab_start)
    stats = jnp.concatenate([ref_stats.reshape(3, 8, 128), jnp.stack(proxy_stats).reshape(3, 8, 128)])
    stats = stats.reshape(6, 2, 4, 128).transpose(1, 0, 2, 3).reshape(2, 24, 128)
    lse, token_weight, log_weights, final_far = join_stats(
        stats, langs.reshape(16, 128), domain_weights, fin_x
    )
    final_far = final_far.reshape(1024, 1024)
    lse, token_weight = lse.reshape(2048), token_weight.reshape(2048)
    vocab_cols = vocab_start + jnp.arange(vocab_rows, dtype=jnp.int32)

    def to_dlogits(logits, at):
        onehot = (vocab_cols[None, :] == group_targets[at, None]).astype(F32)
        share = jnp.exp(logits - lse[at, None]) - onehot
        return (token_weight[at, None] * share).astype(BF16)

    own, far = slice(0, 1024), slice(1024, 2048)
    d_own = to_dlogits(logits_own, own)
    d_part = jnp.dot(d_own, proxy_head, preferred_element_type=F32).astype(BF16)
    d_final = scatter(d_part, 5)
    d_far = to_dlogits(row_logits(final_far, proxy_head), far)
    rows = (((0,), (0,)), ((), ()))
    grad_head = lax.dot_general(d_own, final_own, rows, preferred_element_type=F32)
    grad_head = grad_head + lax.dot_general(d_far, final_far, rows, preferred_element_type=F32)
    d_mid = norm_backward(mid_sum, proxy_gain_out, d_final)
    (d_mid,) = gather((d_mid,), (False,), (), 6)
    d_mid = d_mid.reshape(1024, 1024)
    grad_down = lax.dot_general(
        hidden_act, d_mid, (((0,), (0,)), ((), ())), preferred_element_type=F32
    )
    d_act = lax.dot_general(d_mid, down_w, (((1,), (1,)), ((), ())), preferred_element_type=F32)
    d_both = jnp.concatenate(gate_grads(d_act, gate_pre, up_pre), axis=1)
    grad_gu = lax.dot_general(
        normed_in, d_both, (((0,), (0,)), ((), ())), preferred_element_type=F32
    )
    grad_gu = grad_gu.astype(BF16).reshape(8, 128, 128)
    grad_down = grad_down.astype(BF16).reshape(64, 8, 128).transpose(1, 0, 2)
    grad_gate, grad_up, grad_down = home(grad_gu, grad_down, 7)
    return (log_weights[:, 0], grad_gate, grad_up, grad_down, grad_head)


def solution(mesh):
    in_specs = (
        P(("dp", "fsdp", "tp"), None),
        P(("dp", "fsdp"), None),
        P(("dp", "fsdp")),
        P(("dp", "fsdp")),
        P(),
        P(("fsdp", "tp"), None),
        P(),
        P(),
        P("fsdp", "tp"),
        P("fsdp", "tp"),
        P("tp", "fsdp"),
        P(("fsdp", "tp"), None),
        P(),
    )
    out_specs = (P(), P("fsdp", "tp"), P("fsdp", "tp"), P("tp", "fsdp"), P(("fsdp", "tp"), None))
    return jax.shard_map(local, mesh=mesh, in_specs=in_specs, out_specs=out_specs, check_vma=False)
```

```python
import functools

import jax
import jax.numpy as jnp
from jax import lax
from jax.experimental import pallas as pl
from jax.experimental.pallas import tpu as pltpu
from jax.sharding import PartitionSpec as P

EPSILON = 1e-05
STEP_SIZE = 1.0
SMOOTHING = 0.001
LANGS = 64
MESH = pl.DeviceIdType.MESH
F32, BF16 = jnp.float32, jnp.bfloat16


class Place:
    def __init__(self):
        self.dp = lax.axis_index("dp")
        f, t = lax.axis_index("fsdp"), lax.axis_index("tp")
        self.f, self.t = f, t
        self.y, self.c = lax.div(f, 2), lax.rem(f, 2)
        self.z, self.xh = lax.div(t, 2), lax.rem(t, 2)
        self.p = self.xh
        c = self.c
        self.a = (1 - c) * self.y + c * self.z
        self.b = (1 - c) * self.z + c * self.y

    def at(self, dp=None, y=None, z=None, xh=None, c=None):
        pick = lambda new, old: old if new is None else new
        dp, y, z = pick(dp, self.dp), pick(y, self.y), pick(z, self.z)
        xh, c = pick(xh, self.xh), pick(c, self.c)
        return {"dp": dp, "fsdp": y * 2 + c, "tp": z * 2 + xh}

    def on_a(self, a):
        c = self.c
        return self.at(y=(1 - c) * a + c * self.y, z=(1 - c) * self.z + c * a)

    def on_b(self, b):
        c = self.c
        return self.at(y=(1 - c) * self.y + c * b, z=(1 - c) * b + c * self.z)

    def on_ab(self, a, b):
        c = self.c
        return self.at(y=(1 - c) * a + c * b, z=(1 - c) * b + c * a)

    def core(self):
        return self.at(c=1 - self.c)

    def partner(self):
        return self.at(xh=1 - self.xh)

    def neighbour(self):
        return self.at(dp=1 - self.dp)

    def opposite(self):
        return self.at(dp=1 - self.dp, xh=1 - self.xh)


class Copies:
    def __init__(self, send, recv):
        self.send, self.recv, self.n, self.all = send, recv, 0, []

    def start(self, src, dst, to):
        copy = pltpu.make_async_remote_copy(
            src_ref=src,
            dst_ref=dst,
            send_sem=self.send.at[self.n],
            recv_sem=self.recv.at[self.n],
            device_id=to,
            device_id_type=MESH,
        )
        copy.start()
        self.n += 1
        self.all.append(copy)
        return copy

    def drain(self):
        for copy in self.all:
            copy.wait_send()


def greet(peers):
    barrier = pltpu.get_barrier_semaphore()
    for peer in peers:
        pl.semaphore_signal(barrier, inc=1, device_id=peer, device_id_type=MESH)
    pl.semaphore_wait(barrier, len(peers))


def ring(i, k):
    return lax.rem(i + k, 4)


OFFSETS = [(k, i) for k in (2, 1, 3, 0) for i in range(4) if k or i]
ROWS = (2, 3, 1, 0)


def rms_rows(values, gain):
    values = values.astype(F32)
    return values * lax.rsqrt(jnp.mean(values * values, axis=-1, keepdims=True) + EPSILON) * gain


def to_plane(go, me, view, slot=None):
    sent = {}
    for k, i in OFFSETS:
        to = me.on_ab(ring(me.a, i), ring(me.b, k))
        sent[k, i] = go.start(view, view if slot is None else slot(k, i), to)
    return sent


def forward_body(
    ids, hid, gain_in, gain_out, refh, ref_gain, gate, up, down, head,
    normed, pre, fin, fin_x, mid, ref_st, tgt, lang, dnw,
    idsg, gus, guw, ref_all, headv, rhs, logit, x, r0, acc, rs, give, rp,
    send, recv, local,
):
    me = Place()
    a, b, c, p, f = me.a, me.b, me.c, me.p, me.f
    go = Copies(send, recv)
    plane = [me.on_ab(ring(a, i), ring(b, k)) for k, i in OFFSETS]
    x_peers = [me.partner(), me.neighbour(), me.opposite()]
    flips = [me.at(y=ring(me.y, k), c=1 - c) for k in range(4)]
    greet(plane + x_peers + flips)
    take_head = pltpu.make_async_copy(head, headv, local.at[0])
    take_head.start()
    normed[c, b, a, p] = rms_rows(hid[...], gain_in[...]).astype(BF16)
    idsg[c, b, a, 0, p] = ids[...]
    s1 = [go.start(normed.at[c, b, a, p], normed.at[c, b, a, p], me.partner())]
    for g, to in zip((0, 1, 1), x_peers):
        s1.append(go.start(ids, idsg.at[c, b, a, g, p], to))
    low = lax.broadcasted_iota(jnp.int32, (128, 128), 1) < 64
    for i in range(4):
        g = gate[:, 128 * i : 128 * (i + 1)].astype(F32)
        u = up[:, 128 * i : 128 * (i + 1)].astype(F32)
        gus[2 * i] = jnp.where(low, g, pltpu.roll(u, 64, 1)).astype(BF16)
        gus[2 * i + 1] = jnp.where(low, pltpu.roll(g, 64, 1), u).astype(BF16)
    here = pl.ds(pl.multiple_of(f * 128, 128), 128)
    w_sent = []
    for j in range(1, 8):
        o = lax.rem(f + j, 8)
        to = {"dp": me.dp, "fsdp": o, "tp": me.t}
        w_sent.append(go.start(gus.at[o], guw.at[f], to))
        w_sent.append(go.start(down.at[o], dnw.at[:, here], to))
    guw[f] = gus[f]
    dnw[:, here] = down[f]
    ref_all[c, b, a, p] = rms_rows(refh[...], ref_gain[...]).astype(BF16)
    r1 = go.start(ref_all.at[c, b, a, p], ref_all.at[c, b, a, p], me.partner())
    for copy in s1:
        copy.wait_recv()
    s2 = to_plane(go, me, normed.at[c, b, a])
    s2_ids = to_plane(go, me, idsg.at[c, b, a])
    r1.wait_recv()
    unit = ref_all.at[c, b, a]
    r2 = [go.start(unit, unit, me.on_a(ring(a, k))) for k in (1, 3, 2)]
    s3 = []
    for k in (2, 1, 3, 0):
        for i in range(4):
            if k or i:
                s2[k, i].wait_recv()
        row = normed.at[c, ring(b, 4 - k)]
        s3.append(go.start(row, row, me.core()))
    for copy in s2_ids.values():
        copy.wait_recv()
    ids_across = go.start(idsg.at[c], idsg.at[c], me.core())
    for copy in w_sent:
        copy.wait_recv()

    def ffn(cc, bb):
        h = jnp.dot(
            normed[cc, bb].reshape(128, 1024), guw[...].reshape(1024, 128),
            preferred_element_type=F32,
        )
        pre[cc, bb] = h
        h = (h * jax.nn.sigmoid(h) * pltpu.roll(h, 64, 1)).astype(BF16)[:, :64]
        x[cc, bb] = jnp.dot(h, dnw[...], preferred_element_type=F32).astype(BF16)

    across = []
    for n, m in enumerate(ROWS):
        s3[n].wait_recv()
        bb = ring(a, m)
        ffn(1 - c, bb)
        across.append(go.start(x.at[1 - c, bb], r0.at[bb], me.core()))
    rs_sent = {}
    for n, m in enumerate(ROWS):
        bb = ring(b, m)
        ffn(c, bb)
        across[n].wait_recv()
        total = x[c, bb].astype(F32) + r0[bb].astype(F32)
        acc[bb] = total.astype(BF16).reshape(acc.shape[1:])
        for i in range(4):
            if m or i:
                to = me.on_ab(ring(a, i), bb)
                rs_sent[m, i] = go.start(acc.at[bb, ring(a, i)], rs.at[4 * m + i], to)
    for copy in r2:
        copy.wait_recv()
    right_b, left_b = me.on_b(ring(b, 1)), me.on_b(ring(b, 3))
    unit = ref_all.at[c, b]
    r3 = [go.start(unit, unit, right_b), go.start(unit, unit, left_b)]
    cross = {0: go.start(unit, unit, me.core())}
    ids_across.wait_recv()
    for g in range(2):
        for cc in range(2):
            for bb in range(4):
                row = idsg[cc, bb, 0, g, 0]
                for j in range(1, 8):
                    row = row + idsg[cc, bb, j // 2, g, j % 2]
                tgt[8 * g + 4 * cc + bb] = row[0:1]
                lang[8 * g + 4 * cc + bb] = row[1:2]
    vocab = lax.broadcasted_iota(jnp.int32, (1024, 256), 0) + (f * 8 + me.t) * 1024

    def ref_rows(m):
        b_own, b_far = ring(b, m), ring(a, m)
        rhs[0:128] = ref_all[c, b_own].reshape(128, 4096)
        rhs[128:256] = ref_all[1 - c, b_far].reshape(128, 4096)

        @pl.loop(0, 4)
        def _(n):
            at = pl.ds(pl.multiple_of(n * 256, 256), 256)
            logit[at] = lax.dot_general(
                headv[at], rhs[...], (((1,), (1,)), ((), ())), preferred_element_type=F32
            )

        value = logit[...]
        high = jnp.max(value, axis=0, keepdims=True)
        want = jnp.concatenate([tgt[4 * c + b_own], tgt[4 * (1 - c) + b_far]], axis=1)
        picked = jnp.sum(jnp.where(vocab == want, value, 0.0), axis=0, keepdims=True)
        total = jnp.sum(jnp.exp(value - high), axis=0, keepdims=True)
        for s, got in enumerate((high, total, picked)):
            ref_st[s, 4 * c + b_own] = got[:, :128]
            ref_st[s, 4 * (1 - c) + b_far] = got[:, 128:]

    take_head.wait()
    cross[0].wait_recv()
    ref_rows(0)
    for copy in rs_sent.values():
        copy.wait_recv()
    total = acc[b, a].astype(F32)
    for m, i in rs_sent:
        total = total + rs[4 * m + i].astype(F32)
    first, second = total[0:16], total[16:32]
    own = jnp.where(p == 0, first, second)
    give[...] = jnp.where(p == 0, second, first).astype(BF16)
    swap = go.start(give, rp, me.partner())
    swap.wait_recv()
    middle = hid[...].astype(F32) + (own + rp[...].astype(F32))
    mid[...] = middle
    fin[c, b, a, p] = rms_rows(middle, gain_out[...]).astype(BF16)
    block = fin.at[c, b, a, p]
    f1 = go.start(block, block, me.partner())
    f_x = [go.start(block, fin_x.at[p], to) for to in x_peers[1:]]
    f1.wait_recv()
    f2 = to_plane(go, me, fin.at[c, b, a])
    r3[0].wait_recv()
    half = ref_all.at[c, ring(b, 3), pl.ds(0, 2)]
    r4 = [go.start(half, half, right_b)]
    r3[1].wait_recv()
    half = ref_all.at[c, ring(b, 1), pl.ds(2, 2)]
    r4.append(go.start(half, half, left_b))
    for m in (3, 1):
        unit = ref_all.at[c, ring(b, m)]
        cross[m] = go.start(unit, unit, me.core())
    cross[3].wait_recv()
    ref_rows(3)
    f3 = []
    for k in (2, 1, 3, 0):
        for i in range(4):
            if k or i:
                f2[k, i].wait_recv()
        row = fin.at[c, ring(b, 4 - k)]
        f3.append(go.start(row, row, me.core()))
    for copy in r4:
        copy.wait_recv()
    unit = ref_all.at[c, ring(b, 2)]
    cross[2] = go.start(unit, unit, me.core())
    cross[1].wait_recv()
    ref_rows(1)
    cross[2].wait_recv()
    ref_rows(2)
    for copy in f3 + f_x:
        copy.wait_recv()
    go.drain()


def forward(ids, hid, gain_in, gain_out, refh, ref_gain, gate, up, down, head):
    vmem = pl.BlockSpec(memory_space=pltpu.VMEM)
    shape = jax.ShapeDtypeStruct
    return pl.pallas_call(
        forward_body,
        out_shape=[
            shape((2, 4, 4, 2, 16, 1024), BF16),
            shape((2, 4, 128, 128), F32),
            shape((2, 4, 4, 2, 16, 1024), BF16),
            shape((2, 16, 1024), BF16),
            shape((16, 1024), F32),
            shape((3, 8, 1, 128), F32),
            shape((16, 1, 128), jnp.int32),
            shape((16, 1, 128), jnp.int32),
            shape((64, 1024), BF16),
        ],
        in_specs=[vmem] * 9 + [pl.BlockSpec(memory_space=pl.ANY)],
        out_specs=[vmem] * 9,
        scratch_shapes=[
            pltpu.VMEM((2, 4, 4, 2, 2, 8, 128), jnp.int32),
            pltpu.VMEM((8, 128, 128), BF16),
            pltpu.VMEM((8, 128, 128), BF16),
            pltpu.VMEM((2, 4, 4, 2, 16, 4096), BF16),
            pltpu.VMEM((1024, 4096), BF16),
            pltpu.VMEM((256, 4096), BF16),
            pltpu.VMEM((1024, 256), F32),
            pltpu.VMEM((2, 4, 128, 1024), BF16),
            pltpu.VMEM((4, 128, 1024), BF16),
            pltpu.VMEM((4, 4, 32, 1024), BF16),
            pltpu.VMEM((16, 32, 1024), BF16),
            pltpu.VMEM((16, 1024), BF16),
            pltpu.VMEM((16, 1024), BF16),
            pltpu.SemaphoreType.DMA((110,)),
            pltpu.SemaphoreType.DMA((110,)),
            pltpu.SemaphoreType.DMA((1,)),
        ],
        compiler_params=pltpu.CompilerParams(
            collective_id=1, has_side_effects=True, vmem_limit_bytes=60 * 2**20
        ),
        name="forward",
    )(ids, hid, gain_in, gain_out, refh, ref_gain, gate, up, down, head)


def join_all(pieces):
    out = []
    for base in (0, 12):
        high = functools.reduce(jnp.maximum, [s[base : base + 4] for s in pieces])
        total = pick = None
        for s in pieces:
            t = s[base + 4 : base + 8] * jnp.exp(s[base : base + 4] - high)
            k = s[base + 8 : base + 12]
            total, pick = (t, k) if total is None else (total + t, pick + k)
        out += [high, total, pick]
    return jnp.concatenate(out, axis=0)


def stats_body(
    st, lang, dw, fin_x, lse, tw, logw, fin, slot_c, slot_yz, slot_x, both, ls, lc, send, recv
):
    me = Place()
    a, b, c, p = me.a, me.b, me.c, me.p
    go = Copies(send, recv)
    plane = [me.on_ab(ring(a, i), ring(b, k)) for k, i in OFFSETS]
    x_peers = [me.partner(), me.neighbour(), me.opposite()]
    greet(plane + x_peers + [me.core()])
    slot_c[c] = st[c]
    half = go.start(st.at[1 - c], slot_c.at[c], me.core())
    fin[c, b, a] = fin_x[...]
    half.wait_recv()
    yz = me.y * 4 + me.z
    slot_c_other = slot_c[1 - c]
    mine = slot_c[c]
    first = jnp.where(c == 0, mine, slot_c_other)
    second = jnp.where(c == 0, slot_c_other, mine)
    slot_yz[yz] = join_all([first, second])
    sent = to_plane(go, me, slot_yz.at[yz])
    beside = to_plane(go, me, fin_x, lambda k, i: fin.at[c, b, a])
    for copy in sent.values():
        copy.wait_recv()
    slot_x[0, p] = join_all([slot_yz[j] for j in range(16)])
    spread = [
        go.start(slot_x.at[0, p], slot_x.at[g, p], to) for g, to in zip((0, 1, 1), x_peers)
    ]
    for copy in spread:
        copy.wait_recv()
    both[c, 0] = join_all([slot_x[0, 0], slot_x[0, 1]])
    both[c, 1] = join_all([slot_x[1, 0], slot_x[1, 1]])
    share = go.start(both.at[c], both.at[c], me.core())
    across = []
    for k in (2, 1, 3, 0):
        for i in range(4):
            if k or i:
                beside[k, i].wait_recv()
        row = fin.at[c, ring(b, 4 - k)]
        across.append(go.start(row, row, me.core()))
    share.wait_recv()
    excess = [None, None]
    for g in range(2):
        now = [jnp.concatenate([both[0, g, 4 * i : 4 * i + 4], both[1, g, 4 * i : 4 * i + 4]]) for i in range(6)]
        ref_loss = now[0] + jnp.log(now[1]) - now[2]
        proxy_lse = now[3] + jnp.log(now[4])
        lse[8 * g : 8 * g + 8] = proxy_lse
        excess[g] = jnp.maximum(proxy_lse - now[5] - ref_loss, 0.0)
    every = lang[...]
    for l in range(LANGS):
        here = every == l
        e = jnp.where(here[:8], excess[0], 0.0) + jnp.where(here[8:], excess[1], 0.0)
        n = jnp.where(here[:8], 1.0, 0.0) + jnp.where(here[8:], 1.0, 0.0)
        ls[l : l + 1] = jnp.sum(e, axis=0, keepdims=True)
        lc[l : l + 1] = jnp.sum(n, axis=0, keepdims=True)
    wide = lambda v: jnp.broadcast_to(jnp.sum(v[...], axis=1, keepdims=True), (LANGS, 128))
    count = jnp.maximum(wide(lc), 1.0)
    score = jnp.log(dw[...]) + STEP_SIZE * (wide(ls) / count)
    score = jnp.exp(score - jnp.max(score, axis=0, keepdims=True))
    mixture = score / jnp.sum(score, axis=0, keepdims=True)
    new = (1.0 - SMOOTHING) * mixture + SMOOTHING / LANGS
    logw[...] = jnp.log(new)
    per_token = new / count * 2048.0
    weight = jnp.zeros(every.shape, F32)
    for l in range(LANGS):
        weight = jnp.where(every == l, per_token[l : l + 1], weight)
    tw[...] = weight
    for copy in across:
        copy.wait_recv()
    go.drain()


def join_stats(stats, lang, domain_weights, fin_x):
    vmem = pl.BlockSpec(memory_space=pltpu.VMEM)
    return pl.pallas_call(
        stats_body,
        out_shape=[
            jax.ShapeDtypeStruct((16, 128), F32),
            jax.ShapeDtypeStruct((16, 128), F32),
            jax.ShapeDtypeStruct((LANGS, 128), F32),
            jax.ShapeDtypeStruct((2, 4, 4, 2, 16, 1024), BF16),
        ],
        in_specs=[vmem] * 4,
        out_specs=[vmem] * 4,
        scratch_shapes=[
            pltpu.VMEM((2, 24, 128), F32),
            pltpu.VMEM((16, 24, 128), F32),
            pltpu.VMEM((2, 2, 24, 128), F32),
            pltpu.VMEM((2, 2, 24, 128), F32),
            pltpu.VMEM((LANGS, 128), F32),
            pltpu.VMEM((LANGS, 128), F32),
            pltpu.SemaphoreType.DMA((40,)),
            pltpu.SemaphoreType.DMA((40,)),
        ],
        compiler_params=pltpu.CompilerParams(collective_id=4, has_side_effects=True),
        name="stats",
    )(stats, lang, jnp.broadcast_to(domain_weights[:, None], (LANGS, 128)), fin_x)


def backward_body(
    x, mid, gain, lse, tw, tgt, d_t, f_own, f_far, head, normed, pre, down_w,
    grad_head, gate, up, down,
    vd, vo, vf, vh, vn, vp, r0, acc, rs, give, rp, dmid, comb, oth, s4, rg, gh,
    send, recv, hsend, hrecv, local, gsem,
):
    me = Place()
    a, b, c, p, f = me.a, me.b, me.c, me.p, me.f
    go = Copies(send, recv)
    plane = [me.on_ab(ring(a, i), ring(b, k)) for k, i in OFFSETS]
    homes = [
        (i, side, {"dp": me.dp if side == 0 else 1 - me.dp, "fsdp": 2 * ring(me.y, i) + me.dp, "tp": me.t})
        for i in range(4)
        for side in range(2)
    ]
    flips = [me.at(y=ring(me.y, k), c=1 - c) for k in range(4)]
    across_dp = [me.at(dp=1 - me.dp, y=ring(me.y, k), c=cc) for k in range(4) for cc in range(2)]
    greet(plane + [me.partner()] + flips + across_dp)
    loads = [
        pltpu.make_async_copy(src, dst, local.at[n])
        for n, (src, dst) in enumerate(
            ((head, vh), (f_far, vf), (d_t, vd), (f_own, vo), (normed, vn), (pre, vp))
        )
    ]
    across = []
    for m in ROWS:
        bb = ring(a, m)
        across.append(go.start(x.at[1 - c, bb], r0.at[bb], me.core()))
    for load in loads:
        load.start()
    sent = {}
    for n, m in enumerate(ROWS):
        bb = ring(b, m)
        across[n].wait_recv()
        total = x[c, bb].astype(F32) + r0[bb].astype(F32)
        acc[bb] = total.astype(BF16).reshape(acc.shape[1:])
        for i in range(4):
            if m or i:
                to = me.on_ab(ring(a, i), bb)
                sent[m, i] = go.start(acc.at[bb, ring(a, i)], rs.at[4 * m + i], to)
    for load in loads[:4]:
        load.wait()
    lanes = (((1,), (1,)), ((), ()))
    base = (f * 8 + me.t) * 1024

    def head_rows(n):
        at = pl.ds(pl.multiple_of(n * 128, 128), 128)
        logits = lax.dot_general(vh[at], vf[...], lanes, preferred_element_type=F32)
        vocab = lax.broadcasted_iota(jnp.int32, (128, 1024), 0) + (base + n * 128)
        hit = jnp.where(vocab == tgt[...], 1.0, 0.0)
        d = (tw[...] * (jnp.exp(logits - lse[...]) - hit)).astype(BF16)
        gh[at] = jnp.dot(d, vf[...], preferred_element_type=F32) + jnp.dot(
            vd[at], vo[...], preferred_element_type=F32
        )
        pltpu.make_async_copy(gh.at[at], grad_head.at[at], gsem.at[n]).start()

    pl.loop(0, 4)(head_rows)
    for copy in sent.values():
        copy.wait_recv()
    total = acc[b, a].astype(F32)
    for m, i in sent:
        total = total + rs[4 * m + i].astype(F32)
    first, second = total[0:16], total[16:32]
    own = jnp.where(p == 0, first, second)
    give[...] = jnp.where(p == 0, second, first).astype(BF16)
    swap = go.start(give, rp, me.partner())
    pl.loop(4, 5)(head_rows)
    swap.wait_recv()
    d_final = own + rp[...].astype(F32)
    middle = mid[...]
    inv = lax.rsqrt(jnp.mean(middle * middle, axis=1, keepdims=True) + EPSILON)
    scaled = d_final * gain[...]
    inner = jnp.mean(middle * scaled, axis=1, keepdims=True)
    dmid[c, b, a, p] = (inv * scaled - middle * inv * inv * inv * inner).astype(BF16)
    block = dmid.at[c, b, a, p]
    d1 = go.start(block, block, me.partner())
    pl.loop(5, 6)(head_rows)
    d1.wait_recv()
    d2 = to_plane(go, me, dmid.at[c, b, a])
    pl.loop(6, 8)(head_rows)
    loads[4].wait()
    loads[5].wait()
    low = lax.broadcasted_iota(jnp.int32, (1024, 128), 1) < 64
    h = vp[...]
    s = jax.nn.sigmoid(h)
    turned = pltpu.roll(h, 64, 1)
    act = (h * s * turned).astype(BF16)[:, :64]
    slope = turned * jnp.where(low, s * (1.0 + h * (1.0 - s)), pltpu.roll(s, 64, 1))
    d3 = []
    for k in (2, 1, 3, 0):
        for i in range(4):
            if k or i:
                d2[k, i].wait_recv()
        row = dmid.at[c, ring(b, 4 - k)]
        d3.append(go.start(row, row, me.core()))
    for copy in d3:
        copy.wait_recv()
    dm = dmid[...].reshape(1024, 1024)
    twice = jnp.concatenate([down_w[...], down_w[...]], axis=0)
    d_act = lax.dot_general(dm, twice, lanes, preferred_element_type=F32)
    d_both = (d_act * slope).astype(BF16)
    rows = (((0,), (0,)), ((), ()))
    g_gu = lax.dot_general(d_both, vn[...], rows, preferred_element_type=F32)
    g_dn = lax.dot_general(act, dm, rows, preferred_element_type=F32)
    for j in range(8):
        at = slice(128 * j, 128 * (j + 1))
        comb[j % 2, j // 2, 0:128] = g_gu[:, at].astype(BF16)
        comb[j % 2, j // 2, 128:192] = g_dn[:, at].astype(BF16)
    swap = go.start(comb.at[1 - me.dp], oth, me.neighbour())
    swap.wait_recv()
    s4[...] = (comb[me.dp].astype(F32) + oth[...].astype(F32)).astype(BF16)

    def homeward(i, side, to, src=0):
        n = 2 * i + side
        return pltpu.make_async_remote_copy(
            src_ref=s4.at[ring(me.y, i)],
            dst_ref=rg.at[src],
            send_sem=hsend.at[n],
            recv_sem=hrecv.at[src],
            device_id=to,
            device_id_type=MESH,
        )

    for i, side, to in homes:
        if i == 0 and side == 0:
            @pl.when(c != me.dp)
            def _(to=to):
                homeward(0, 0, to, f).start()

            @pl.when(c == me.dp)
            def _():
                rg[f] = s4[me.y]
        else:
            homeward(i, side, to, f).start()
    for j in range(8):
        arrived = homeward(1, 0, homes[2][2], j)

        @pl.when(jnp.logical_or(f != j, c != me.dp))
        def _(arrived=arrived):
            arrived.wait_recv()

        got = rg[j].astype(F32)
        gu = got[0:128].T
        gate[:, 64 * j : 64 * (j + 1)] = gu[:, :64]
        up[:, 64 * j : 64 * (j + 1)] = gu[:, 64:]
        down[64 * j : 64 * (j + 1)] = got[128:192]
    for i, side, to in homes:
        if i == 0 and side == 0:
            @pl.when(c != me.dp)
            def _(to=to):
                homeward(0, 0, to, f).wait_send()
        else:
            homeward(i, side, to, f).wait_send()
    for n in range(8):
        at = pl.ds(128 * n, 128)
        pltpu.make_async_copy(gh.at[at], grad_head.at[at], gsem.at[n]).wait()
    go.drain()


def backward(x, mid, gain, lse, tw, tgt, d_t, f_own, f_far, head, normed, pre, down_w):
    vmem = pl.BlockSpec(memory_space=pltpu.VMEM)
    hbm = pl.BlockSpec(memory_space=pl.ANY)
    shape = jax.ShapeDtypeStruct
    big = pltpu.VMEM((1024, 1024), BF16)
    return pl.pallas_call(
        backward_body,
        out_shape=[
            shape((1024, 1024), F32),
            shape((128, 512), F32),
            shape((128, 512), F32),
            shape((512, 128), F32),
        ],
        in_specs=[vmem] * 6 + [hbm] * 6 + [vmem],
        out_specs=[hbm] + [vmem] * 3,
        scratch_shapes=[
            big, big, big, big, big,
            pltpu.VMEM((1024, 128), F32),
            pltpu.VMEM((4, 128, 1024), BF16),
            pltpu.VMEM((4, 4, 32, 1024), BF16),
            pltpu.VMEM((16, 32, 1024), BF16),
            pltpu.VMEM((16, 1024), BF16),
            pltpu.VMEM((16, 1024), BF16),
            pltpu.VMEM((2, 4, 4, 2, 16, 1024), BF16),
            pltpu.VMEM((2, 4, 192, 128), BF16),
            pltpu.VMEM((4, 192, 128), BF16),
            pltpu.VMEM((4, 192, 128), BF16),
            pltpu.VMEM((8, 192, 128), BF16),
            pltpu.VMEM((1024, 1024), F32),
            pltpu.SemaphoreType.DMA((50,)),
            pltpu.SemaphoreType.DMA((50,)),
            pltpu.SemaphoreType.DMA((8,)),
            pltpu.SemaphoreType.DMA((8,)),
            pltpu.SemaphoreType.DMA((6,)),
            pltpu.SemaphoreType.DMA((8,)),
        ],
        compiler_params=pltpu.CompilerParams(
            collective_id=5, has_side_effects=True, vmem_limit_bytes=56 * 2**20
        ),
        name="backward",
    )(x.reshape(2, 4, 128, 1024), mid, gain, lse, tw, tgt, d_t, f_own, f_far, head, normed, pre, down_w)


def row_logits(row_block, head):
    return lax.dot_general(row_block, head, (((1,), (1,)), ((), ())), preferred_element_type=F32)


def piece_stats(logits, part_targets, vocab_start):
    vocab_rows = vocab_start + jnp.arange(logits.shape[0], dtype=jnp.int32)
    high_val = jnp.max(logits, axis=0)
    exp_total = jnp.sum(jnp.exp(logits - high_val[None, :]), axis=0)
    picked = jnp.sum(jnp.where(vocab_rows[:, None] == part_targets[None, :], logits, 0.0), axis=0)
    return (high_val, exp_total, picked)


def local(
    ref_hidden,
    proxy_hidden,
    targets,
    languages,
    ref_gain,
    ref_head,
    proxy_gain_in,
    proxy_gain_out,
    gate_weight,
    up_weight,
    down_weight,
    proxy_head,
    domain_weights,
):
    me = Place()
    vocab_rows = ref_head.shape[0]
    vocab_start = lax.axis_index(("fsdp", "tp")) * vocab_rows
    mine = lambda v: lax.dynamic_slice_in_dim(v, me.t * 16, 16, 0)
    hidden = mine(proxy_hidden)
    ids = jnp.tile(jnp.stack([mine(targets), mine(languages)]), (4, 8))
    lanes = lax.broadcasted_iota(jnp.int32, (8, 128), 1)
    ids = jnp.where(lax.div(lanes, 16) == me.a * 2 + me.p, ids, 0)
    normed_in, pre, final_own, fin_x, mid_sum, ref_stats, group_targets, langs, down_w = forward(
        ids,
        hidden,
        proxy_gain_in[None],
        proxy_gain_out[None],
        ref_hidden,
        ref_gain[None],
        gate_weight,
        up_weight,
        down_weight.reshape(8, 64, 128),
        ref_head,
    )
    group_targets = group_targets.reshape(2048)
    normed_in = normed_in.reshape(1024, 1024)
    pre = pre.reshape(1024, 128)
    final_own = final_own.reshape(1024, 1024)
    logits_t = row_logits(proxy_head, final_own)
    proxy_stats = piece_stats(logits_t, group_targets[:1024], vocab_start)
    stats = jnp.concatenate([ref_stats.reshape(3, 8, 128), jnp.stack(proxy_stats).reshape(3, 8, 128)])
    stats = stats.reshape(6, 2, 4, 128).transpose(1, 0, 2, 3).reshape(2, 24, 128)
    lse, token_weight, log_weights, final_far = join_stats(
        stats, langs.reshape(16, 128), domain_weights, fin_x
    )
    final_far = final_far.reshape(1024, 1024)
    lse, token_weight = lse.reshape(2048), token_weight.reshape(2048)
    vocab_cols = vocab_start + jnp.arange(vocab_rows, dtype=jnp.int32)
    hit = (vocab_cols[:, None] == group_targets[None, :1024]).astype(F32)
    d_t = (token_weight[None, :1024] * (jnp.exp(logits_t - lse[None, :1024]) - hit)).astype(BF16)
    d_part = lax.dot_general(
        d_t, proxy_head, (((0,), (0,)), ((), ())), preferred_element_type=F32
    ).astype(BF16)
    grad_head, grad_gate, grad_up, grad_down = backward(
        d_part,
        mid_sum,
        proxy_gain_out[None],
        lse[None, 1024:],
        token_weight[None, 1024:],
        group_targets[None, 1024:],
        d_t,
        final_own,
        final_far,
        proxy_head,
        normed_in,
        pre,
        down_w,
    )
    return (log_weights[:, 0], grad_gate, grad_up, grad_down, grad_head)


def solution(mesh):
    in_specs = (
        P(("dp", "fsdp", "tp"), None),
        P(("dp", "fsdp"), None),
        P(("dp", "fsdp")),
        P(("dp", "fsdp")),
        P(),
        P(("fsdp", "tp"), None),
        P(),
        P(),
        P("fsdp", "tp"),
        P("fsdp", "tp"),
        P("tp", "fsdp"),
        P(("fsdp", "tp"), None),
        P(),
    )
    out_specs = (P(), P("fsdp", "tp"), P("fsdp", "tp"), P("tp", "fsdp"), P(("fsdp", "tp"), None))
    return jax.shard_map(local, mesh=mesh, in_specs=in_specs, out_specs=out_specs, check_vma=False)
```

```python
import functools

import jax
import jax.numpy as jnp
from jax import lax
from jax.experimental import pallas as pl
from jax.experimental.pallas import tpu as pltpu
from jax.sharding import PartitionSpec as P

EPSILON = 1e-05
STEP_SIZE = 1.0
SMOOTHING = 0.001
LANGS = 64
MESH = pl.DeviceIdType.MESH
F32, BF16 = jnp.float32, jnp.bfloat16


class Place:
    def __init__(self):
        self.dp = lax.axis_index("dp")
        f, t = lax.axis_index("fsdp"), lax.axis_index("tp")
        self.f, self.t = f, t
        self.y, self.c = lax.div(f, 2), lax.rem(f, 2)
        self.z, self.xh = lax.div(t, 2), lax.rem(t, 2)
        self.p = self.xh
        c = self.c
        self.a = (1 - c) * self.y + c * self.z
        self.b = (1 - c) * self.z + c * self.y

    def at(self, dp=None, y=None, z=None, xh=None, c=None):
        pick = lambda new, old: old if new is None else new
        dp, y, z = pick(dp, self.dp), pick(y, self.y), pick(z, self.z)
        xh, c = pick(xh, self.xh), pick(c, self.c)
        return {"dp": dp, "fsdp": y * 2 + c, "tp": z * 2 + xh}

    def on_a(self, a):
        c = self.c
        return self.at(y=(1 - c) * a + c * self.y, z=(1 - c) * self.z + c * a)

    def on_b(self, b):
        c = self.c
        return self.at(y=(1 - c) * self.y + c * b, z=(1 - c) * b + c * self.z)

    def on_ab(self, a, b):
        c = self.c
        return self.at(y=(1 - c) * a + c * b, z=(1 - c) * b + c * a)

    def core(self):
        return self.at(c=1 - self.c)

    def partner(self):
        return self.at(xh=1 - self.xh)

    def neighbour(self):
        return self.at(dp=1 - self.dp)

    def opposite(self):
        return self.at(dp=1 - self.dp, xh=1 - self.xh)


class Copies:
    def __init__(self, send, recv):
        self.send, self.recv, self.n, self.all = send, recv, 0, []

    def start(self, src, dst, to):
        copy = pltpu.make_async_remote_copy(
            src_ref=src,
            dst_ref=dst,
            send_sem=self.send.at[self.n],
            recv_sem=self.recv.at[self.n],
            device_id=to,
            device_id_type=MESH,
        )
        copy.start()
        self.n += 1
        self.all.append(copy)
        return copy

    def drain(self):
        for copy in self.all:
            copy.wait_send()


def greet(peers):
    barrier = pltpu.get_barrier_semaphore()
    for peer in peers:
        pl.semaphore_signal(barrier, inc=1, device_id=peer, device_id_type=MESH)
    pl.semaphore_wait(barrier, len(peers))


def ring(i, k):
    return lax.rem(i + k, 4)


OFFSETS = [(k, i) for k in (2, 1, 3, 0) for i in range(4) if k or i]
ROWS = (2, 3, 1, 0)


def rms_rows(values, gain):
    values = values.astype(F32)
    return values * lax.rsqrt(jnp.mean(values * values, axis=-1, keepdims=True) + EPSILON) * gain


def to_plane(go, me, view, slot=None):
    sent = {}
    for k, i in OFFSETS:
        to = me.on_ab(ring(me.a, i), ring(me.b, k))
        sent[k, i] = go.start(view, view if slot is None else slot(k, i), to)
    return sent


def forward_body(
    ids, hid, gain_in, gain_out, refh, ref_gain, gate, up, down, head,
    normed, pre, fin, fin_x, mid, ref_st, tl, dnw,
    idsg, guw, ref_all, headv, rhs, logit, x, rs, give, rp,
    send, recv, local,
):
    me = Place()
    a, b, c, p, f = me.a, me.b, me.c, me.p, me.f
    go = Copies(send, recv)
    plane = [me.on_ab(ring(a, i), ring(b, k)) for k, i in OFFSETS]
    flips = [me.at(y=ring(me.y, k), c=1 - c) for k in range(4)]
    greet(plane + flips + [me.partner(), me.neighbour()])
    take_head = pltpu.make_async_copy(head, headv, local.at[0])
    take_head.start()
    normed[b, a] = rms_rows(hid[...], gain_in[...]).astype(BF16).reshape(2, 16, 1024)
    s2 = to_plane(go, me, normed.at[b, a])
    idsg[b, a] = ids[...]
    s2_ids = to_plane(go, me, idsg.at[b, a])
    here = pl.ds(pl.multiple_of(f * 128, 128), 128)
    w_sent = []
    for k in range(4):
        yy = ring(me.y, k)
        part = pl.ds(pl.multiple_of(yy * 128, 128), 128)
        for cc in (c, 1 - c) if k else (1 - c,):
            to = me.at(y=yy, c=cc)
            w_sent.append(go.start(gate.at[:, part], guw.at[f, :, pl.ds(0, 128)], to))
            w_sent.append(go.start(up.at[:, part], guw.at[f, :, pl.ds(128, 128)], to))
            w_sent.append(go.start(down.at[part], dnw.at[:, here], to))
    part = pl.ds(pl.multiple_of(me.y * 128, 128), 128)
    guw[f, :, 0:128] = gate[:, part]
    guw[f, :, 128:256] = up[:, part]
    dnw[:, here] = down[part]
    ref_all[c, b, a, p] = rms_rows(refh[...], ref_gain[...]).astype(BF16)
    r1 = go.start(ref_all.at[c, b, a, p], ref_all.at[c, b, a, p], me.partner())
    for copy in w_sent:
        copy.wait_recv()
    rs_sent = {}
    for n, k in enumerate((2, 1, 3, 0)):
        for i in range(4):
            if k or i:
                s2[k, i].wait_recv()
        m = (4 - k) % 4
        bb = ring(b, m)
        h = jnp.dot(
            normed[bb].reshape(128, 1024), guw[...].reshape(1024, 256),
            preferred_element_type=F32,
        )
        pre[bb] = h
        g = h[:, :128]
        h = (g * jax.nn.sigmoid(g) * h[:, 128:]).astype(BF16)
        h = jnp.dot(h, dnw[...], preferred_element_type=F32).astype(BF16)
        x[bb] = h.reshape(4, 32, 1024)
        for i in range(4):
            if m or i:
                to = me.on_ab(ring(a, i), bb)
                rs_sent[m, i] = go.start(x.at[bb, ring(a, i)], rs.at[4 * m + i], to)
    r1.wait_recv()
    unit = ref_all.at[c, b, a]
    r2 = [go.start(unit, unit, me.on_a(ring(a, k))) for k in (1, 3, 2)]
    for copy in s2_ids.values():
        copy.wait_recv()
    for bb in range(4):
        row = idsg[bb, 0] + idsg[bb, 1] + idsg[bb, 2] + idsg[bb, 3]
        tl[0, 0, 4 * c + bb] = row[0:1]
        tl[0, 1, 4 * c + bb] = row[1:2]
    mine = pl.ds(4 * c, 4)
    ids_across = [
        go.start(tl.at[0, n, mine], tl.at[0, n, mine], me.core()) for n in range(2)
    ]
    for copy in r2 + ids_across:
        copy.wait_recv()
    ids_far = go.start(tl.at[0], tl.at[1], me.neighbour())
    right_b, left_b = me.on_b(ring(b, 1)), me.on_b(ring(b, 3))
    unit = ref_all.at[c, b]
    r3 = [go.start(unit, unit, right_b), go.start(unit, unit, left_b)]
    cross = {0: go.start(unit, unit, me.core())}
    vocab = lax.broadcasted_iota(jnp.int32, (1024, 256), 0) + (f * 8 + me.t) * 1024

    def ref_rows(m):
        b_own, b_far = ring(b, m), ring(a, m)
        rhs[0:128] = ref_all[c, b_own].reshape(128, 4096)
        rhs[128:256] = ref_all[1 - c, b_far].reshape(128, 4096)

        @pl.loop(0, 4)
        def _(n):
            at = pl.ds(pl.multiple_of(n * 256, 256), 256)
            logit[at] = lax.dot_general(
                headv[at], rhs[...], (((1,), (1,)), ((), ())), preferred_element_type=F32
            )

        value = logit[...]
        high = jnp.max(value, axis=0, keepdims=True)
        want = jnp.concatenate([tl[0, 0, 4 * c + b_own], tl[0, 0, 4 * (1 - c) + b_far]], axis=1)
        picked = jnp.sum(jnp.where(vocab == want, value, 0.0), axis=0, keepdims=True)
        total = jnp.sum(jnp.exp(value - high), axis=0, keepdims=True)
        for s, got in enumerate((high, total, picked)):
            ref_st[s, 4 * c + b_own] = got[:, :128]
            ref_st[s, 4 * (1 - c) + b_far] = got[:, 128:]

    take_head.wait()
    for copy in rs_sent.values():
        copy.wait_recv()
    total = x[b, a].astype(F32)
    for m, i in rs_sent:
        total = total + rs[4 * m + i].astype(F32)
    give[...] = total.astype(BF16)
    swap = go.start(give, rp, me.partner())
    cross[0].wait_recv()
    ref_rows(0)
    swap.wait_recv()
    middle = hid[...].astype(F32) + (give[...].astype(F32) + rp[...].astype(F32))
    mid[...] = middle
    fin[c, b, a] = rms_rows(middle, gain_out[...]).astype(BF16).reshape(2, 16, 1024)
    f2 = to_plane(go, me, fin.at[c, b, a])
    f_x = go.start(fin.at[c, b, a], fin_x, me.neighbour())
    r3[0].wait_recv()
    half = ref_all.at[c, ring(b, 3), pl.ds(0, 2)]
    r4 = [go.start(half, half, right_b)]
    r3[1].wait_recv()
    half = ref_all.at[c, ring(b, 1), pl.ds(2, 2)]
    r4.append(go.start(half, half, left_b))
    for m in (3, 1):
        unit = ref_all.at[c, ring(b, m)]
        cross[m] = go.start(unit, unit, me.core())
    cross[3].wait_recv()
    ref_rows(3)
    f3 = []
    for k in (2, 1, 3, 0):
        for i in range(4):
            if k or i:
                f2[k, i].wait_recv()
        row = fin.at[c, ring(b, 4 - k)]
        f3.append(go.start(row, row, me.core()))
    for copy in r4:
        copy.wait_recv()
    unit = ref_all.at[c, ring(b, 2)]
    cross[2] = go.start(unit, unit, me.core())
    cross[1].wait_recv()
    ref_rows(1)
    cross[2].wait_recv()
    ref_rows(2)
    for copy in f3 + [f_x, ids_far]:
        copy.wait_recv()
    go.drain()


def forward(ids, hid, gain_in, gain_out, refh, ref_gain, gate, up, down, head):
    vmem = pl.BlockSpec(memory_space=pltpu.VMEM)
    shape = jax.ShapeDtypeStruct
    return pl.pallas_call(
        forward_body,
        out_shape=[
            shape((4, 4, 2, 16, 1024), BF16),
            shape((4, 128, 256), F32),
            shape((2, 4, 4, 2, 16, 1024), BF16),
            shape((2, 16, 1024), BF16),
            shape((32, 1024), F32),
            shape((3, 8, 1, 128), F32),
            shape((2, 2, 8, 1, 128), jnp.int32),
            shape((128, 1024), BF16),
        ],
        in_specs=[vmem] * 9 + [pl.BlockSpec(memory_space=pl.ANY)],
        out_specs=[vmem] * 8,
        scratch_shapes=[
            pltpu.VMEM((4, 4, 8, 128), jnp.int32),
            pltpu.VMEM((8, 128, 256), BF16),
            pltpu.VMEM((2, 4, 4, 2, 16, 4096), BF16),
            pltpu.VMEM((1024, 4096), BF16),
            pltpu.VMEM((256, 4096), BF16),
            pltpu.VMEM((1024, 256), F32),
            pltpu.VMEM((4, 4, 32, 1024), BF16),
            pltpu.VMEM((16, 32, 1024), BF16),
            pltpu.VMEM((32, 1024), BF16),
            pltpu.VMEM((32, 1024), BF16),
            pltpu.SemaphoreType.DMA((110,)),
            pltpu.SemaphoreType.DMA((110,)),
            pltpu.SemaphoreType.DMA((1,)),
        ],
        compiler_params=pltpu.CompilerParams(
            collective_id=1, has_side_effects=True, vmem_limit_bytes=60 * 2**20
        ),
        name="forward",
    )(ids, hid, gain_in, gain_out, refh, ref_gain, gate, up, down, head)


def join_all(pieces):
    out = []
    for base in (0, 12):
        high = functools.reduce(jnp.maximum, [s[base : base + 4] for s in pieces])
        total = pick = None
        for s in pieces:
            t = s[base + 4 : base + 8] * jnp.exp(s[base : base + 4] - high)
            k = s[base + 8 : base + 12]
            total, pick = (t, k) if total is None else (total + t, pick + k)
        out += [high, total, pick]
    return jnp.concatenate(out, axis=0)


def stats_body(
    st, lang, dw, fin_x, lse, tw, logw, fin, slot_c, slot_yz, slot_x, both, ls, lc, send, recv
):
    me = Place()
    a, b, c, p = me.a, me.b, me.c, me.p
    go = Copies(send, recv)
    plane = [me.on_ab(ring(a, i), ring(b, k)) for k, i in OFFSETS]
    x_peers = [me.partner(), me.neighbour(), me.opposite()]
    greet(plane + x_peers + [me.core()])
    slot_c[c] = st[c]
    half = go.start(st.at[1 - c], slot_c.at[c], me.core())
    fin[c, b, a] = fin_x[...]
    half.wait_recv()
    yz = me.y * 4 + me.z
    slot_c_other = slot_c[1 - c]
    mine = slot_c[c]
    first = jnp.where(c == 0, mine, slot_c_other)
    second = jnp.where(c == 0, slot_c_other, mine)
    slot_yz[yz] = join_all([first, second])
    sent = to_plane(go, me, slot_yz.at[yz])
    beside = to_plane(go, me, fin_x, lambda k, i: fin.at[c, b, a])
    for copy in sent.values():
        copy.wait_recv()
    slot_x[0, p] = join_all([slot_yz[j] for j in range(16)])
    spread = [
        go.start(slot_x.at[0, p], slot_x.at[g, p], to) for g, to in zip((0, 1, 1), x_peers)
    ]
    for copy in spread:
        copy.wait_recv()
    both[c, 0] = join_all([slot_x[0, 0], slot_x[0, 1]])
    both[c, 1] = join_all([slot_x[1, 0], slot_x[1, 1]])
    share = go.start(both.at[c], both.at[c], me.core())
    across = []
    for k in (2, 1, 3, 0):
        for i in range(4):
            if k or i:
                beside[k, i].wait_recv()
        row = fin.at[c, ring(b, 4 - k)]
        across.append(go.start(row, row, me.core()))
    share.wait_recv()
    excess = [None, None]
    for g in range(2):
        now = [jnp.concatenate([both[0, g, 4 * i : 4 * i + 4], both[1, g, 4 * i : 4 * i + 4]]) for i in range(6)]
        ref_loss = now[0] + jnp.log(now[1]) - now[2]
        proxy_lse = now[3] + jnp.log(now[4])
        lse[8 * g : 8 * g + 8] = proxy_lse
        excess[g] = jnp.maximum(proxy_lse - now[5] - ref_loss, 0.0)
    every = lang[...]
    for l in range(LANGS):
        here = every == l
        e = jnp.where(here[:8], excess[0], 0.0) + jnp.where(here[8:], excess[1], 0.0)
        n = jnp.where(here[:8], 1.0, 0.0) + jnp.where(here[8:], 1.0, 0.0)
        ls[l : l + 1] = jnp.sum(e, axis=0, keepdims=True)
        lc[l : l + 1] = jnp.sum(n, axis=0, keepdims=True)
    wide = lambda v: jnp.broadcast_to(jnp.sum(v[...], axis=1, keepdims=True), (LANGS, 128))
    count = jnp.maximum(wide(lc), 1.0)
    score = jnp.log(dw[...]) + STEP_SIZE * (wide(ls) / count)
    score = jnp.exp(score - jnp.max(score, axis=0, keepdims=True))
    mixture = score / jnp.sum(score, axis=0, keepdims=True)
    new = (1.0 - SMOOTHING) * mixture + SMOOTHING / LANGS
    logw[...] = jnp.log(new)
    per_token = new / count * 2048.0
    weight = jnp.zeros(every.shape, F32)
    for l in range(LANGS):
        weight = jnp.where(every == l, per_token[l : l + 1], weight)
    tw[...] = weight
    for copy in across:
        copy.wait_recv()
    go.drain()


def join_stats(stats, lang, domain_weights, fin_x):
    vmem = pl.BlockSpec(memory_space=pltpu.VMEM)
    return pl.pallas_call(
        stats_body,
        out_shape=[
            jax.ShapeDtypeStruct((16, 128), F32),
            jax.ShapeDtypeStruct((16, 128), F32),
            jax.ShapeDtypeStruct((LANGS, 128), F32),
            jax.ShapeDtypeStruct((2, 4, 4, 2, 16, 1024), BF16),
        ],
        in_specs=[vmem] * 4,
        out_specs=[vmem] * 4,
        scratch_shapes=[
            pltpu.VMEM((2, 24, 128), F32),
            pltpu.VMEM((16, 24, 128), F32),
            pltpu.VMEM((2, 2, 24, 128), F32),
            pltpu.VMEM((2, 2, 24, 128), F32),
            pltpu.VMEM((LANGS, 128), F32),
            pltpu.VMEM((LANGS, 128), F32),
            pltpu.SemaphoreType.DMA((40,)),
            pltpu.SemaphoreType.DMA((40,)),
        ],
        compiler_params=pltpu.CompilerParams(collective_id=4, has_side_effects=True),
        name="stats",
    )(stats, lang, jnp.broadcast_to(domain_weights[:, None], (LANGS, 128)), fin_x)


def backward_body(
    x, mid, gain, lse, tw, tgt, d_t, f_own, f_far, head, normed, pre, down_w,
    grad_head, gate, up, down,
    vd, vo, vf, vh, vn, vp, r0, acc, rs, give, rp, dmid, comb, oc, sc, ox, sx, rg, gh,
    send, recv, hsend, hrecv, local, gsem,
):
    me = Place()
    a, b, c, p, f = me.a, me.b, me.c, me.p, me.f
    go = Copies(send, recv)
    plane = [me.on_ab(ring(a, i), ring(b, k)) for k, i in OFFSETS]
    across_dp = [me.at(dp=1 - me.dp, y=ring(me.y, k)) for k in range(4)]
    greet(plane + [me.partner(), me.core()] + across_dp)
    loads = [
        pltpu.make_async_copy(src, dst, local.at[n])
        for n, (src, dst) in enumerate(
            ((head, vh), (f_far, vf), (d_t, vd), (f_own, vo), (normed, vn), (pre, vp))
        )
    ]
    across = []
    for m in ROWS:
        bb = ring(a, m)
        across.append(go.start(x.at[1 - c, bb], r0.at[bb], me.core()))
    for load in loads:
        load.start()
    sent = {}
    for n, m in enumerate(ROWS):
        bb = ring(b, m)
        across[n].wait_recv()
        total = x[c, bb].astype(F32) + r0[bb].astype(F32)
        acc[bb] = total.astype(BF16).reshape(acc.shape[1:])
        for i in range(4):
            if m or i:
                to = me.on_ab(ring(a, i), bb)
                sent[m, i] = go.start(acc.at[bb, ring(a, i)], rs.at[4 * m + i], to)
    for load in loads[:4]:
        load.wait()
    lanes = (((1,), (1,)), ((), ()))
    base = (f * 8 + me.t) * 1024

    def head_rows(n):
        at = pl.ds(pl.multiple_of(n * 128, 128), 128)
        logits = lax.dot_general(vh[at], vf[...], lanes, preferred_element_type=F32)
        vocab = lax.broadcasted_iota(jnp.int32, (128, 1024), 0) + (base + n * 128)
        hit = jnp.where(vocab == tgt[...], 1.0, 0.0)
        d = (tw[...] * (jnp.exp(logits - lse[...]) - hit)).astype(BF16)
        gh[at] = jnp.dot(d, vf[...], preferred_element_type=F32) + jnp.dot(
            vd[at], vo[...], preferred_element_type=F32
        )
        pltpu.make_async_copy(gh.at[at], grad_head.at[at], gsem.at[n]).start()

    pl.loop(0, 4)(head_rows)
    for copy in sent.values():
        copy.wait_recv()
    total = acc[b, a].astype(F32)
    for m, i in sent:
        total = total + rs[4 * m + i].astype(F32)
    give[...] = total.astype(BF16)
    swap = go.start(give, rp, me.partner())
    pl.loop(4, 5)(head_rows)
    swap.wait_recv()
    d_final = give[...].astype(F32) + rp[...].astype(F32)
    middle = mid[...]
    inv = lax.rsqrt(jnp.mean(middle * middle, axis=1, keepdims=True) + EPSILON)
    scaled = d_final * gain[...]
    inner = jnp.mean(middle * scaled, axis=1, keepdims=True)
    d_mid = (inv * scaled - middle * inv * inv * inv * inner).astype(BF16)
    dmid[b, a] = d_mid.reshape(2, 16, 1024)
    d2 = to_plane(go, me, dmid.at[b, a])
    pl.loop(5, 8)(head_rows)
    loads[4].wait()
    loads[5].wait()
    g, u = vp[:, :128], vp[:, 128:]
    s = jax.nn.sigmoid(g)
    act = (g * s * u).astype(BF16)
    gate_slope = u * s * (1.0 + g * (1.0 - s))
    up_slope = g * s
    for copy in d2.values():
        copy.wait_recv()
    dm = dmid[...].reshape(512, 1024)
    d_act = lax.dot_general(dm, down_w[...], lanes, preferred_element_type=F32)
    rows = (((0,), (0,)), ((), ()))
    for n, (left, right) in enumerate(
        (
            ((d_act * gate_slope).astype(BF16), vn[...]),
            ((d_act * up_slope).astype(BF16), vn[...]),
            (act, dm),
        )
    ):
        grad = lax.dot_general(left, right, rows, preferred_element_type=F32).astype(BF16)
        for j in range(8):
            comb[j % 2, j // 2 % 2, j // 4, 128 * n : 128 * (n + 1)] = grad[
                :, 128 * j : 128 * (j + 1)
            ]
    swap = go.start(comb.at[1 - c], oc, me.core())
    swap.wait_recv()
    sc[...] = (comb[c].astype(F32) + oc[...].astype(F32)).astype(BF16)
    swap = go.start(sc.at[1 - me.dp], ox, me.neighbour())
    swap.wait_recv()
    sx[...] = (sc[me.dp].astype(F32) + ox[...].astype(F32)).astype(BF16)
    half, odd = lax.div(me.y, 2), lax.rem(me.y, 2)

    def homeward(e, side, src):
        h = lax.rem(half + e, 2)
        return pltpu.make_async_remote_copy(
            src_ref=sx.at[h],
            dst_ref=rg.at[src],
            send_sem=hsend.at[2 * e + side],
            recv_sem=hrecv.at[src],
            device_id=me.at(dp=1 - me.dp if side else me.dp, y=2 * h + me.dp),
            device_id_type=MESH,
        )

    stays = odd == me.dp
    for e, side in ((1, 1), (1, 0), (0, 1)):
        homeward(e, side, me.y).start()

    @pl.when(jnp.logical_not(stays))
    def _():
        homeward(0, 0, me.y).start()

    @pl.when(stays)
    def _():
        rg[me.y] = sx[half]

    for j in range(4):

        @pl.when(jnp.logical_or(me.y != j, jnp.logical_not(stays)))
        def _(j=j):
            homeward(1, 1, j).wait_recv()

        at = slice(128 * j, 128 * (j + 1))
        got = rg[j].astype(F32)
        gate[:, at] = got[0:128].T
        up[:, at] = got[128:256].T
        down[at] = got[256:384]
    for e, side in ((1, 1), (1, 0), (0, 1)):
        homeward(e, side, me.y).wait_send()

    @pl.when(jnp.logical_not(stays))
    def _():
        homeward(0, 0, me.y).wait_send()

    for n in range(8):
        at = pl.ds(128 * n, 128)
        pltpu.make_async_copy(gh.at[at], grad_head.at[at], gsem.at[n]).wait()
    go.drain()


def backward(x, mid, gain, lse, tw, tgt, d_t, f_own, f_far, head, normed, pre, down_w):
    vmem = pl.BlockSpec(memory_space=pltpu.VMEM)
    hbm = pl.BlockSpec(memory_space=pl.ANY)
    shape = jax.ShapeDtypeStruct
    big = pltpu.VMEM((1024, 1024), BF16)
    return pl.pallas_call(
        backward_body,
        out_shape=[
            shape((1024, 1024), F32),
            shape((128, 512), F32),
            shape((128, 512), F32),
            shape((512, 128), F32),
        ],
        in_specs=[vmem] * 6 + [hbm] * 6 + [vmem],
        out_specs=[hbm] + [vmem] * 3,
        scratch_shapes=[
            big, big, big, big,
            pltpu.VMEM((512, 1024), BF16),
            pltpu.VMEM((512, 256), F32),
            pltpu.VMEM((4, 128, 1024), BF16),
            pltpu.VMEM((4, 4, 32, 1024), BF16),
            pltpu.VMEM((16, 32, 1024), BF16),
            pltpu.VMEM((32, 1024), BF16),
            pltpu.VMEM((32, 1024), BF16),
            pltpu.VMEM((4, 4, 2, 16, 1024), BF16),
            pltpu.VMEM((2, 2, 2, 384, 128), BF16),
            pltpu.VMEM((2, 2, 384, 128), BF16),
            pltpu.VMEM((2, 2, 384, 128), BF16),
            pltpu.VMEM((2, 384, 128), BF16),
            pltpu.VMEM((2, 384, 128), BF16),
            pltpu.VMEM((4, 384, 128), BF16),
            pltpu.VMEM((1024, 1024), F32),
            pltpu.SemaphoreType.DMA((50,)),
            pltpu.SemaphoreType.DMA((50,)),
            pltpu.SemaphoreType.DMA((4,)),
            pltpu.SemaphoreType.DMA((4,)),
            pltpu.SemaphoreType.DMA((6,)),
            pltpu.SemaphoreType.DMA((8,)),
        ],
        compiler_params=pltpu.CompilerParams(
            collective_id=5, has_side_effects=True, vmem_limit_bytes=56 * 2**20
        ),
        name="backward",
    )(x.reshape(2, 4, 128, 1024), mid, gain, lse, tw, tgt, d_t, f_own, f_far, head, normed, pre, down_w)


def row_logits(row_block, head):
    return lax.dot_general(row_block, head, (((1,), (1,)), ((), ())), preferred_element_type=F32)


def piece_stats(logits, part_targets, vocab_start):
    vocab_rows = vocab_start + jnp.arange(logits.shape[0], dtype=jnp.int32)
    high_val = jnp.max(logits, axis=0)
    exp_total = jnp.sum(jnp.exp(logits - high_val[None, :]), axis=0)
    picked = jnp.sum(jnp.where(vocab_rows[:, None] == part_targets[None, :], logits, 0.0), axis=0)
    return (high_val, exp_total, picked)


def local(
    ref_hidden,
    proxy_hidden,
    targets,
    languages,
    ref_gain,
    ref_head,
    proxy_gain_in,
    proxy_gain_out,
    gate_weight,
    up_weight,
    down_weight,
    proxy_head,
    domain_weights,
):
    me = Place()
    vocab_rows = ref_head.shape[0]
    vocab_start = lax.axis_index(("fsdp", "tp")) * vocab_rows
    mine = lambda v: lax.dynamic_slice_in_dim(v, me.z * 32, 32, 0)
    ids = jnp.tile(jnp.stack([mine(targets), mine(languages)]), (4, 4))
    lanes = lax.broadcasted_iota(jnp.int32, (8, 128), 1)
    ids = jnp.where(lax.div(lanes, 32) == me.a, ids, 0)
    normed_in, pre, final_own, fin_x, mid_sum, ref_stats, ids, down_w = forward(
        ids,
        mine(proxy_hidden),
        proxy_gain_in[None],
        proxy_gain_out[None],
        ref_hidden,
        ref_gain[None],
        gate_weight,
        up_weight,
        down_weight,
        ref_head,
    )
    group_targets, langs = ids[:, 0].reshape(2048), ids[:, 1].reshape(16, 128)
    normed_in = normed_in.reshape(512, 1024)
    pre = pre.reshape(512, 256)
    final_own = final_own.reshape(1024, 1024)
    logits_t = row_logits(proxy_head, final_own)
    proxy_stats = piece_stats(logits_t, group_targets[:1024], vocab_start)
    stats = jnp.concatenate([ref_stats.reshape(3, 8, 128), jnp.stack(proxy_stats).reshape(3, 8, 128)])
    stats = stats.reshape(6, 2, 4, 128).transpose(1, 0, 2, 3).reshape(2, 24, 128)
    lse, token_weight, log_weights, final_far = join_stats(
        stats, langs, domain_weights, fin_x
    )
    final_far = final_far.reshape(1024, 1024)
    lse, token_weight = lse.reshape(2048), token_weight.reshape(2048)
    vocab_cols = vocab_start + jnp.arange(vocab_rows, dtype=jnp.int32)
    hit = (vocab_cols[:, None] == group_targets[None, :1024]).astype(F32)
    d_t = (token_weight[None, :1024] * (jnp.exp(logits_t - lse[None, :1024]) - hit)).astype(BF16)
    d_part = lax.dot_general(
        d_t, proxy_head, (((0,), (0,)), ((), ())), preferred_element_type=F32
    ).astype(BF16)
    grad_head, grad_gate, grad_up, grad_down = backward(
        d_part,
        mid_sum,
        proxy_gain_out[None],
        lse[None, 1024:],
        token_weight[None, 1024:],
        group_targets[None, 1024:],
        d_t,
        final_own,
        final_far,
        proxy_head,
        normed_in,
        pre,
        down_w,
    )
    return (log_weights[:, 0], grad_gate, grad_up, grad_down, grad_head)


def solution(mesh):
    in_specs = (
        P(("dp", "fsdp", "tp"), None),
        P(("dp", "fsdp"), None),
        P(("dp", "fsdp")),
        P(("dp", "fsdp")),
        P(),
        P(("fsdp", "tp"), None),
        P(),
        P(),
        P("fsdp", "tp"),
        P("fsdp", "tp"),
        P("tp", "fsdp"),
        P(("fsdp", "tp"), None),
        P(),
    )
    out_specs = (P(), P("fsdp", "tp"), P("fsdp", "tp"), P("tp", "fsdp"), P(("fsdp", "tp"), None))
    return jax.shard_map(local, mesh=mesh, in_specs=in_specs, out_specs=out_specs, check_vma=False)
```

```python
import functools

import jax
import jax.numpy as jnp
from jax import lax
from jax.experimental import pallas as pl
from jax.experimental.pallas import tpu as pltpu
from jax.sharding import PartitionSpec as P

EPSILON = 1e-05
STEP_SIZE = 1.0
SMOOTHING = 0.001
LANGS = 64
MESH = pl.DeviceIdType.MESH
F32, BF16 = jnp.float32, jnp.bfloat16


class Place:
    def __init__(self):
        self.dp = lax.axis_index("dp")
        f, t = lax.axis_index("fsdp"), lax.axis_index("tp")
        self.f, self.t = f, t
        self.y, self.c = lax.div(f, 2), lax.rem(f, 2)
        self.z, self.xh = lax.div(t, 2), lax.rem(t, 2)
        self.p = self.xh
        c = self.c
        self.a = (1 - c) * self.y + c * self.z
        self.b = (1 - c) * self.z + c * self.y

    def at(self, dp=None, y=None, z=None, xh=None, c=None):
        pick = lambda new, old: old if new is None else new
        dp, y, z = pick(dp, self.dp), pick(y, self.y), pick(z, self.z)
        xh, c = pick(xh, self.xh), pick(c, self.c)
        return {"dp": dp, "fsdp": y * 2 + c, "tp": z * 2 + xh}

    def on_a(self, a):
        c = self.c
        return self.at(y=(1 - c) * a + c * self.y, z=(1 - c) * self.z + c * a)

    def on_b(self, b):
        c = self.c
        return self.at(y=(1 - c) * self.y + c * b, z=(1 - c) * b + c * self.z)

    def on_ab(self, a, b):
        c = self.c
        return self.at(y=(1 - c) * a + c * b, z=(1 - c) * b + c * a)

    def core(self):
        return self.at(c=1 - self.c)

    def partner(self):
        return self.at(xh=1 - self.xh)

    def neighbour(self):
        return self.at(dp=1 - self.dp)

    def opposite(self):
        return self.at(dp=1 - self.dp, xh=1 - self.xh)


class Copies:
    def __init__(self, send, recv):
        self.send, self.recv, self.n, self.all = send, recv, 0, []

    def start(self, src, dst, to):
        copy = pltpu.make_async_remote_copy(
            src_ref=src,
            dst_ref=dst,
            send_sem=self.send.at[self.n],
            recv_sem=self.recv.at[self.n],
            device_id=to,
            device_id_type=MESH,
        )
        copy.start()
        self.n += 1
        self.all.append(copy)
        return copy

    def drain(self):
        for copy in self.all:
            copy.wait_send()


def greet(peers):
    barrier = pltpu.get_barrier_semaphore()
    for peer in peers:
        pl.semaphore_signal(barrier, inc=1, device_id=peer, device_id_type=MESH)
    pl.semaphore_wait(barrier, len(peers))


def ring(i, k):
    return lax.rem(i + k, 4)


OFFSETS = [(k, i) for k in (2, 1, 3, 0) for i in range(4) if k or i]
ROWS = (2, 3, 1, 0)


def rms_rows(values, gain):
    values = values.astype(F32)
    return values * lax.rsqrt(jnp.mean(values * values, axis=-1, keepdims=True) + EPSILON) * gain


def to_plane(go, me, view):
    sent = {}
    for k, i in OFFSETS:
        to = me.on_ab(ring(me.a, i), ring(me.b, k))
        sent[k, i] = go.start(view, view, to)
    return sent


class Spread:
    def __init__(self, go, me, view):
        self.go, self.me, self.view = go, me, view
        own = view(me.b, me.a)
        self.near = {i: go.start(own, own, me.on_a(ring(me.a, i))) for i in (2, 1, 3)}
        self.along = {(k, 0): go.start(own, own, me.on_b(ring(me.b, k))) for k in (2, 1, 3)}

    def hand_on(self):
        me = self.me
        for i in (1, 3, 2):
            self.near[i].wait_recv()
            unit = self.view(me.b, ring(me.a, 4 - i))
            for k in (2, 1, 3):
                self.along[k, i] = self.go.start(unit, unit, me.on_b(ring(me.b, k)))

    def row(self, k):
        if k:
            for i in range(4):
                self.along[k, i].wait_recv()
        return ring(self.me.b, (4 - k) % 4)


class Collect:
    def __init__(self, go, me, rb, ra):
        self.go, self.me, self.rb, self.ra, self.sent = go, me, rb, ra, []

    def row(self, m, view):
        if m:
            self.sent.append(self.go.start(view, self.rb.at[m], self.me.on_b(ring(self.me.b, m))))

    def total(self, own, units):
        go, me = self.go, self.me
        for copy in self.sent:
            copy.wait_recv()
        row = own[...].astype(F32)
        for m in (1, 2, 3):
            row = row + self.rb[m].astype(F32)
        units[...] = row.astype(BF16)
        swaps = [
            go.start(units.at[ring(me.a, i)], self.ra.at[i], me.on_a(ring(me.a, i))) for i in (2, 1, 3)
        ]
        for copy in swaps:
            copy.wait_recv()
        total = units[me.a].astype(F32)
        for i in (1, 2, 3):
            total = total + self.ra[i].astype(F32)
        return total


def forward_body(
    ids, hid, gain_in, gain_out, refh, ref_gain, gate, up, down, head,
    normed, pre, fin, fin_x, mid, ref_st, tl, dnw,
    idsg, guw, ref_all, headv, rhs, logit, x, rb, ra, units, give, rp,
    send, recv, local,
):
    me = Place()
    a, b, c, p, f = me.a, me.b, me.c, me.p, me.f
    go = Copies(send, recv)
    rings = [me.on_a(ring(a, k)) for k in (1, 2, 3)] + [me.on_b(ring(b, k)) for k in (1, 2, 3)]
    greet(rings + [me.core(), me.partner(), me.neighbour()])
    take_head = pltpu.make_async_copy(head, headv, local.at[0])
    take_head.start()
    normed[b, a] = rms_rows(hid[...], gain_in[...]).astype(BF16).reshape(2, 16, 1024)
    s2 = Spread(go, me, lambda bb, aa: normed.at[bb, aa])
    idsg[b, a] = ids[...]
    s2_ids = Spread(go, me, lambda bb, aa: idsg.at[bb, aa])
    here = pl.ds(pl.multiple_of(f * 128, 128), 128)

    def weights(ff, to, y=None):
        lanes = pl.ds(pl.multiple_of(ff * 128, 128), 128)
        pieces = [guw.at[ff], dnw.at[:, lanes]]
        if y is None:
            return [go.start(v, v, to) for v in pieces]
        part = pl.ds(pl.multiple_of(y * 128, 128), 128)
        return [
            go.start(gate.at[:, part], guw.at[ff, :, pl.ds(0, 128)], to),
            go.start(up.at[:, part], guw.at[ff, :, pl.ds(128, 128)], to),
            go.start(down.at[part], pieces[1], to),
        ]

    w_sent = {k: weights(f, me.at(y=ring(me.y, k)), ring(me.y, k)) for k in (2, 1, 3)}
    w_core = weights(f, me.core(), me.y)
    part = pl.ds(pl.multiple_of(me.y * 128, 128), 128)
    guw[f, :, 0:128] = gate[:, part]
    guw[f, :, 128:256] = up[:, part]
    dnw[:, here] = down[part]
    ref_all[c, b, a, p] = rms_rows(refh[...], ref_gain[...]).astype(BF16)
    r1 = go.start(ref_all.at[c, b, a, p], ref_all.at[c, b, a, p], me.partner())
    s2.hand_on()
    s2_ids.hand_on()
    r1.wait_recv()
    unit = ref_all.at[c, b, a]
    r2 = [go.start(unit, unit, me.on_a(ring(a, k))) for k in (1, 3, 2)]
    for k in (1, 3, 2):
        for copy in w_sent[k]:
            copy.wait_recv()
        w_core += weights(2 * ring(me.y, 4 - k) + c, me.core())
    for copy in w_core:
        copy.wait_recv()
    collect = Collect(go, me, rb, ra)
    for k in (0, 1, 3, 2):
        bb = s2.row(k)
        h = jnp.dot(
            normed[bb].reshape(128, 1024), guw[...].reshape(1024, 256),
            preferred_element_type=F32,
        )
        pre[bb] = h
        g = h[:, :128]
        h = (g * jax.nn.sigmoid(g) * h[:, 128:]).astype(BF16)
        h = jnp.dot(h, dnw[...], preferred_element_type=F32).astype(BF16)
        x[bb] = h.reshape(4, 32, 1024)
        collect.row((4 - k) % 4, x.at[bb])
    for copy in r2:
        copy.wait_recv()
    right_b, left_b = me.on_b(ring(b, 1)), me.on_b(ring(b, 3))
    unit = ref_all.at[c, b]
    cross = {0: go.start(unit, unit, me.core())}
    r3 = [go.start(unit, unit, right_b), go.start(unit, unit, left_b)]
    for k in (1, 2, 3):
        s2_ids.row(k)
    for bb in range(4):
        row = idsg[bb, 0] + idsg[bb, 1] + idsg[bb, 2] + idsg[bb, 3]
        tl[0, 0, 4 * c + bb] = row[0:1]
        tl[0, 1, 4 * c + bb] = row[1:2]
    mine = pl.ds(4 * c, 4)
    ids_across = [
        go.start(tl.at[0, n, mine], tl.at[0, n, mine], me.core()) for n in range(2)
    ]
    for copy in ids_across:
        copy.wait_recv()
    ids_far = go.start(tl.at[0], tl.at[1], me.neighbour())
    vocab = lax.broadcasted_iota(jnp.int32, (1024, 256), 0) + (f * 8 + me.t) * 1024

    def ref_rows(m):
        b_own, b_far = ring(b, m), ring(a, m)
        rhs[0:128] = ref_all[c, b_own].reshape(128, 4096)
        rhs[128:256] = ref_all[1 - c, b_far].reshape(128, 4096)

        @pl.loop(0, 4)
        def _(n):
            at = pl.ds(pl.multiple_of(n * 256, 256), 256)
            logit[at] = lax.dot_general(
                headv[at], rhs[...], (((1,), (1,)), ((), ())), preferred_element_type=F32
            )

        value = logit[...]
        high = jnp.max(value, axis=0, keepdims=True)
        want = jnp.concatenate([tl[0, 0, 4 * c + b_own], tl[0, 0, 4 * (1 - c) + b_far]], axis=1)
        picked = jnp.sum(jnp.where(vocab == want, value, 0.0), axis=0, keepdims=True)
        total = jnp.sum(jnp.exp(value - high), axis=0, keepdims=True)
        for s, got in enumerate((high, total, picked)):
            ref_st[s, 4 * c + b_own] = got[:, :128]
            ref_st[s, 4 * (1 - c) + b_far] = got[:, 128:]

    take_head.wait()
    cross[0].wait_recv()
    ref_rows(0)
    give[...] = collect.total(x.at[b], units).astype(BF16)
    swap = go.start(give, rp, me.partner())
    swap.wait_recv()
    middle = hid[...].astype(F32) + (give[...].astype(F32) + rp[...].astype(F32))
    mid[...] = middle
    fin[c, b, a] = rms_rows(middle, gain_out[...]).astype(BF16).reshape(2, 16, 1024)
    f2 = Spread(go, me, lambda bb, aa: fin.at[c, bb, aa])
    f_x = go.start(fin.at[c, b, a], fin_x, me.neighbour())
    f2.hand_on()
    r3[0].wait_recv()
    half = ref_all.at[c, ring(b, 3), pl.ds(0, 2)]
    r4 = [go.start(half, half, right_b)]
    r3[1].wait_recv()
    half = ref_all.at[c, ring(b, 1), pl.ds(2, 2)]
    r4.append(go.start(half, half, left_b))
    for m in (3, 1):
        unit = ref_all.at[c, ring(b, m)]
        cross[m] = go.start(unit, unit, me.core())
    cross[3].wait_recv()
    ref_rows(3)
    f3 = []
    for k in (0, 1, 3, 2):
        row = fin.at[c, f2.row(k)]
        f3.append(go.start(row, row, me.core()))
    for copy in r4:
        copy.wait_recv()
    unit = ref_all.at[c, ring(b, 2)]
    cross[2] = go.start(unit, unit, me.core())
    cross[1].wait_recv()
    ref_rows(1)
    cross[2].wait_recv()
    ref_rows(2)
    for copy in f3 + [f_x, ids_far]:
        copy.wait_recv()
    go.drain()


def forward(ids, hid, gain_in, gain_out, refh, ref_gain, gate, up, down, head):
    vmem = pl.BlockSpec(memory_space=pltpu.VMEM)
    shape = jax.ShapeDtypeStruct
    return pl.pallas_call(
        forward_body,
        out_shape=[
            shape((4, 4, 2, 16, 1024), BF16),
            shape((4, 128, 256), F32),
            shape((2, 4, 4, 2, 16, 1024), BF16),
            shape((2, 16, 1024), BF16),
            shape((32, 1024), F32),
            shape((3, 8, 1, 128), F32),
            shape((2, 2, 8, 1, 128), jnp.int32),
            shape((128, 1024), BF16),
        ],
        in_specs=[vmem] * 9 + [pl.BlockSpec(memory_space=pl.ANY)],
        out_specs=[vmem] * 8,
        scratch_shapes=[
            pltpu.VMEM((4, 4, 8, 128), jnp.int32),
            pltpu.VMEM((8, 128, 256), BF16),
            pltpu.VMEM((2, 4, 4, 2, 16, 4096), BF16),
            pltpu.VMEM((1024, 4096), BF16),
            pltpu.VMEM((256, 4096), BF16),
            pltpu.VMEM((1024, 256), F32),
            pltpu.VMEM((4, 4, 32, 1024), BF16),
            pltpu.VMEM((4, 4, 32, 1024), BF16),
            pltpu.VMEM((4, 32, 1024), BF16),
            pltpu.VMEM((4, 32, 1024), BF16),
            pltpu.VMEM((32, 1024), BF16),
            pltpu.VMEM((32, 1024), BF16),
            pltpu.SemaphoreType.DMA((110,)),
            pltpu.SemaphoreType.DMA((110,)),
            pltpu.SemaphoreType.DMA((1,)),
        ],
        compiler_params=pltpu.CompilerParams(
            collective_id=1, has_side_effects=True, vmem_limit_bytes=60 * 2**20
        ),
        name="forward",
    )(ids, hid, gain_in, gain_out, refh, ref_gain, gate, up, down, head)


def join_all(pieces):
    out = []
    for base in (0, 12):
        high = functools.reduce(jnp.maximum, [s[base : base + 4] for s in pieces])
        total = pick = None
        for s in pieces:
            t = s[base + 4 : base + 8] * jnp.exp(s[base : base + 4] - high)
            k = s[base + 8 : base + 12]
            total, pick = (t, k) if total is None else (total + t, pick + k)
        out += [high, total, pick]
    return jnp.concatenate(out, axis=0)


def rest_body(
    ref_st, ids, dw, fin, fin_x, mid, gain, head, normed, pre, down_w,
    logw, grad_head, gate, up, down,
    vd, vo, vf, vh, vn, vp, lg, st, slot_c, slot_yz, slot_x, both, lse, tw, ls, lc,
    x, r0, acc, rb, ra, units, give, rp, dmid, comb, oc, sc, ox, sx, rg,
    send, recv, hsend, hrecv, local, gsem,
):
    me = Place()
    a, b, c, p, f = me.a, me.b, me.c, me.p, me.f
    go = Copies(send, recv)
    loads = [
        pltpu.make_async_copy(src, dst, local.at[n])
        for n, (src, dst) in enumerate(((head, vh), (fin, vo), (normed, vn), (pre, vp)))
    ]
    for load in loads:
        load.start()
    plane = [me.on_ab(ring(a, i), ring(b, k)) for k, i in OFFSETS]
    x_peers = [me.partner(), me.neighbour(), me.opposite()]
    across_dp = [me.at(dp=1 - me.dp, y=ring(me.y, k)) for k in (1, 2, 3)]
    greet(plane + x_peers + [me.core()] + across_dp)
    loads[0].wait()
    loads[1].wait()
    lanes = (((1,), (1,)), ((), ()))
    rows = (((0,), (0,)), ((), ()))
    base = (f * 8 + me.t) * 1024
    tile = lambda n: pl.ds(pl.multiple_of(n * 128, 128), 128)

    def line(v):
        return jnp.concatenate([v(r) for r in range(8)], axis=1)

    def own_rows(n, high):
        logits = lax.dot_general(vh[tile(n)], vo[...], lanes, preferred_element_type=F32)
        lg[tile(n)] = logits
        return jnp.maximum(high, jnp.max(logits, axis=0, keepdims=True))

    high = lax.fori_loop(0, 8, own_rows, jnp.full((1, 1024), -jnp.inf, F32))
    own_tgt = line(lambda r: ids[0, 0, r])

    def own_sums(n, carry):
        total, picked = carry
        logits = lg[tile(n)]
        vocab = lax.broadcasted_iota(jnp.int32, (128, 1024), 0) + (base + n * 128)
        total += jnp.sum(jnp.exp(logits - high), axis=0, keepdims=True)
        picked += jnp.sum(jnp.where(vocab == own_tgt, logits, 0.0), axis=0, keepdims=True)
        return total, picked

    zero = jnp.zeros((1, 1024), F32)
    total, picked = lax.fori_loop(0, 8, own_sums, (zero, zero))
    for r in range(8):
        h, q = r // 4, r % 4
        for s in range(3):
            st[h, 4 * s + q : 4 * s + q + 1] = ref_st[s, r]
        for s, v in enumerate((high, total, picked)):
            st[h, 12 + 4 * s + q : 13 + 4 * s + q] = v[:, 128 * r : 128 * (r + 1)]
    slot_c[c] = st[c]
    half = go.start(st.at[1 - c], slot_c.at[c], me.core())
    half.wait_recv()
    yz = me.y * 4 + me.z
    slot_yz[yz] = join_all([slot_c[0], slot_c[1]])
    sent = to_plane(go, me, slot_yz.at[yz])
    vf[c, b, a] = fin_x[...]
    beside = Spread(go, me, lambda bb, aa: vf.at[c, bb, aa])
    for copy in sent.values():
        copy.wait_recv()
    slot_x[0, p] = join_all([slot_yz[j] for j in range(16)])
    spread = [
        go.start(slot_x.at[0, p], slot_x.at[g, p], to) for g, to in zip((0, 1, 1), x_peers)
    ]
    beside.hand_on()
    for copy in spread:
        copy.wait_recv()
    both[c, 0] = join_all([slot_x[0, 0], slot_x[0, 1]])
    both[c, 1] = join_all([slot_x[1, 0], slot_x[1, 1]])
    share = go.start(both.at[c], both.at[c], me.core())
    share.wait_recv()
    excess = [None, None]
    for g in range(2):
        now = [
            jnp.concatenate([both[0, g, 4 * i : 4 * i + 4], both[1, g, 4 * i : 4 * i + 4]])
            for i in range(6)
        ]
        ref_loss = now[0] + jnp.log(now[1]) - now[2]
        proxy_lse = now[3] + jnp.log(now[4])
        lse[8 * g : 8 * g + 8] = proxy_lse
        excess[g] = jnp.maximum(proxy_lse - now[5] - ref_loss, 0.0)
    every = jnp.concatenate([ids[g, 1, r] for g in range(2) for r in range(8)], axis=0)
    for l in range(LANGS):
        here = every == l
        e = jnp.where(here[:8], excess[0], 0.0) + jnp.where(here[8:], excess[1], 0.0)
        n = jnp.where(here[:8], 1.0, 0.0) + jnp.where(here[8:], 1.0, 0.0)
        ls[l : l + 1] = jnp.sum(e, axis=0, keepdims=True)
        lc[l : l + 1] = jnp.sum(n, axis=0, keepdims=True)
    wide = lambda v: jnp.broadcast_to(jnp.sum(v[...], axis=1, keepdims=True), (LANGS, 128))
    count = jnp.maximum(wide(lc), 1.0)
    score = jnp.log(dw[...]) + STEP_SIZE * (wide(ls) / count)
    score = jnp.exp(score - jnp.max(score, axis=0, keepdims=True))
    mixture = score / jnp.sum(score, axis=0, keepdims=True)
    new = (1.0 - SMOOTHING) * mixture + SMOOTHING / LANGS
    logw[...] = jnp.log(new)
    per_token = new / count * 2048.0
    weight = jnp.zeros(every.shape, F32)
    for l in range(LANGS):
        weight = jnp.where(every == l, per_token[l : l + 1], weight)
    tw[...] = weight
    lse_own, tw_own = line(lambda r: lse[r : r + 1]), line(lambda r: tw[r : r + 1])

    @pl.loop(0, 8)
    def _(n):
        vocab = lax.broadcasted_iota(jnp.int32, (128, 1024), 0) + (base + n * 128)
        hit = jnp.where(vocab == own_tgt, 1.0, 0.0)
        vd[tile(n)] = (tw_own * (jnp.exp(lg[tile(n)] - lse_own) - hit)).astype(BF16)

    def d_rows(cc):
        at = pl.ds(pl.multiple_of(cc * 512, 512), 512)
        part = lax.dot_general(vd[:, at], vh[...], rows, preferred_element_type=F32)
        x[cc] = part.astype(BF16).reshape(4, 128, 1024)

    d_rows(1 - c)
    across = {}
    for m in ROWS:
        bb = ring(a, m)
        across[m] = go.start(x.at[1 - c, bb], r0.at[bb], me.core())
    d_rows(c)
    collect = Collect(go, me, rb, ra)
    for m in ROWS:
        bb = ring(b, m)
        across[m].wait_recv()
        joined = x[c, bb].astype(F32) + r0[bb].astype(F32)
        acc[bb] = joined.astype(BF16).reshape(acc.shape[1:])
        collect.row(m, acc.at[bb])
    far = []
    for k in (0, 1, 3, 2):
        row = vf.at[c, beside.row(k)]
        far.append(go.start(row, row, me.core()))
    for copy in far:
        copy.wait_recv()
    far_tgt = line(lambda r: ids[1, 0, r])

    def head_rows(n):
        at = tile(n)
        states = vf[...].reshape(1024, 1024)
        logits = lax.dot_general(vh[at], states, lanes, preferred_element_type=F32)
        vocab = lax.broadcasted_iota(jnp.int32, (128, 1024), 0) + (base + n * 128)
        hit = jnp.where(vocab == far_tgt, 1.0, 0.0)
        lse_far = line(lambda r: lse[8 + r : 9 + r])
        tw_far = line(lambda r: tw[8 + r : 9 + r])
        d = (tw_far * (jnp.exp(logits - lse_far) - hit)).astype(BF16)
        lg[at] = jnp.dot(d, states, preferred_element_type=F32) + jnp.dot(
            vd[at], vo[...], preferred_element_type=F32
        )
        pltpu.make_async_copy(lg.at[at], grad_head.at[at], gsem.at[n]).start()

    pl.loop(0, 4)(head_rows)
    give[...] = collect.total(acc.at[b], units).astype(BF16)
    swap = go.start(give, rp, me.partner())
    pl.loop(4, 6)(head_rows)
    swap.wait_recv()
    d_final = give[...].astype(F32) + rp[...].astype(F32)
    middle = mid[...]
    inv = lax.rsqrt(jnp.mean(middle * middle, axis=1, keepdims=True) + EPSILON)
    scaled = d_final * gain[...]
    inner = jnp.mean(middle * scaled, axis=1, keepdims=True)
    d_mid = (inv * scaled - middle * inv * inv * inv * inner).astype(BF16)
    dmid[b, a] = d_mid.reshape(2, 16, 1024)
    d2 = Spread(go, me, lambda bb, aa: dmid.at[bb, aa])
    pl.loop(6, 8)(head_rows)
    d2.hand_on()
    loads[2].wait()
    loads[3].wait()
    g, u = vp[:, :128], vp[:, 128:]
    s = jax.nn.sigmoid(g)
    act = (g * s * u).astype(BF16)
    gate_slope = u * s * (1.0 + g * (1.0 - s))
    up_slope = g * s
    for k in (1, 3, 2):
        d2.row(k)
    dm = dmid[...].reshape(512, 1024)
    d_act = lax.dot_general(dm, down_w[...], lanes, preferred_element_type=F32)
    for n, (left, right) in enumerate(
        (
            ((d_act * gate_slope).astype(BF16), vn[...]),
            ((d_act * up_slope).astype(BF16), vn[...]),
            (act, dm),
        )
    ):
        grad = lax.dot_general(left, right, rows, preferred_element_type=F32).astype(BF16)
        for j in range(8):
            comb[j % 2, j // 2 % 2, j // 4, 128 * n : 128 * (n + 1)] = grad[
                :, 128 * j : 128 * (j + 1)
            ]
    swap = go.start(comb.at[1 - c], oc, me.core())
    swap.wait_recv()
    sc[...] = (comb[c].astype(F32) + oc[...].astype(F32)).astype(BF16)
    swap = go.start(sc.at[1 - me.dp], ox, me.neighbour())
    swap.wait_recv()
    sx[...] = (sc[me.dp].astype(F32) + ox[...].astype(F32)).astype(BF16)
    half, odd = lax.div(me.y, 2), lax.rem(me.y, 2)

    def homeward(e, side, src):
        h = lax.rem(half + e, 2)
        return pltpu.make_async_remote_copy(
            src_ref=sx.at[h],
            dst_ref=rg.at[src],
            send_sem=hsend.at[2 * e + side],
            recv_sem=hrecv.at[src],
            device_id=me.at(dp=1 - me.dp if side else me.dp, y=2 * h + me.dp),
            device_id_type=MESH,
        )

    stays = odd == me.dp
    for e, side in ((1, 1), (1, 0), (0, 1)):
        homeward(e, side, me.y).start()

    @pl.when(jnp.logical_not(stays))
    def _():
        homeward(0, 0, me.y).start()

    @pl.when(stays)
    def _():
        rg[me.y] = sx[half]

    for j in range(4):

        @pl.when(jnp.logical_or(me.y != j, jnp.logical_not(stays)))
        def _(j=j):
            homeward(1, 1, j).wait_recv()

        at = slice(128 * j, 128 * (j + 1))
        got = rg[j].astype(F32)
        gate[:, at] = got[0:128].T
        up[:, at] = got[128:256].T
        down[at] = got[256:384]
    for e, side in ((1, 1), (1, 0), (0, 1)):
        homeward(e, side, me.y).wait_send()

    @pl.when(jnp.logical_not(stays))
    def _():
        homeward(0, 0, me.y).wait_send()

    for n in range(8):
        at = pl.ds(128 * n, 128)
        pltpu.make_async_copy(lg.at[at], grad_head.at[at], gsem.at[n]).wait()
    go.drain()


def rest(ref_st, ids, domain_weights, fin, fin_x, mid, gain, head, normed, pre, down_w):
    vmem = pl.BlockSpec(memory_space=pltpu.VMEM)
    hbm = pl.BlockSpec(memory_space=pl.ANY)
    shape = jax.ShapeDtypeStruct
    big = pltpu.VMEM((1024, 1024), BF16)
    return pl.pallas_call(
        rest_body,
        out_shape=[
            shape((LANGS, 128), F32),
            shape((1024, 1024), F32),
            shape((128, 512), F32),
            shape((128, 512), F32),
            shape((512, 128), F32),
        ],
        in_specs=[vmem] * 3 + [hbm] + [vmem] * 3 + [hbm] * 3 + [vmem],
        out_specs=[vmem, hbm] + [vmem] * 3,
        scratch_shapes=[
            big, big,
            pltpu.VMEM((2, 4, 4, 2, 16, 1024), BF16),
            big,
            pltpu.VMEM((512, 1024), BF16),
            pltpu.VMEM((512, 256), F32),
            pltpu.VMEM((1024, 1024), F32),
            pltpu.VMEM((2, 24, 128), F32),
            pltpu.VMEM((2, 24, 128), F32),
            pltpu.VMEM((16, 24, 128), F32),
            pltpu.VMEM((2, 2, 24, 128), F32),
            pltpu.VMEM((2, 2, 24, 128), F32),
            pltpu.VMEM((16, 128), F32),
            pltpu.VMEM((16, 128), F32),
            pltpu.VMEM((LANGS, 128), F32),
            pltpu.VMEM((LANGS, 128), F32),
            pltpu.VMEM((2, 4, 128, 1024), BF16),
            pltpu.VMEM((4, 128, 1024), BF16),
            pltpu.VMEM((4, 4, 32, 1024), BF16),
            pltpu.VMEM((4, 4, 32, 1024), BF16),
            pltpu.VMEM((4, 32, 1024), BF16),
            pltpu.VMEM((4, 32, 1024), BF16),
            pltpu.VMEM((32, 1024), BF16),
            pltpu.VMEM((32, 1024), BF16),
            pltpu.VMEM((4, 4, 2, 16, 1024), BF16),
            pltpu.VMEM((2, 2, 2, 384, 128), BF16),
            pltpu.VMEM((2, 2, 384, 128), BF16),
            pltpu.VMEM((2, 2, 384, 128), BF16),
            pltpu.VMEM((2, 384, 128), BF16),
            pltpu.VMEM((2, 384, 128), BF16),
            pltpu.VMEM((4, 384, 128), BF16),
            pltpu.SemaphoreType.DMA((90,)),
            pltpu.SemaphoreType.DMA((90,)),
            pltpu.SemaphoreType.DMA((4,)),
            pltpu.SemaphoreType.DMA((4,)),
            pltpu.SemaphoreType.DMA((4,)),
            pltpu.SemaphoreType.DMA((8,)),
        ],
        compiler_params=pltpu.CompilerParams(
            collective_id=5, has_side_effects=True, vmem_limit_bytes=44 * 2**20
        ),
        name="rest",
    )(
        ref_st, ids, jnp.broadcast_to(domain_weights[:, None], (LANGS, 128)), fin, fin_x,
        mid, gain, head, normed, pre, down_w,
    )


def local(
    ref_hidden,
    proxy_hidden,
    targets,
    languages,
    ref_gain,
    ref_head,
    proxy_gain_in,
    proxy_gain_out,
    gate_weight,
    up_weight,
    down_weight,
    proxy_head,
    domain_weights,
):
    me = Place()
    mine = lambda v: lax.dynamic_slice_in_dim(v, me.z * 32, 32, 0)
    ids = jnp.tile(jnp.stack([mine(targets), mine(languages)]), (4, 4))
    lanes = lax.broadcasted_iota(jnp.int32, (8, 128), 1)
    ids = jnp.where(lax.div(lanes, 32) == me.a, ids, 0)
    normed_in, pre, final_own, fin_x, mid_sum, ref_stats, ids, down_w = forward(
        ids,
        mine(proxy_hidden),
        proxy_gain_in[None],
        proxy_gain_out[None],
        ref_hidden,
        ref_gain[None],
        gate_weight,
        up_weight,
        down_weight,
        ref_head,
    )
    log_weights, grad_head, grad_gate, grad_up, grad_down = rest(
        ref_stats,
        ids,
        domain_weights,
        final_own.reshape(1024, 1024),
        fin_x,
        mid_sum,
        proxy_gain_out[None],
        proxy_head,
        normed_in.reshape(512, 1024),
        pre.reshape(512, 256),
        down_w,
    )
    return (log_weights[:, 0], grad_gate, grad_up, grad_down, grad_head)


def solution(mesh):
    in_specs = (
        P(("dp", "fsdp", "tp"), None),
        P(("dp", "fsdp"), None),
        P(("dp", "fsdp")),
        P(("dp", "fsdp")),
        P(),
        P(("fsdp", "tp"), None),
        P(),
        P(),
        P("fsdp", "tp"),
        P("fsdp", "tp"),
        P("tp", "fsdp"),
        P(("fsdp", "tp"), None),
        P(),
    )
    out_specs = (P(), P("fsdp", "tp"), P("fsdp", "tp"), P("tp", "fsdp"), P(("fsdp", "tp"), None))
    return jax.shard_map(local, mesh=mesh, in_specs=in_specs, out_specs=out_specs, check_vma=False)
```

```python
import functools

import jax
import jax.numpy as jnp
from jax import lax
from jax.experimental import pallas as pl
from jax.experimental.pallas import tpu as pltpu
from jax.sharding import PartitionSpec as P

EPSILON = 1e-05
STEP_SIZE = 1.0
SMOOTHING = 0.001
LANGS = 64
VMEM_LIMIT = 58
MESH = pl.DeviceIdType.MESH
F32, BF16 = jnp.float32, jnp.bfloat16


class Place:
    def __init__(self):
        self.dp = lax.axis_index("dp")
        f, t = lax.axis_index("fsdp"), lax.axis_index("tp")
        self.f, self.t = f, t
        self.y, self.c = lax.div(f, 2), lax.rem(f, 2)
        self.z, self.xh = lax.div(t, 2), lax.rem(t, 2)
        self.p = self.xh
        c = self.c
        self.a = (1 - c) * self.y + c * self.z
        self.b = (1 - c) * self.z + c * self.y

    def at(self, dp=None, y=None, z=None, xh=None, c=None):
        pick = lambda new, old: old if new is None else new
        dp, y, z = pick(dp, self.dp), pick(y, self.y), pick(z, self.z)
        xh, c = pick(xh, self.xh), pick(c, self.c)
        return {"dp": dp, "fsdp": y * 2 + c, "tp": z * 2 + xh}

    def on_a(self, a):
        c = self.c
        return self.at(y=(1 - c) * a + c * self.y, z=(1 - c) * self.z + c * a)

    def on_b(self, b):
        c = self.c
        return self.at(y=(1 - c) * self.y + c * b, z=(1 - c) * b + c * self.z)

    def on_ab(self, a, b):
        c = self.c
        return self.at(y=(1 - c) * a + c * b, z=(1 - c) * b + c * a)

    def core(self):
        return self.at(c=1 - self.c)

    def partner(self):
        return self.at(xh=1 - self.xh)

    def neighbour(self):
        return self.at(dp=1 - self.dp)

    def opposite(self):
        return self.at(dp=1 - self.dp, xh=1 - self.xh)


class Copies:
    def __init__(self, send, recv):
        self.send, self.recv, self.n, self.all = send, recv, 0, []

    def start(self, src, dst, to):
        copy = pltpu.make_async_remote_copy(
            src_ref=src,
            dst_ref=dst,
            send_sem=self.send.at[self.n],
            recv_sem=self.recv.at[self.n],
            device_id=to,
            device_id_type=MESH,
        )
        copy.start()
        self.n += 1
        self.all.append(copy)
        return copy

    def drain(self):
        for copy in self.all:
            copy.wait_send()


def greet(peers):
    barrier = pltpu.get_barrier_semaphore()
    for peer in peers:
        pl.semaphore_signal(barrier, inc=1, device_id=peer, device_id_type=MESH)
    pl.semaphore_wait(barrier, len(peers))


def ring(i, k):
    return lax.rem(i + k, 4)


OFFSETS = [(k, i) for k in (2, 1, 3, 0) for i in range(4) if k or i]
ROWS = (2, 3, 1, 0)


def rms_rows(values, gain):
    values = values.astype(F32)
    return values * lax.rsqrt(jnp.mean(values * values, axis=-1, keepdims=True) + EPSILON) * gain


def to_plane(go, me, view):
    sent = {}
    for k, i in OFFSETS:
        to = me.on_ab(ring(me.a, i), ring(me.b, k))
        sent[k, i] = go.start(view, view, to)
    return sent


class Spread:
    def __init__(self, go, me, view):
        self.go, self.me, self.view = go, me, view
        own = view(me.b, me.a)
        self.near = {i: go.start(own, own, me.on_a(ring(me.a, i))) for i in (2, 1, 3)}
        self.along = {(k, 0): go.start(own, own, me.on_b(ring(me.b, k))) for k in (2, 1, 3)}

    def hand_on(self):
        me = self.me
        for i in (1, 3, 2):
            self.near[i].wait_recv()
            unit = self.view(me.b, ring(me.a, 4 - i))
            for k in (2, 1, 3):
                self.along[k, i] = self.go.start(unit, unit, me.on_b(ring(me.b, k)))

    def row(self, k):
        if k:
            for i in range(4):
                self.along[k, i].wait_recv()
        return ring(self.me.b, (4 - k) % 4)


class Collect:
    def __init__(self, go, me, rb, ra):
        self.go, self.me, self.rb, self.ra, self.sent = go, me, rb, ra, []

    def row(self, m, view):
        if m:
            self.sent.append(self.go.start(view, self.rb.at[m], self.me.on_b(ring(self.me.b, m))))

    def total(self, own, units):
        go, me = self.go, self.me
        for copy in self.sent:
            copy.wait_recv()
        row = own[...].astype(F32)
        for m in (1, 2, 3):
            row = row + self.rb[m].astype(F32)
        units[...] = row.astype(BF16)
        swaps = [
            go.start(units.at[ring(me.a, i)], self.ra.at[i], me.on_a(ring(me.a, i))) for i in (2, 1, 3)
        ]
        for copy in swaps:
            copy.wait_recv()
        total = units[me.a].astype(F32)
        for i in (1, 2, 3):
            total = total + self.ra[i].astype(F32)
        return total


def join_all(pieces):
    out = []
    for base in (0, 12):
        high = functools.reduce(jnp.maximum, [s[base : base + 4] for s in pieces])
        total = pick = None
        for s in pieces:
            t = s[base + 4 : base + 8] * jnp.exp(s[base : base + 4] - high)
            k = s[base + 8 : base + 12]
            total, pick = (t, k) if total is None else (total + t, pick + k)
        out += [high, total, pick]
    return jnp.concatenate(out, axis=0)


def step_body(
    ids, hid, gain_in, gain_out, refh, ref_gain, gate, up, down, dw, head, proxy_head,
    logw, grad_head, g_gate, g_up, g_down,
    normed, pre, fin, fin_x, mid, ref_st, tl, dnw,
    idsg, guw, ref_all, headv, rhs, logit, x, rb, ra, units, give, rp,
    vf, vh, lg, st, slot_c, slot_yz, slot_x, both, lse, tw, ls, lc,
    d_x, r0, acc, d_rb, d_ra, d_units, d_give, d_rp, dmid, comb, oc, sc, ox, sx, rg,
    send, recv, hsend, hrecv, local,
):
    me = Place()
    a, b, c, p, f = me.a, me.b, me.c, me.p, me.f
    go = Copies(send, recv)
    plane = [me.on_ab(ring(a, i), ring(b, k)) for k, i in OFFSETS]
    x_peers = [me.partner(), me.neighbour(), me.opposite()]
    across_dp = [me.at(dp=1 - me.dp, y=ring(me.y, k)) for k in (1, 2, 3)]
    vd = headv.at[:, pl.ds(0, 1024)]
    take_proxy = pltpu.make_async_copy(proxy_head, vh, local.at[1])
    greet(plane + x_peers + [me.core()] + across_dp)
    take_head = pltpu.make_async_copy(head, headv, local.at[0])
    take_head.start()
    take_proxy.start()
    normed[b, a] = rms_rows(hid[...], gain_in[...]).astype(BF16).reshape(2, 16, 1024)
    s2 = Spread(go, me, lambda bb, aa: normed.at[bb, aa])
    idsg[b, a] = ids[...]
    s2_ids = Spread(go, me, lambda bb, aa: idsg.at[bb, aa])
    here = pl.ds(pl.multiple_of(f * 128, 128), 128)

    def weights(ff, to, y=None):
        lanes = pl.ds(pl.multiple_of(ff * 128, 128), 128)
        pieces = [guw.at[ff], dnw.at[:, lanes]]
        if y is None:
            return [go.start(v, v, to) for v in pieces]
        part = pl.ds(pl.multiple_of(y * 128, 128), 128)
        return [
            go.start(gate.at[:, part], guw.at[ff, :, pl.ds(0, 128)], to),
            go.start(up.at[:, part], guw.at[ff, :, pl.ds(128, 128)], to),
            go.start(down.at[part], pieces[1], to),
        ]

    w_sent = {k: weights(f, me.at(y=ring(me.y, k)), ring(me.y, k)) for k in (2, 1, 3)}
    w_core = weights(f, me.core(), me.y)
    part = pl.ds(pl.multiple_of(me.y * 128, 128), 128)
    guw[f, :, 0:128] = gate[:, part]
    guw[f, :, 128:256] = up[:, part]
    dnw[:, here] = down[part]
    ref_all[c, b, a, p] = rms_rows(refh[...], ref_gain[...]).astype(BF16)
    r1 = go.start(ref_all.at[c, b, a, p], ref_all.at[c, b, a, p], me.partner())
    s2.hand_on()
    s2_ids.hand_on()
    r1.wait_recv()
    unit = ref_all.at[c, b, a]
    r2 = [go.start(unit, unit, me.on_a(ring(a, k))) for k in (1, 3, 2)]
    for k in (1, 3, 2):
        for copy in w_sent[k]:
            copy.wait_recv()
        w_core += weights(2 * ring(me.y, 4 - k) + c, me.core())
    for copy in w_core:
        copy.wait_recv()
    collect = Collect(go, me, rb, ra)
    for k in (0, 1, 3, 2):
        bb = s2.row(k)
        h = jnp.dot(
            normed[bb].reshape(128, 1024), guw[...].reshape(1024, 256),
            preferred_element_type=F32,
        )
        pre[bb] = h
        g = h[:, :128]
        h = (g * jax.nn.sigmoid(g) * h[:, 128:]).astype(BF16)
        h = jnp.dot(h, dnw[...], preferred_element_type=F32).astype(BF16)
        x[bb] = h.reshape(4, 32, 1024)
        collect.row((4 - k) % 4, x.at[bb])
    for copy in r2:
        copy.wait_recv()
    right_b, left_b = me.on_b(ring(b, 1)), me.on_b(ring(b, 3))
    unit = ref_all.at[c, b]
    cross = {0: go.start(unit, unit, me.core())}
    r3 = [go.start(unit, unit, right_b), go.start(unit, unit, left_b)]
    for k in (1, 2, 3):
        s2_ids.row(k)
    for bb in range(4):
        row = idsg[bb, 0] + idsg[bb, 1] + idsg[bb, 2] + idsg[bb, 3]
        tl[0, 0, 4 * c + bb] = row[0:1]
        tl[0, 1, 4 * c + bb] = row[1:2]
    mine = pl.ds(4 * c, 4)
    ids_across = [
        go.start(tl.at[0, n, mine], tl.at[0, n, mine], me.core()) for n in range(2)
    ]
    for copy in ids_across:
        copy.wait_recv()
    ids_far = go.start(tl.at[0], tl.at[1], me.neighbour())
    vocab = lax.broadcasted_iota(jnp.int32, (1024, 256), 0) + (f * 8 + me.t) * 1024

    def ref_rows(m):
        b_own, b_far = ring(b, m), ring(a, m)
        rhs[0:128] = ref_all[c, b_own].reshape(128, 4096)
        rhs[128:256] = ref_all[1 - c, b_far].reshape(128, 4096)

        @pl.loop(0, 4)
        def _(n):
            at = pl.ds(pl.multiple_of(n * 256, 256), 256)
            logit[at] = lax.dot_general(
                headv[at], rhs[...], (((1,), (1,)), ((), ())), preferred_element_type=F32
            )

        value = logit[...]
        high = jnp.max(value, axis=0, keepdims=True)
        want = jnp.concatenate([tl[0, 0, 4 * c + b_own], tl[0, 0, 4 * (1 - c) + b_far]], axis=1)
        picked = jnp.sum(jnp.where(vocab == want, value, 0.0), axis=0, keepdims=True)
        total = jnp.sum(jnp.exp(value - high), axis=0, keepdims=True)
        for s, got in enumerate((high, total, picked)):
            ref_st[s, 4 * c + b_own] = got[:, :128]
            ref_st[s, 4 * (1 - c) + b_far] = got[:, 128:]

    take_head.wait()
    cross[0].wait_recv()
    ref_rows(0)
    give[...] = collect.total(x.at[b], units).astype(BF16)
    swap = go.start(give, rp, me.partner())
    swap.wait_recv()
    middle = hid[...].astype(F32) + (give[...].astype(F32) + rp[...].astype(F32))
    mid[...] = middle
    fin[c, b, a] = rms_rows(middle, gain_out[...]).astype(BF16).reshape(2, 16, 1024)
    f2 = Spread(go, me, lambda bb, aa: fin.at[c, bb, aa])
    f_x = go.start(fin.at[c, b, a], fin_x, me.neighbour())
    f2.hand_on()
    r3[0].wait_recv()
    half = ref_all.at[c, ring(b, 3), pl.ds(0, 2)]
    r4 = [go.start(half, half, right_b)]
    r3[1].wait_recv()
    half = ref_all.at[c, ring(b, 1), pl.ds(2, 2)]
    r4.append(go.start(half, half, left_b))
    for m in (3, 1):
        unit = ref_all.at[c, ring(b, m)]
        cross[m] = go.start(unit, unit, me.core())
    cross[3].wait_recv()
    ref_rows(3)
    f3 = []
    for k in (0, 1, 3, 2):
        row = fin.at[c, f2.row(k)]
        f3.append(go.start(row, row, me.core()))
    for copy in f3 + [f_x, ids_far]:
        copy.wait_recv()
    take_proxy.wait()
    lanes = (((1,), (1,)), ((), ()))
    rows = (((0,), (0,)), ((), ()))
    base = (f * 8 + me.t) * 1024
    tile = lambda n: pl.ds(pl.multiple_of(n * 128, 128), 128)

    def line(v):
        return jnp.concatenate([v(r) for r in range(8)], axis=1)

    def own_rows(n, high):
        logits = lax.dot_general(vh[tile(n)], fin[...].reshape(1024, 1024), lanes, preferred_element_type=F32)
        lg[tile(n)] = logits
        return jnp.maximum(high, jnp.max(logits, axis=0, keepdims=True))

    high = lax.fori_loop(0, 8, own_rows, jnp.full((1, 1024), -jnp.inf, F32))
    for copy in r4:
        copy.wait_recv()
    unit = ref_all.at[c, ring(b, 2)]
    cross[2] = go.start(unit, unit, me.core())
    own_tgt = line(lambda r: tl[0, 0, r])

    def own_sums(n, carry):
        total, picked = carry
        logits = lg[tile(n)]
        vocab = lax.broadcasted_iota(jnp.int32, (128, 1024), 0) + (base + n * 128)
        total += jnp.sum(jnp.exp(logits - high), axis=0, keepdims=True)
        picked += jnp.sum(jnp.where(vocab == own_tgt, logits, 0.0), axis=0, keepdims=True)
        return total, picked

    zero = jnp.zeros((1, 1024), F32)
    total, picked = lax.fori_loop(0, 8, own_sums, (zero, zero))
    cross[1].wait_recv()
    ref_rows(1)
    cross[2].wait_recv()
    ref_rows(2)
    for r in range(8):
        h, q = r // 4, r % 4
        for s in range(3):
            st[h, 4 * s + q : 4 * s + q + 1] = ref_st[s, r]
        for s, v in enumerate((high, total, picked)):
            st[h, 12 + 4 * s + q : 13 + 4 * s + q] = v[:, 128 * r : 128 * (r + 1)]
    slot_c[c] = st[c]
    half = go.start(st.at[1 - c], slot_c.at[c], me.core())
    half.wait_recv()
    yz = me.y * 4 + me.z
    slot_yz[yz] = join_all([slot_c[0], slot_c[1]])
    sent = to_plane(go, me, slot_yz.at[yz])
    vf[c, b, a] = fin_x[...]
    beside = Spread(go, me, lambda bb, aa: vf.at[c, bb, aa])
    for copy in sent.values():
        copy.wait_recv()
    slot_x[0, p] = join_all([slot_yz[j] for j in range(16)])
    spread = [
        go.start(slot_x.at[0, p], slot_x.at[g, p], to) for g, to in zip((0, 1, 1), x_peers)
    ]
    beside.hand_on()
    for copy in spread:
        copy.wait_recv()
    both[c, 0] = join_all([slot_x[0, 0], slot_x[0, 1]])
    both[c, 1] = join_all([slot_x[1, 0], slot_x[1, 1]])
    share = go.start(both.at[c], both.at[c], me.core())
    share.wait_recv()
    excess = [None, None]
    for g in range(2):
        now = [
            jnp.concatenate([both[0, g, 4 * i : 4 * i + 4], both[1, g, 4 * i : 4 * i + 4]])
            for i in range(6)
        ]
        ref_loss = now[0] + jnp.log(now[1]) - now[2]
        proxy_lse = now[3] + jnp.log(now[4])
        lse[8 * g : 8 * g + 8] = proxy_lse
        excess[g] = jnp.maximum(proxy_lse - now[5] - ref_loss, 0.0)
    every = jnp.concatenate([tl[g, 1, r] for g in range(2) for r in range(8)], axis=0)
    for l in range(LANGS):
        here = every == l
        e = jnp.where(here[:8], excess[0], 0.0) + jnp.where(here[8:], excess[1], 0.0)
        n = jnp.where(here[:8], 1.0, 0.0) + jnp.where(here[8:], 1.0, 0.0)
        ls[l : l + 1] = jnp.sum(e, axis=0, keepdims=True)
        lc[l : l + 1] = jnp.sum(n, axis=0, keepdims=True)
    wide = lambda v: jnp.broadcast_to(jnp.sum(v[...], axis=1, keepdims=True), (LANGS, 128))
    count = jnp.maximum(wide(lc), 1.0)
    score = jnp.log(dw[...]) + STEP_SIZE * (wide(ls) / count)
    score = jnp.exp(score - jnp.max(score, axis=0, keepdims=True))
    mixture = score / jnp.sum(score, axis=0, keepdims=True)
    new = (1.0 - SMOOTHING) * mixture + SMOOTHING / LANGS
    logw[...] = jnp.log(new)
    per_token = new / count * 2048.0
    weight = jnp.zeros(every.shape, F32)
    for l in range(LANGS):
        weight = jnp.where(every == l, per_token[l : l + 1], weight)
    tw[...] = weight
    lse_own, tw_own = line(lambda r: lse[r : r + 1]), line(lambda r: tw[r : r + 1])

    @pl.loop(0, 8)
    def _(n):
        vocab = lax.broadcasted_iota(jnp.int32, (128, 1024), 0) + (base + n * 128)
        hit = jnp.where(vocab == own_tgt, 1.0, 0.0)
        vd[tile(n)] = (tw_own * (jnp.exp(lg[tile(n)] - lse_own) - hit)).astype(BF16)

    def d_rows(cc):
        at = pl.ds(pl.multiple_of(cc * 512, 512), 512)
        part = lax.dot_general(vd[:, at], vh[...], rows, preferred_element_type=F32)
        d_x[cc] = part.astype(BF16).reshape(4, 128, 1024)

    d_rows(1 - c)
    across = {}
    for m in ROWS:
        bb = ring(a, m)
        across[m] = go.start(d_x.at[1 - c, bb], r0.at[bb], me.core())
    d_rows(c)
    collect = Collect(go, me, d_rb, d_ra)
    for m in ROWS:
        bb = ring(b, m)
        across[m].wait_recv()
        joined = d_x[c, bb].astype(F32) + r0[bb].astype(F32)
        acc[bb] = joined.astype(BF16).reshape(acc.shape[1:])
        collect.row(m, acc.at[bb])
    far = []
    for k in (0, 1, 3, 2):
        row = vf.at[c, beside.row(k)]
        far.append(go.start(row, row, me.core()))
    for copy in far:
        copy.wait_recv()
    far_tgt = line(lambda r: tl[1, 0, r])

    def head_rows(n):
        at = tile(n)
        states = vf[...].reshape(1024, 1024)
        logits = lax.dot_general(vh[at], states, lanes, preferred_element_type=F32)
        vocab = lax.broadcasted_iota(jnp.int32, (128, 1024), 0) + (base + n * 128)
        hit = jnp.where(vocab == far_tgt, 1.0, 0.0)
        lse_far = line(lambda r: lse[8 + r : 9 + r])
        tw_far = line(lambda r: tw[8 + r : 9 + r])
        d = (tw_far * (jnp.exp(logits - lse_far) - hit)).astype(BF16)
        grad_head[at] = jnp.dot(d, states, preferred_element_type=F32) + jnp.dot(
            vd[at], fin[...].reshape(1024, 1024), preferred_element_type=F32
        )

    pl.loop(0, 4)(head_rows)
    d_give[...] = collect.total(acc.at[b], d_units).astype(BF16)
    swap = go.start(d_give, d_rp, me.partner())
    pl.loop(4, 6)(head_rows)
    swap.wait_recv()
    d_final = d_give[...].astype(F32) + d_rp[...].astype(F32)
    middle = mid[...]
    inv = lax.rsqrt(jnp.mean(middle * middle, axis=1, keepdims=True) + EPSILON)
    scaled = d_final * gain_out[...]
    inner = jnp.mean(middle * scaled, axis=1, keepdims=True)
    d_mid = (inv * scaled - middle * inv * inv * inv * inner).astype(BF16)
    dmid[b, a] = d_mid.reshape(2, 16, 1024)
    d2 = Spread(go, me, lambda bb, aa: dmid.at[bb, aa])
    pl.loop(6, 8)(head_rows)
    d2.hand_on()
    h = pre[...].reshape(512, 256)
    g, u = h[:, :128], h[:, 128:]
    s = jax.nn.sigmoid(g)
    act = (g * s * u).astype(BF16)
    gate_slope = u * s * (1.0 + g * (1.0 - s))
    up_slope = g * s
    for k in (1, 3, 2):
        d2.row(k)
    dm = dmid[...].reshape(512, 1024)
    states_in = normed[...].reshape(512, 1024)
    d_act = lax.dot_general(dm, dnw[...], lanes, preferred_element_type=F32)
    for n, (left, right) in enumerate(
        (
            ((d_act * gate_slope).astype(BF16), states_in),
            ((d_act * up_slope).astype(BF16), states_in),
            (act, dm),
        )
    ):
        grad = lax.dot_general(left, right, rows, preferred_element_type=F32).astype(BF16)
        for j in range(8):
            comb[j % 2, j // 2 % 2, j // 4, 128 * n : 128 * (n + 1)] = grad[
                :, 128 * j : 128 * (j + 1)
            ]
    swap = go.start(comb.at[1 - c], oc, me.core())
    swap.wait_recv()
    sc[...] = (comb[c].astype(F32) + oc[...].astype(F32)).astype(BF16)
    swap = go.start(sc.at[1 - me.dp], ox, me.neighbour())
    swap.wait_recv()
    sx[...] = (sc[me.dp].astype(F32) + ox[...].astype(F32)).astype(BF16)
    half, odd = lax.div(me.y, 2), lax.rem(me.y, 2)

    def homeward(e, side, src):
        h = lax.rem(half + e, 2)
        return pltpu.make_async_remote_copy(
            src_ref=sx.at[h],
            dst_ref=rg.at[src],
            send_sem=hsend.at[2 * e + side],
            recv_sem=hrecv.at[src],
            device_id=me.at(dp=1 - me.dp if side else me.dp, y=2 * h + me.dp),
            device_id_type=MESH,
        )

    stays = odd == me.dp
    for e, side in ((1, 1), (1, 0), (0, 1)):
        homeward(e, side, me.y).start()

    @pl.when(jnp.logical_not(stays))
    def _():
        homeward(0, 0, me.y).start()

    @pl.when(stays)
    def _():
        rg[me.y] = sx[half]

    for j in range(4):

        @pl.when(jnp.logical_or(me.y != j, jnp.logical_not(stays)))
        def _(j=j):
            homeward(1, 1, j).wait_recv()

        at = slice(128 * j, 128 * (j + 1))
        got = rg[j].astype(F32)
        g_gate[:, at] = got[0:128].T
        g_up[:, at] = got[128:256].T
        g_down[at] = got[256:384]
    for e, side in ((1, 1), (1, 0), (0, 1)):
        homeward(e, side, me.y).wait_send()

    @pl.when(jnp.logical_not(stays))
    def _():
        homeward(0, 0, me.y).wait_send()

    go.drain()


def step(ids, hid, gain_in, gain_out, refh, ref_gain, gate, up, down, domain_weights, head, proxy_head):
    vmem = pl.BlockSpec(memory_space=pltpu.VMEM)
    hbm = pl.BlockSpec(memory_space=pl.ANY)
    shape = jax.ShapeDtypeStruct
    half = lambda *s: pltpu.VMEM(s, BF16)
    full = lambda *s: pltpu.VMEM(s, F32)
    ints = lambda *s: pltpu.VMEM(s, jnp.int32)
    return pl.pallas_call(
        step_body,
        out_shape=[
            shape((LANGS, 128), F32),
            shape((1024, 1024), F32),
            shape((128, 512), F32),
            shape((128, 512), F32),
            shape((512, 128), F32),
        ],
        in_specs=[vmem] * 10 + [hbm] * 2,
        out_specs=[vmem] * 5,
        scratch_shapes=[
            half(4, 4, 2, 16, 1024),
            full(4, 128, 256),
            half(2, 4, 4, 2, 16, 1024),
            half(2, 16, 1024),
            full(32, 1024),
            full(3, 8, 1, 128),
            ints(2, 2, 8, 1, 128),
            half(128, 1024),
            ints(4, 4, 8, 128),
            half(8, 128, 256),
            half(2, 4, 4, 2, 16, 4096),
            half(1024, 4096),
            half(256, 4096),
            full(1024, 256),
            half(4, 4, 32, 1024),
            half(4, 4, 32, 1024),
            half(4, 32, 1024),
            half(4, 32, 1024),
            half(32, 1024),
            half(32, 1024),
            half(2, 4, 4, 2, 16, 1024),
            half(1024, 1024),
            full(1024, 1024),
            full(2, 24, 128),
            full(2, 24, 128),
            full(16, 24, 128),
            full(2, 2, 24, 128),
            full(2, 2, 24, 128),
            full(16, 128),
            full(16, 128),
            full(LANGS, 128),
            full(LANGS, 128),
            half(2, 4, 128, 1024),
            half(4, 128, 1024),
            half(4, 4, 32, 1024),
            half(4, 4, 32, 1024),
            half(4, 32, 1024),
            half(4, 32, 1024),
            half(32, 1024),
            half(32, 1024),
            half(4, 4, 2, 16, 1024),
            half(2, 2, 2, 384, 128),
            half(2, 2, 384, 128),
            half(2, 2, 384, 128),
            half(2, 384, 128),
            half(2, 384, 128),
            half(4, 384, 128),
            pltpu.SemaphoreType.DMA((200,)),
            pltpu.SemaphoreType.DMA((200,)),
            pltpu.SemaphoreType.DMA((4,)),
            pltpu.SemaphoreType.DMA((4,)),
            pltpu.SemaphoreType.DMA((2,)),
        ],
        compiler_params=pltpu.CompilerParams(
            collective_id=1, has_side_effects=True, vmem_limit_bytes=VMEM_LIMIT * 2**20
        ),
        name="step",
    )(
        ids, hid, gain_in, gain_out, refh, ref_gain, gate, up, down,
        jnp.broadcast_to(domain_weights[:, None], (LANGS, 128)), head, proxy_head,
    )


def local(
    ref_hidden,
    proxy_hidden,
    targets,
    languages,
    ref_gain,
    ref_head,
    proxy_gain_in,
    proxy_gain_out,
    gate_weight,
    up_weight,
    down_weight,
    proxy_head,
    domain_weights,
):
    me = Place()
    mine = lambda v: lax.dynamic_slice_in_dim(v, me.z * 32, 32, 0)
    ids = jnp.tile(jnp.stack([mine(targets), mine(languages)]), (4, 4))
    lanes = lax.broadcasted_iota(jnp.int32, (8, 128), 1)
    ids = jnp.where(lax.div(lanes, 32) == me.a, ids, 0)
    log_weights, grad_head, grad_gate, grad_up, grad_down = step(
        ids,
        mine(proxy_hidden),
        proxy_gain_in[None],
        proxy_gain_out[None],
        ref_hidden,
        ref_gain[None],
        gate_weight,
        up_weight,
        down_weight,
        domain_weights,
        ref_head,
        proxy_head,
    )
    return (log_weights[:, 0], grad_gate, grad_up, grad_down, grad_head)


def solution(mesh):
    in_specs = (
        P(("dp", "fsdp", "tp"), None),
        P(("dp", "fsdp"), None),
        P(("dp", "fsdp")),
        P(("dp", "fsdp")),
        P(),
        P(("fsdp", "tp"), None),
        P(),
        P(),
        P("fsdp", "tp"),
        P("fsdp", "tp"),
        P("tp", "fsdp"),
        P(("fsdp", "tp"), None),
        P(),
    )
    out_specs = (P(), P("fsdp", "tp"), P("fsdp", "tp"), P("tp", "fsdp"), P(("fsdp", "tp"), None))
    return jax.shard_map(local, mesh=mesh, in_specs=in_specs, out_specs=out_specs, check_vma=False)
```

```python
import functools

import jax
import jax.numpy as jnp
from jax import lax
from jax.experimental import pallas as pl
from jax.experimental.pallas import tpu as pltpu
from jax.sharding import PartitionSpec as P

EPSILON = 1e-05
STEP_SIZE = 1.0
SMOOTHING = 0.001
LANGS = 64
VMEM_LIMIT = 58
MESH = pl.DeviceIdType.MESH
F32, BF16 = jnp.float32, jnp.bfloat16


class Place:
    def __init__(self):
        self.dp = lax.axis_index("dp")
        f, t = lax.axis_index("fsdp"), lax.axis_index("tp")
        self.f, self.t = f, t
        self.y, self.c = lax.div(f, 2), lax.rem(f, 2)
        self.z, self.xh = lax.div(t, 2), lax.rem(t, 2)
        self.p = self.xh
        c = self.c
        self.a = (1 - c) * self.y + c * self.z
        self.b = (1 - c) * self.z + c * self.y

    def at(self, dp=None, y=None, z=None, xh=None, c=None):
        pick = lambda new, old: old if new is None else new
        dp, y, z = pick(dp, self.dp), pick(y, self.y), pick(z, self.z)
        xh, c = pick(xh, self.xh), pick(c, self.c)
        return {"dp": dp, "fsdp": y * 2 + c, "tp": z * 2 + xh}

    def on_a(self, a):
        c = self.c
        return self.at(y=(1 - c) * a + c * self.y, z=(1 - c) * self.z + c * a)

    def on_b(self, b):
        c = self.c
        return self.at(y=(1 - c) * self.y + c * b, z=(1 - c) * b + c * self.z)

    def on_ab(self, a, b):
        c = self.c
        return self.at(y=(1 - c) * a + c * b, z=(1 - c) * b + c * a)

    def core(self):
        return self.at(c=1 - self.c)

    def partner(self):
        return self.at(xh=1 - self.xh)

    def neighbour(self):
        return self.at(dp=1 - self.dp)

    def opposite(self):
        return self.at(dp=1 - self.dp, xh=1 - self.xh)


class Copies:
    def __init__(self, send, recv):
        self.send, self.recv, self.n, self.all = send, recv, 0, []

    def start(self, src, dst, to):
        copy = pltpu.make_async_remote_copy(
            src_ref=src,
            dst_ref=dst,
            send_sem=self.send.at[self.n],
            recv_sem=self.recv.at[self.n],
            device_id=to,
            device_id_type=MESH,
        )
        copy.start()
        self.n += 1
        self.all.append(copy)
        return copy

    def drain(self):
        for copy in self.all:
            copy.wait_send()


def greet(peers):
    barrier = pltpu.get_barrier_semaphore()
    for peer in peers:
        pl.semaphore_signal(barrier, inc=1, device_id=peer, device_id_type=MESH)
    pl.semaphore_wait(barrier, len(peers))


def ring(i, k):
    return lax.rem(i + k, 4)


OFFSETS = [(k, i) for k in (2, 1, 3, 0) for i in range(4) if k or i]
ROWS = (2, 3, 1, 0)


def rms_rows(values, gain):
    values = values.astype(F32)
    return values * lax.rsqrt(jnp.mean(values * values, axis=-1, keepdims=True) + EPSILON) * gain


def to_plane(go, me, view):
    sent = {}
    for k, i in OFFSETS:
        to = me.on_ab(ring(me.a, i), ring(me.b, k))
        sent[k, i] = go.start(view, view, to)
    return sent


class Spread:
    def __init__(self, go, me, view):
        self.go, self.me, self.view = go, me, view
        own = view(me.b, me.a)
        self.near = {i: go.start(own, own, me.on_a(ring(me.a, i))) for i in (2, 1, 3)}
        self.along = {(k, 0): go.start(own, own, me.on_b(ring(me.b, k))) for k in (2, 1, 3)}

    def hand_on(self):
        me = self.me
        for i in (1, 3, 2):
            self.near[i].wait_recv()
            unit = self.view(me.b, ring(me.a, 4 - i))
            for k in (2, 1, 3):
                self.along[k, i] = self.go.start(unit, unit, me.on_b(ring(me.b, k)))

    def row(self, k):
        if k:
            for i in range(4):
                self.along[k, i].wait_recv()
        return ring(self.me.b, (4 - k) % 4)


class Collect:
    def __init__(self, go, me, rb, ra):
        self.go, self.me, self.rb, self.ra, self.sent = go, me, rb, ra, []

    def row(self, m, view):
        if m:
            self.sent.append(self.go.start(view, self.rb.at[m], self.me.on_b(ring(self.me.b, m))))

    def turn(self, own, units):
        go, me = self.go, self.me
        for copy in self.sent:
            copy.wait_recv()
        row = own[...].astype(F32)
        for m in (1, 2, 3):
            row = row + self.rb[m].astype(F32)
        units[...] = row.astype(BF16)
        self.swaps = [
            go.start(units.at[ring(me.a, i)], self.ra.at[i], me.on_a(ring(me.a, i))) for i in (2, 1, 3)
        ]

    def total(self, units):
        for copy in self.swaps:
            copy.wait_recv()
        total = units[self.me.a].astype(F32)
        for i in (1, 2, 3):
            total = total + self.ra[i].astype(F32)
        return total


def join_all(pieces):
    out = []
    for base in (0, 12):
        high = functools.reduce(jnp.maximum, [s[base : base + 4] for s in pieces])
        total = pick = None
        for s in pieces:
            t = s[base + 4 : base + 8] * jnp.exp(s[base : base + 4] - high)
            k = s[base + 8 : base + 12]
            total, pick = (t, k) if total is None else (total + t, pick + k)
        out += [high, total, pick]
    return jnp.concatenate(out, axis=0)


def step_body(
    targets, languages, hid, gain_in, gain_out, refh, ref_gain, gate, up, down, dw, head, proxy_head,
    logw, grad_head, g_gate, g_up, g_down,
    normed, pre, fin, fin_x, mid, ref_st, tl, dnw,
    idsg, guw, ref_all, headv, rhs, logit, x, rb, ra, units, give, rp,
    vf, vh, lg, st, slot_c, slot_yz, slot_x, both, lse, tw, ls, lc,
    d_x, r0, acc, d_rb, d_ra, d_units, d_give, d_rp, dmid, comb, oc, sc, ox, sx, rg,
    send, recv, hsend, hrecv, local,
):
    me = Place()
    a, b, c, p, f = me.a, me.b, me.c, me.p, me.f
    go = Copies(send, recv)
    plane = [me.on_ab(ring(a, i), ring(b, k)) for k, i in OFFSETS]
    x_peers = [me.partner(), me.neighbour(), me.opposite()]
    across_dp = [me.at(dp=1 - me.dp, y=ring(me.y, k)) for k in (1, 2, 3)]
    vd = headv.at[:, pl.ds(0, 1024)]
    take_proxy = pltpu.make_async_copy(proxy_head, vh, local.at[1])
    greet(plane + x_peers + [me.core()] + across_dp)
    take_head = pltpu.make_async_copy(head, headv, local.at[0])
    take_head.start()
    take_proxy.start()
    own_hid = pl.ds(pl.multiple_of(me.z * 32, 32), 32)
    normed[b, a] = rms_rows(hid[own_hid], gain_in[...]).astype(BF16).reshape(2, 16, 1024)
    s2 = Spread(go, me, lambda bb, aa: normed.at[bb, aa])
    both_ids = jnp.concatenate([targets[...], languages[...]] * 4, axis=0)
    turn = lax.rem(a - me.z + 4, 4)
    turned = both_ids
    for n in (1, 2, 3):
        turned = jnp.where(turn == n, pltpu.roll(both_ids, 32 * n, 1), turned)
    lane_unit = lax.div(lax.broadcasted_iota(jnp.int32, (8, 128), 1), 32)
    idsg[b, a] = jnp.where(lane_unit == a, turned, 0)
    s2_ids = Spread(go, me, lambda bb, aa: idsg.at[bb, aa])
    here = pl.ds(pl.multiple_of(f * 128, 128), 128)

    def weights(ff, to, y=None):
        lanes = pl.ds(pl.multiple_of(ff * 128, 128), 128)
        pieces = [guw.at[ff], dnw.at[:, lanes]]
        if y is None:
            return [go.start(v, v, to) for v in pieces]
        part = pl.ds(pl.multiple_of(y * 128, 128), 128)
        return [
            go.start(gate.at[:, part], guw.at[ff, :, pl.ds(0, 128)], to),
            go.start(up.at[:, part], guw.at[ff, :, pl.ds(128, 128)], to),
            go.start(down.at[part], pieces[1], to),
        ]

    w_sent = {k: weights(f, me.at(y=ring(me.y, k)), ring(me.y, k)) for k in (2, 1, 3)}
    w_core = weights(f, me.core(), me.y)
    part = pl.ds(pl.multiple_of(me.y * 128, 128), 128)
    guw[f, :, 0:128] = gate[:, part]
    guw[f, :, 128:256] = up[:, part]
    dnw[:, here] = down[part]
    ref_all[c, b, a, p] = rms_rows(refh[...], ref_gain[...]).astype(BF16)
    r1 = go.start(ref_all.at[c, b, a, p], ref_all.at[c, b, a, p], me.partner())
    s2.hand_on()
    s2_ids.hand_on()
    r1.wait_recv()
    unit = ref_all.at[c, b, a]
    r2 = [go.start(unit, unit, me.on_a(ring(a, k))) for k in (1, 3, 2)]
    for k in (1, 3, 2):
        for copy in w_sent[k]:
            copy.wait_recv()
        w_core += weights(2 * ring(me.y, 4 - k) + c, me.core())
    for copy in w_core:
        copy.wait_recv()
    collect = Collect(go, me, rb, ra)
    for k in (1, 3, 2, 0):
        bb = s2.row(k)
        h = jnp.dot(
            normed[bb].reshape(128, 1024), guw[...].reshape(1024, 256),
            preferred_element_type=F32,
        )
        pre[bb] = h
        g = h[:, :128]
        h = (g * jax.nn.sigmoid(g) * h[:, 128:]).astype(BF16)
        h = jnp.dot(h, dnw[...], preferred_element_type=F32).astype(BF16)
        x[bb] = h.reshape(4, 32, 1024)
        collect.row((4 - k) % 4, x.at[bb])
    for copy in r2:
        copy.wait_recv()
    right_b, left_b = me.on_b(ring(b, 1)), me.on_b(ring(b, 3))
    unit = ref_all.at[c, b]
    cross = {0: go.start(unit, unit, me.core())}
    r3 = [go.start(unit, unit, right_b), go.start(unit, unit, left_b)]
    for k in (1, 2, 3):
        s2_ids.row(k)
    for bb in range(4):
        row = idsg[bb, 0] + idsg[bb, 1] + idsg[bb, 2] + idsg[bb, 3]
        tl[0, 0, 4 * c + bb] = row[0:1]
        tl[0, 1, 4 * c + bb] = row[1:2]
    mine = pl.ds(4 * c, 4)
    ids_across = [
        go.start(tl.at[0, n, mine], tl.at[0, n, mine], me.core()) for n in range(2)
    ]
    for copy in ids_across:
        copy.wait_recv()
    ids_far = go.start(tl.at[0], tl.at[1], me.neighbour())
    vocab = lax.broadcasted_iota(jnp.int32, (1024, 256), 0) + (f * 8 + me.t) * 1024

    def ref_rows(m):
        b_own, b_far = ring(b, m), ring(a, m)
        rhs[0:128] = ref_all[c, b_own].reshape(128, 4096)
        rhs[128:256] = ref_all[1 - c, b_far].reshape(128, 4096)

        @pl.loop(0, 4)
        def _(n):
            at = pl.ds(pl.multiple_of(n * 256, 256), 256)
            logit[at] = lax.dot_general(
                headv[at], rhs[...], (((1,), (1,)), ((), ())), preferred_element_type=F32
            )

        value = logit[...]
        high = jnp.max(value, axis=0, keepdims=True)
        want = jnp.concatenate([tl[0, 0, 4 * c + b_own], tl[0, 0, 4 * (1 - c) + b_far]], axis=1)
        picked = jnp.sum(jnp.where(vocab == want, value, 0.0), axis=0, keepdims=True)
        total = jnp.sum(jnp.exp(value - high), axis=0, keepdims=True)
        for s, got in enumerate((high, total, picked)):
            ref_st[s, 4 * c + b_own] = got[:, :128]
            ref_st[s, 4 * (1 - c) + b_far] = got[:, 128:]

    take_head.wait()
    cross[0].wait_recv()
    ref_rows(0)
    collect.turn(x.at[b], units)
    give[...] = collect.total(units).astype(BF16)
    swap = go.start(give, rp, me.partner())
    swap.wait_recv()
    middle = hid[own_hid].astype(F32) + (give[...].astype(F32) + rp[...].astype(F32))
    mid[...] = middle
    fin[c, b, a] = rms_rows(middle, gain_out[...]).astype(BF16).reshape(2, 16, 1024)
    f2 = Spread(go, me, lambda bb, aa: fin.at[c, bb, aa])
    f_x = go.start(fin.at[c, b, a], fin_x, me.neighbour())
    f2.hand_on()
    r3[0].wait_recv()
    half = ref_all.at[c, ring(b, 3), pl.ds(0, 2)]
    r4 = [go.start(half, half, right_b)]
    r3[1].wait_recv()
    half = ref_all.at[c, ring(b, 1), pl.ds(2, 2)]
    r4.append(go.start(half, half, left_b))
    for m in (3, 1):
        unit = ref_all.at[c, ring(b, m)]
        cross[m] = go.start(unit, unit, me.core())
    cross[3].wait_recv()
    ref_rows(3)
    f3 = []
    for k in (0, 1, 3, 2):
        row = fin.at[c, f2.row(k)]
        f3.append(go.start(row, row, me.core()))
    for copy in f3 + [f_x, ids_far]:
        copy.wait_recv()
    take_proxy.wait()
    lanes = (((1,), (1,)), ((), ()))
    rows = (((0,), (0,)), ((), ()))
    base = (f * 8 + me.t) * 1024
    tile = lambda n: pl.ds(pl.multiple_of(n * 128, 128), 128)

    def line(v):
        return jnp.concatenate([v(r) for r in range(8)], axis=1)

    def own_rows(n, high):
        logits = lax.dot_general(vh[tile(n)], fin[...].reshape(1024, 1024), lanes, preferred_element_type=F32)
        lg[tile(n)] = logits
        return jnp.maximum(high, jnp.max(logits, axis=0, keepdims=True))

    high = lax.fori_loop(0, 8, own_rows, jnp.full((1, 1024), -jnp.inf, F32))
    for copy in r4:
        copy.wait_recv()
    unit = ref_all.at[c, ring(b, 2)]
    cross[2] = go.start(unit, unit, me.core())
    own_tgt = line(lambda r: tl[0, 0, r])

    def own_sums(n, carry):
        total, picked = carry
        logits = lg[tile(n)]
        vocab = lax.broadcasted_iota(jnp.int32, (128, 1024), 0) + (base + n * 128)
        total += jnp.sum(jnp.exp(logits - high), axis=0, keepdims=True)
        picked += jnp.sum(jnp.where(vocab == own_tgt, logits, 0.0), axis=0, keepdims=True)
        return total, picked

    zero = jnp.zeros((1, 1024), F32)
    total, picked = lax.fori_loop(0, 8, own_sums, (zero, zero))
    cross[1].wait_recv()
    ref_rows(1)
    cross[2].wait_recv()
    ref_rows(2)
    for r in range(8):
        h, q = r // 4, r % 4
        for s in range(3):
            st[h, 4 * s + q : 4 * s + q + 1] = ref_st[s, r]
        for s, v in enumerate((high, total, picked)):
            st[h, 12 + 4 * s + q : 13 + 4 * s + q] = v[:, 128 * r : 128 * (r + 1)]
    slot_c[c] = st[c]
    half = go.start(st.at[1 - c], slot_c.at[c], me.core())
    half.wait_recv()
    yz = me.y * 4 + me.z
    slot_yz[yz] = join_all([slot_c[0], slot_c[1]])
    sent = to_plane(go, me, slot_yz.at[yz])
    vf[c, b, a] = fin_x[...]
    for copy in sent.values():
        copy.wait_recv()
    slot_x[0, p] = join_all([slot_yz[j] for j in range(16)])
    spread = [
        go.start(slot_x.at[0, p], slot_x.at[g, p], to) for g, to in zip((0, 1, 1), x_peers)
    ]
    beside = Spread(go, me, lambda bb, aa: vf.at[c, bb, aa])
    for copy in spread:
        copy.wait_recv()
    both[c, 0] = join_all([slot_x[0, 0], slot_x[0, 1]])
    both[c, 1] = join_all([slot_x[1, 0], slot_x[1, 1]])
    share = go.start(both.at[c], both.at[c], me.core())
    share.wait_recv()
    beside.hand_on()
    excess = [None, None]
    for g in range(2):
        now = [
            jnp.concatenate([both[0, g, 4 * i : 4 * i + 4], both[1, g, 4 * i : 4 * i + 4]])
            for i in range(6)
        ]
        ref_loss = now[0] + jnp.log(now[1]) - now[2]
        proxy_lse = now[3] + jnp.log(now[4])
        lse[8 * g : 8 * g + 8] = proxy_lse
        excess[g] = jnp.maximum(proxy_lse - now[5] - ref_loss, 0.0)
    every = jnp.concatenate([tl[g, 1, r] for g in range(2) for r in range(8)], axis=0)
    for l in range(LANGS):
        here = every == l
        e = jnp.where(here[:8], excess[0], 0.0) + jnp.where(here[8:], excess[1], 0.0)
        n = jnp.where(here[:8], 1.0, 0.0) + jnp.where(here[8:], 1.0, 0.0)
        ls[l : l + 1] = jnp.sum(e, axis=0, keepdims=True)
        lc[l : l + 1] = jnp.sum(n, axis=0, keepdims=True)
    wide = lambda v: jnp.broadcast_to(jnp.sum(v[...], axis=1, keepdims=True), (LANGS, 128))
    count = jnp.maximum(wide(lc), 1.0)
    prior = jnp.broadcast_to(jnp.log(dw[...]), (128, LANGS)).T
    score = prior + STEP_SIZE * (wide(ls) / count)
    score = jnp.exp(score - jnp.max(score, axis=0, keepdims=True))
    mixture = score / jnp.sum(score, axis=0, keepdims=True)
    new = (1.0 - SMOOTHING) * mixture + SMOOTHING / LANGS
    logw[...] = jnp.log(new).T[0:1]
    per_token = new / count * 2048.0
    weight = jnp.zeros(every.shape, F32)
    for l in range(LANGS):
        weight = jnp.where(every == l, per_token[l : l + 1], weight)
    tw[...] = weight
    lse_own, tw_own = line(lambda r: lse[r : r + 1]), line(lambda r: tw[r : r + 1])

    @pl.loop(0, 8)
    def _(n):
        vocab = lax.broadcasted_iota(jnp.int32, (128, 1024), 0) + (base + n * 128)
        hit = jnp.where(vocab == own_tgt, 1.0, 0.0)
        vd[tile(n)] = (tw_own * (jnp.exp(lg[tile(n)] - lse_own) - hit)).astype(BF16)

    def d_rows(cc):
        at = pl.ds(pl.multiple_of(cc * 512, 512), 512)
        part = lax.dot_general(vd[:, at], vh[...], rows, preferred_element_type=F32)
        d_x[cc] = part.astype(BF16).reshape(4, 128, 1024)

    d_rows(1 - c)
    across = {}
    for m in ROWS:
        bb = ring(a, m)
        across[m] = go.start(d_x.at[1 - c, bb], r0.at[bb], me.core())
    d_rows(c)
    collect = Collect(go, me, d_rb, d_ra)
    for m in ROWS:
        bb = ring(b, m)
        across[m].wait_recv()
        joined = d_x[c, bb].astype(F32) + r0[bb].astype(F32)
        acc[bb] = joined.astype(BF16).reshape(acc.shape[1:])
        collect.row(m, acc.at[bb])
    far = []
    for k in (0, 1, 3, 2):
        row = vf.at[c, beside.row(k)]
        far.append(go.start(row, row, me.core()))
    for copy in far:
        copy.wait_recv()
    far_tgt = line(lambda r: tl[1, 0, r])

    def head_rows(n):
        at = tile(n)
        states = vf[...].reshape(1024, 1024)
        logits = lax.dot_general(vh[at], states, lanes, preferred_element_type=F32)
        vocab = lax.broadcasted_iota(jnp.int32, (128, 1024), 0) + (base + n * 128)
        hit = jnp.where(vocab == far_tgt, 1.0, 0.0)
        lse_far = line(lambda r: lse[8 + r : 9 + r])
        tw_far = line(lambda r: tw[8 + r : 9 + r])
        d = (tw_far * (jnp.exp(logits - lse_far) - hit)).astype(BF16)
        grad = jnp.dot(d, states, preferred_element_type=F32)
        grad += jnp.dot(vd[at], fin[...].reshape(1024, 1024), preferred_element_type=F32)
        grad_head[at] = grad.astype(BF16)

    pl.loop(0, 2)(head_rows)
    collect.turn(acc.at[b], d_units)
    pl.loop(2, 4)(head_rows)
    d_give[...] = collect.total(d_units).astype(BF16)
    swap = go.start(d_give, d_rp, me.partner())
    pl.loop(4, 6)(head_rows)
    swap.wait_recv()
    d_final = d_give[...].astype(F32) + d_rp[...].astype(F32)
    middle = mid[...]
    inv = lax.rsqrt(jnp.mean(middle * middle, axis=1, keepdims=True) + EPSILON)
    scaled = d_final * gain_out[...]
    inner = jnp.mean(middle * scaled, axis=1, keepdims=True)
    d_mid = (inv * scaled - middle * inv * inv * inv * inner).astype(BF16)
    dmid[b, a] = d_mid.reshape(2, 16, 1024)
    d2 = Spread(go, me, lambda bb, aa: dmid.at[bb, aa])
    pl.loop(6, 8)(head_rows)
    d2.hand_on()
    h = pre[...].reshape(512, 256)
    g, u = h[:, :128], h[:, 128:]
    s = jax.nn.sigmoid(g)
    act = (g * s * u).astype(BF16)
    gate_slope = u * s * (1.0 + g * (1.0 - s))
    up_slope = g * s
    for k in (1, 3, 2):
        d2.row(k)
    dm = dmid[...].reshape(512, 1024)
    states_in = normed[...].reshape(512, 1024)
    d_act = lax.dot_general(dm, dnw[...], lanes, preferred_element_type=F32)
    for n, (left, right) in enumerate(
        (
            ((d_act * gate_slope).astype(BF16), states_in),
            ((d_act * up_slope).astype(BF16), states_in),
            (act, dm),
        )
    ):
        grad = lax.dot_general(left, right, rows, preferred_element_type=F32).astype(BF16)
        for j in range(8):
            comb[j % 2, j // 2 % 2, j // 4, 128 * n : 128 * (n + 1)] = grad[
                :, 128 * j : 128 * (j + 1)
            ]
    swap = go.start(comb.at[1 - c], oc, me.core())
    swap.wait_recv()
    sc[...] = (comb[c].astype(F32) + oc[...].astype(F32)).astype(BF16)
    swap = go.start(sc.at[1 - me.dp], ox, me.neighbour())
    swap.wait_recv()
    sx[...] = (sc[me.dp].astype(F32) + ox[...].astype(F32)).astype(BF16)
    half, odd = lax.div(me.y, 2), lax.rem(me.y, 2)

    def homeward(e, side, src):
        h = lax.rem(half + e, 2)
        return pltpu.make_async_remote_copy(
            src_ref=sx.at[h],
            dst_ref=rg.at[src],
            send_sem=hsend.at[2 * e + side],
            recv_sem=hrecv.at[src],
            device_id=me.at(dp=1 - me.dp if side else me.dp, y=2 * h + me.dp),
            device_id_type=MESH,
        )

    stays = odd == me.dp
    for e, side in ((1, 1), (1, 0), (0, 1)):
        homeward(e, side, me.y).start()

    @pl.when(jnp.logical_not(stays))
    def _():
        homeward(0, 0, me.y).start()

    @pl.when(stays)
    def _():
        rg[me.y] = sx[half]

    for j in range(4):

        @pl.when(jnp.logical_or(me.y != j, jnp.logical_not(stays)))
        def _(j=j):
            homeward(1, 1, j).wait_recv()

        at = slice(128 * j, 128 * (j + 1))
        got = rg[j].astype(F32)
        g_gate[:, at] = got[0:128].T.astype(BF16)
        g_up[:, at] = got[128:256].T.astype(BF16)
        g_down[at] = rg[j, 256:384]
    for e, side in ((1, 1), (1, 0), (0, 1)):
        homeward(e, side, me.y).wait_send()

    @pl.when(jnp.logical_not(stays))
    def _():
        homeward(0, 0, me.y).wait_send()

    go.drain()


def step(*arrays):
    vmem = pl.BlockSpec(memory_space=pltpu.VMEM)
    hbm = pl.BlockSpec(memory_space=pl.ANY)
    shape = jax.ShapeDtypeStruct
    half = lambda *s: pltpu.VMEM(s, BF16)
    full = lambda *s: pltpu.VMEM(s, F32)
    ints = lambda *s: pltpu.VMEM(s, jnp.int32)
    return pl.pallas_call(
        step_body,
        out_shape=[
            shape((1, LANGS), F32),
            shape((1024, 1024), BF16),
            shape((128, 512), BF16),
            shape((128, 512), BF16),
            shape((512, 128), BF16),
        ],
        in_specs=[vmem] * 11 + [hbm] * 2,
        out_specs=[vmem] * 5,
        scratch_shapes=[
            half(4, 4, 2, 16, 1024),
            full(4, 128, 256),
            half(2, 4, 4, 2, 16, 1024),
            half(2, 16, 1024),
            full(32, 1024),
            full(3, 8, 1, 128),
            ints(2, 2, 8, 1, 128),
            half(128, 1024),
            ints(4, 4, 8, 128),
            half(8, 128, 256),
            half(2, 4, 4, 2, 16, 4096),
            half(1024, 4096),
            half(256, 4096),
            full(1024, 256),
            half(4, 4, 32, 1024),
            half(4, 4, 32, 1024),
            half(4, 32, 1024),
            half(4, 32, 1024),
            half(32, 1024),
            half(32, 1024),
            half(2, 4, 4, 2, 16, 1024),
            half(1024, 1024),
            full(1024, 1024),
            full(2, 24, 128),
            full(2, 24, 128),
            full(16, 24, 128),
            full(2, 2, 24, 128),
            full(2, 2, 24, 128),
            full(16, 128),
            full(16, 128),
            full(LANGS, 128),
            full(LANGS, 128),
            half(2, 4, 128, 1024),
            half(4, 128, 1024),
            half(4, 4, 32, 1024),
            half(4, 4, 32, 1024),
            half(4, 32, 1024),
            half(4, 32, 1024),
            half(32, 1024),
            half(32, 1024),
            half(4, 4, 2, 16, 1024),
            half(2, 2, 2, 384, 128),
            half(2, 2, 384, 128),
            half(2, 2, 384, 128),
            half(2, 384, 128),
            half(2, 384, 128),
            half(4, 384, 128),
            pltpu.SemaphoreType.DMA((200,)),
            pltpu.SemaphoreType.DMA((200,)),
            pltpu.SemaphoreType.DMA((4,)),
            pltpu.SemaphoreType.DMA((4,)),
            pltpu.SemaphoreType.DMA((2,)),
        ],
        compiler_params=pltpu.CompilerParams(
            collective_id=1, has_side_effects=True, vmem_limit_bytes=VMEM_LIMIT * 2**20
        ),
        name="step",
    )(*arrays)


def local(
    ref_hidden,
    proxy_hidden,
    targets,
    languages,
    ref_gain,
    ref_head,
    proxy_gain_in,
    proxy_gain_out,
    gate_weight,
    up_weight,
    down_weight,
    proxy_head,
    domain_weights,
):
    log_weights, grad_head, grad_gate, grad_up, grad_down = step(
        targets[None],
        languages[None],
        proxy_hidden,
        proxy_gain_in[None],
        proxy_gain_out[None],
        ref_hidden,
        ref_gain[None],
        gate_weight,
        up_weight,
        down_weight,
        domain_weights[None],
        ref_head,
        proxy_head,
    )
    grads = [g.astype(F32) for g in (grad_gate, grad_up, grad_down, grad_head)]
    return (log_weights[0], *grads)


def solution(mesh):
    in_specs = (
        P(("dp", "fsdp", "tp"), None),
        P(("dp", "fsdp"), None),
        P(("dp", "fsdp")),
        P(("dp", "fsdp")),
        P(),
        P(("fsdp", "tp"), None),
        P(),
        P(),
        P("fsdp", "tp"),
        P("fsdp", "tp"),
        P("tp", "fsdp"),
        P(("fsdp", "tp"), None),
        P(),
    )
    out_specs = (P(), P("fsdp", "tp"), P("fsdp", "tp"), P("tp", "fsdp"), P(("fsdp", "tp"), None))
    return jax.shard_map(local, mesh=mesh, in_specs=in_specs, out_specs=out_specs, check_vma=False)
```

```python
import functools

import jax
import jax.numpy as jnp
from jax import lax
from jax.experimental import pallas as pl
from jax.experimental.pallas import tpu as pltpu
from jax.sharding import PartitionSpec as P

EPSILON = 1e-05
STEP_SIZE = 1.0
SMOOTHING = 0.001
LANGS = 64
VMEM_LIMIT = 58
MESH = pl.DeviceIdType.MESH
F32, BF16 = jnp.float32, jnp.bfloat16


class Place:
    def __init__(self):
        self.dp = lax.axis_index("dp")
        f, t = lax.axis_index("fsdp"), lax.axis_index("tp")
        self.f, self.t = f, t
        self.y, self.c = lax.div(f, 2), lax.rem(f, 2)
        self.z, self.xh = lax.div(t, 2), lax.rem(t, 2)
        self.p = self.xh
        c = self.c
        self.a = (1 - c) * self.y + c * self.z
        self.b = (1 - c) * self.z + c * self.y

    def at(self, dp=None, y=None, z=None, xh=None, c=None):
        pick = lambda new, old: old if new is None else new
        dp, y, z = pick(dp, self.dp), pick(y, self.y), pick(z, self.z)
        xh, c = pick(xh, self.xh), pick(c, self.c)
        return {"dp": dp, "fsdp": y * 2 + c, "tp": z * 2 + xh}

    def on_a(self, a):
        c = self.c
        return self.at(y=(1 - c) * a + c * self.y, z=(1 - c) * self.z + c * a)

    def on_b(self, b):
        c = self.c
        return self.at(y=(1 - c) * self.y + c * b, z=(1 - c) * b + c * self.z)

    def on_ab(self, a, b):
        c = self.c
        return self.at(y=(1 - c) * a + c * b, z=(1 - c) * b + c * a)

    def core(self):
        return self.at(c=1 - self.c)

    def partner(self):
        return self.at(xh=1 - self.xh)

    def neighbour(self):
        return self.at(dp=1 - self.dp)

    def opposite(self):
        return self.at(dp=1 - self.dp, xh=1 - self.xh)


class Copies:
    def __init__(self, send, recv):
        self.send, self.recv, self.n, self.all = send, recv, 0, []

    def start(self, src, dst, to):
        copy = pltpu.make_async_remote_copy(
            src_ref=src,
            dst_ref=dst,
            send_sem=self.send.at[self.n],
            recv_sem=self.recv.at[self.n],
            device_id=to,
            device_id_type=MESH,
        )
        copy.start()
        self.n += 1
        self.all.append(copy)
        return copy

    def drain(self):
        for copy in self.all:
            copy.wait_send()


def greet(peers):
    barrier = pltpu.get_barrier_semaphore()
    for peer in peers:
        pl.semaphore_signal(barrier, inc=1, device_id=peer, device_id_type=MESH)
    pl.semaphore_wait(barrier, len(peers))


def ring(i, k):
    return lax.rem(i + k, 4)


OFFSETS = [(k, i) for k in (2, 1, 3, 0) for i in range(4) if k or i]
ROWS = (2, 3, 1, 0)


def rms_rows(values, gain):
    values = values.astype(F32)
    return values * lax.rsqrt(jnp.mean(values * values, axis=-1, keepdims=True) + EPSILON) * gain


def to_plane(go, me, view):
    sent = {}
    for k, i in OFFSETS:
        to = me.on_ab(ring(me.a, i), ring(me.b, k))
        sent[k, i] = go.start(view, view, to)
    return sent


class Spread:
    def __init__(self, go, me, view):
        self.go, self.me, self.view = go, me, view
        own = view(me.b, me.a)
        self.near = {i: go.start(own, own, me.on_a(ring(me.a, i))) for i in (2, 1, 3)}
        self.along = {(k, 0): go.start(own, own, me.on_b(ring(me.b, k))) for k in (2, 1, 3)}

    def hand_on(self):
        me = self.me
        for i in (1, 3, 2):
            self.near[i].wait_recv()
            unit = self.view(me.b, ring(me.a, 4 - i))
            for k in (2, 1, 3):
                self.along[k, i] = self.go.start(unit, unit, me.on_b(ring(me.b, k)))

    def row(self, k):
        if k:
            for i in range(4):
                self.along[k, i].wait_recv()
        return ring(self.me.b, (4 - k) % 4)


class Collect:
    def __init__(self, go, me, rb, ra):
        self.go, self.me, self.rb, self.ra, self.sent = go, me, rb, ra, []

    def row(self, m, view):
        if m:
            self.sent.append(self.go.start(view, self.rb.at[m], self.me.on_b(ring(self.me.b, m))))

    def turn(self, own, units):
        go, me = self.go, self.me
        for copy in self.sent:
            copy.wait_recv()
        row = own[...].astype(F32)
        for m in (1, 2, 3):
            row = row + self.rb[m].astype(F32)
        units[...] = row.astype(BF16)
        self.swaps = [
            go.start(units.at[ring(me.a, i)], self.ra.at[i], me.on_a(ring(me.a, i))) for i in (2, 1, 3)
        ]

    def total(self, units):
        for copy in self.swaps:
            copy.wait_recv()
        total = units[self.me.a].astype(F32)
        for i in (1, 2, 3):
            total = total + self.ra[i].astype(F32)
        return total


def join_all(pieces):
    out = []
    for base in (0, 12):
        high = functools.reduce(jnp.maximum, [s[base : base + 4] for s in pieces])
        total = pick = None
        for s in pieces:
            t = s[base + 4 : base + 8] * jnp.exp(s[base : base + 4] - high)
            k = s[base + 8 : base + 12]
            total, pick = (t, k) if total is None else (total + t, pick + k)
        out += [high, total, pick]
    return jnp.concatenate(out, axis=0)


def step_body(
    targets, languages, hid, gain_in, gain_out, refh, ref_gain, gate, up, down, dw, head, proxy_head,
    logw, grad_head, g_gate, g_up, g_down,
    normed, pre, fin, fin_x, mid, ref_st, tl, dnw,
    idsg, guw, ref_all, headv, rhs, logit, x, rb, ra, units, give, rp,
    vf, vh, lg, st, slot_c, slot_yz, slot_x, both, lse, tw, ls, lc,
    d_x, r0, acc, d_rb, d_ra, d_units, d_give, d_rp, dmid, comb, oc, sc, ox, sx, rg,
    send, recv, hsend, hrecv, local,
):
    me = Place()
    a, b, c, p, f = me.a, me.b, me.c, me.p, me.f
    go = Copies(send, recv)
    plane = [me.on_ab(ring(a, i), ring(b, k)) for k, i in OFFSETS]
    x_peers = [me.partner(), me.neighbour(), me.opposite()]
    across_dp = [me.at(dp=1 - me.dp, y=ring(me.y, k)) for k in (1, 2, 3)]
    vd = headv.at[:, pl.ds(0, 1024)]
    take_proxy = pltpu.make_async_copy(proxy_head, vh, local.at[1])
    greet(plane + x_peers + [me.core()] + across_dp)
    take_head = pltpu.make_async_copy(head, headv, local.at[0])
    take_head.start()
    take_proxy.start()
    own_hid = pl.ds(pl.multiple_of(me.z * 32, 32), 32)
    normed[b, a] = rms_rows(hid[own_hid], gain_in[...]).astype(BF16).reshape(2, 16, 1024)
    s2 = Spread(go, me, lambda bb, aa: normed.at[bb, aa])
    both_ids = jnp.concatenate([targets[...], languages[...]] * 4, axis=0)
    turn = lax.rem(a - me.z + 4, 4)
    turned = both_ids
    for n in (1, 2, 3):
        turned = jnp.where(turn == n, pltpu.roll(both_ids, 32 * n, 1), turned)
    lane_unit = lax.div(lax.broadcasted_iota(jnp.int32, (8, 128), 1), 32)
    idsg[b, a] = jnp.where(lane_unit == a, turned, 0)
    s2_ids = Spread(go, me, lambda bb, aa: idsg.at[bb, aa])
    here = pl.ds(pl.multiple_of(f * 128, 128), 128)

    def weights(ff, to, y=None):
        lanes = pl.ds(pl.multiple_of(ff * 128, 128), 128)
        pieces = [guw.at[ff], dnw.at[:, lanes]]
        if y is None:
            return [go.start(v, v, to) for v in pieces]
        part = pl.ds(pl.multiple_of(y * 128, 128), 128)
        return [
            go.start(gate.at[:, part], guw.at[ff, :, pl.ds(0, 128)], to),
            go.start(up.at[:, part], guw.at[ff, :, pl.ds(128, 128)], to),
            go.start(down.at[part], pieces[1], to),
        ]

    w_sent = {k: weights(f, me.at(y=ring(me.y, k)), ring(me.y, k)) for k in (2, 1, 3)}
    w_core = weights(f, me.core(), me.y)
    part = pl.ds(pl.multiple_of(me.y * 128, 128), 128)
    guw[f, :, 0:128] = gate[:, part]
    guw[f, :, 128:256] = up[:, part]
    dnw[:, here] = down[part]
    ref_all[c, b, a, p] = rms_rows(refh[...], ref_gain[...]).astype(BF16)
    r1 = go.start(ref_all.at[c, b, a, p], ref_all.at[c, b, a, p], me.partner())
    s2.hand_on()
    s2_ids.hand_on()
    r1.wait_recv()
    unit = ref_all.at[c, b, a]
    r2 = [go.start(unit, unit, me.on_a(ring(a, k))) for k in (1, 3, 2)]
    for k in (1, 3, 2):
        for copy in w_sent[k]:
            copy.wait_recv()
        w_core += weights(2 * ring(me.y, 4 - k) + c, me.core())
    for copy in w_core:
        copy.wait_recv()
    collect = Collect(go, me, rb, ra)
    for k in (1, 3, 2, 0):
        bb = s2.row(k)
        h = jnp.dot(
            normed[bb].reshape(128, 1024), guw[...].reshape(1024, 256),
            preferred_element_type=F32,
        )
        pre[bb] = h
        g = h[:, :128]
        h = (g * jax.nn.sigmoid(g) * h[:, 128:]).astype(BF16)
        h = jnp.dot(h, dnw[...], preferred_element_type=F32).astype(BF16)
        x[bb] = h.reshape(4, 32, 1024)
        collect.row((4 - k) % 4, x.at[bb])
    for copy in r2:
        copy.wait_recv()
    right_b, left_b = me.on_b(ring(b, 1)), me.on_b(ring(b, 3))
    unit = ref_all.at[c, b]
    cross = {0: go.start(unit, unit, me.core())}
    r3 = [go.start(unit, unit, right_b), go.start(unit, unit, left_b)]
    for k in (1, 2, 3):
        s2_ids.row(k)
    for bb in range(4):
        row = idsg[bb, 0] + idsg[bb, 1] + idsg[bb, 2] + idsg[bb, 3]
        tl[0, 0, 4 * c + bb] = row[0:1]
        tl[0, 1, 4 * c + bb] = row[1:2]
    mine = pl.ds(4 * c, 4)
    ids_across = [
        go.start(tl.at[0, n, mine], tl.at[0, n, mine], me.core()) for n in range(2)
    ]
    for copy in ids_across:
        copy.wait_recv()
    ids_far = go.start(tl.at[0], tl.at[1], me.neighbour())
    vocab = lax.broadcasted_iota(jnp.int32, (1024, 256), 0) + (f * 8 + me.t) * 1024

    def ref_rows(*pair):
        for n, at in enumerate(pair):
            rhs[128 * n : 128 * (n + 1)] = ref_all[at].reshape(128, 4096)

        @pl.loop(0, 4)
        def _(n):
            at = pl.ds(pl.multiple_of(n * 256, 256), 256)
            logit[at] = lax.dot_general(
                headv[at], rhs[...], (((1,), (1,)), ((), ())), preferred_element_type=F32
            )

        value = logit[...]
        high = jnp.max(value, axis=0, keepdims=True)
        want = jnp.concatenate([tl[0, 0, 4 * cc + bb] for cc, bb in pair], axis=1)
        picked = jnp.sum(jnp.where(vocab == want, value, 0.0), axis=0, keepdims=True)
        total = jnp.sum(jnp.exp(value - high), axis=0, keepdims=True)
        for s, got in enumerate((high, total, picked)):
            for n, (cc, bb) in enumerate(pair):
                ref_st[s, 4 * cc + bb] = got[:, 128 * n : 128 * (n + 1)]

    take_head.wait()
    cross[0].wait_recv()
    ref_rows((c, b), (1 - c, a))
    collect.turn(x.at[b], units)
    give[...] = collect.total(units).astype(BF16)
    swap = go.start(give, rp, me.partner())
    swap.wait_recv()
    middle = hid[own_hid].astype(F32) + (give[...].astype(F32) + rp[...].astype(F32))
    mid[...] = middle
    fin[c, b, a] = rms_rows(middle, gain_out[...]).astype(BF16).reshape(2, 16, 1024)
    f2 = Spread(go, me, lambda bb, aa: fin.at[c, bb, aa])
    f_x = go.start(fin.at[c, b, a], fin_x, me.neighbour())
    r3[0].wait_recv()
    half = ref_all.at[c, ring(b, 3), pl.ds(0, 2)]
    r4 = [go.start(half, half, right_b)]
    r3[1].wait_recv()
    half = ref_all.at[c, ring(b, 1), pl.ds(2, 2)]
    r4.append(go.start(half, half, left_b))
    for m in (3, 1):
        unit = ref_all.at[c, ring(b, m)]
        cross[m] = go.start(unit, unit, me.core())
    ref_rows((c, ring(b, 3)), (c, ring(b, 1)))
    f2.hand_on()
    cross[3].wait_recv()
    cross[1].wait_recv()
    ref_rows((1 - c, ring(a, 3)), (1 - c, ring(a, 1)))
    f3 = []
    for k in (0, 1, 3, 2):
        row = fin.at[c, f2.row(k)]
        f3.append(go.start(row, row, me.core()))
    take_proxy.wait()
    lanes = (((1,), (1,)), ((), ()))
    rows = (((0,), (0,)), ((), ()))
    base = (f * 8 + me.t) * 1024
    tile = lambda n: pl.ds(pl.multiple_of(n * 128, 128), 128)

    def line(v):
        return jnp.concatenate([v(r) for r in range(8)], axis=1)

    def half_rows(cc):
        at = pl.ds(pl.multiple_of(cc * 512, 512), 512)

        def some(n, high):
            states = fin[cc].reshape(512, 1024)
            logits = lax.dot_general(vh[tile(n)], states, lanes, preferred_element_type=F32)
            lg[tile(n), at] = logits
            return jnp.maximum(high, jnp.max(logits, axis=0, keepdims=True))

        return lax.fori_loop(0, 8, some, jnp.full((1, 512), -jnp.inf, F32))

    high_own = half_rows(c)
    for copy in r4:
        copy.wait_recv()
    unit = ref_all.at[c, ring(b, 2)]
    cross[2] = go.start(unit, unit, me.core())
    for copy in f3 + [f_x, ids_far]:
        copy.wait_recv()
    high_far = half_rows(1 - c)
    high = jnp.concatenate(
        [jnp.where(c == 0, high_own, high_far), jnp.where(c == 0, high_far, high_own)], axis=1
    )
    own_tgt = line(lambda r: tl[0, 0, r])

    def own_sums(n, carry):
        total, picked = carry
        logits = lg[tile(n)]
        vocab = lax.broadcasted_iota(jnp.int32, (128, 1024), 0) + (base + n * 128)
        total += jnp.sum(jnp.exp(logits - high), axis=0, keepdims=True)
        picked += jnp.sum(jnp.where(vocab == own_tgt, logits, 0.0), axis=0, keepdims=True)
        return total, picked

    zero = jnp.zeros((1, 1024), F32)
    total, picked = lax.fori_loop(0, 8, own_sums, (zero, zero))
    cross[2].wait_recv()
    ref_rows((c, ring(b, 2)), (1 - c, ring(a, 2)))
    for r in range(8):
        h, q = r // 4, r % 4
        for s in range(3):
            st[h, 4 * s + q : 4 * s + q + 1] = ref_st[s, r]
        for s, v in enumerate((high, total, picked)):
            st[h, 12 + 4 * s + q : 13 + 4 * s + q] = v[:, 128 * r : 128 * (r + 1)]
    slot_c[c] = st[c]
    half = go.start(st.at[1 - c], slot_c.at[c], me.core())
    half.wait_recv()
    yz = me.y * 4 + me.z
    slot_yz[yz] = join_all([slot_c[0], slot_c[1]])
    sent = to_plane(go, me, slot_yz.at[yz])
    vf[c, b, a] = fin_x[...]
    for copy in sent.values():
        copy.wait_recv()
    slot_x[0, p] = join_all([slot_yz[j] for j in range(16)])
    spread = [
        go.start(slot_x.at[0, p], slot_x.at[g, p], to) for g, to in zip((0, 1, 1), x_peers)
    ]
    beside = Spread(go, me, lambda bb, aa: vf.at[c, bb, aa])
    for copy in spread:
        copy.wait_recv()
    both[c, 0] = join_all([slot_x[0, 0], slot_x[0, 1]])
    both[c, 1] = join_all([slot_x[1, 0], slot_x[1, 1]])
    share = go.start(both.at[c], both.at[c], me.core())
    share.wait_recv()
    beside.hand_on()
    excess = [None, None]
    for g in range(2):
        now = [
            jnp.concatenate([both[0, g, 4 * i : 4 * i + 4], both[1, g, 4 * i : 4 * i + 4]])
            for i in range(6)
        ]
        ref_loss = now[0] + jnp.log(now[1]) - now[2]
        proxy_lse = now[3] + jnp.log(now[4])
        lse[8 * g : 8 * g + 8] = proxy_lse
        excess[g] = jnp.maximum(proxy_lse - now[5] - ref_loss, 0.0)
    every = jnp.concatenate([tl[g, 1, r] for g in range(2) for r in range(8)], axis=0)
    for l in range(LANGS):
        here = every == l
        e = jnp.where(here[:8], excess[0], 0.0) + jnp.where(here[8:], excess[1], 0.0)
        n = jnp.where(here[:8], 1.0, 0.0) + jnp.where(here[8:], 1.0, 0.0)
        ls[l : l + 1] = jnp.sum(e, axis=0, keepdims=True)
        lc[l : l + 1] = jnp.sum(n, axis=0, keepdims=True)
    wide = lambda v: jnp.broadcast_to(jnp.sum(v[...], axis=1, keepdims=True), (LANGS, 128))
    count = jnp.maximum(wide(lc), 1.0)
    prior = jnp.broadcast_to(jnp.log(dw[...]), (128, LANGS)).T
    score = prior + STEP_SIZE * (wide(ls) / count)
    score = jnp.exp(score - jnp.max(score, axis=0, keepdims=True))
    mixture = score / jnp.sum(score, axis=0, keepdims=True)
    new = (1.0 - SMOOTHING) * mixture + SMOOTHING / LANGS
    logw[...] = jnp.log(new).T[0:1]
    per_token = new / count * 2048.0
    weight = jnp.zeros(every.shape, F32)
    for l in range(LANGS):
        weight = jnp.where(every == l, per_token[l : l + 1], weight)
    tw[...] = weight
    lse_own, tw_own = line(lambda r: lse[r : r + 1]), line(lambda r: tw[r : r + 1])

    @pl.loop(0, 8)
    def _(n):
        vocab = lax.broadcasted_iota(jnp.int32, (128, 1024), 0) + (base + n * 128)
        hit = jnp.where(vocab == own_tgt, 1.0, 0.0)
        vd[tile(n)] = (tw_own * (jnp.exp(lg[tile(n)] - lse_own) - hit)).astype(BF16)

    def d_rows(cc):
        at = pl.ds(pl.multiple_of(cc * 512, 512), 512)
        part = lax.dot_general(vd[:, at], vh[...], rows, preferred_element_type=F32)
        d_x[cc] = part.astype(BF16).reshape(4, 128, 1024)

    d_rows(1 - c)
    across = {}
    for m in ROWS:
        bb = ring(a, m)
        across[m] = go.start(d_x.at[1 - c, bb], r0.at[bb], me.core())
    d_rows(c)
    collect = Collect(go, me, d_rb, d_ra)
    for m in ROWS:
        bb = ring(b, m)
        across[m].wait_recv()
        joined = d_x[c, bb].astype(F32) + r0[bb].astype(F32)
        acc[bb] = joined.astype(BF16).reshape(acc.shape[1:])
        collect.row(m, acc.at[bb])
    far = []
    for k in (0, 1, 3, 2):
        row = vf.at[c, beside.row(k)]
        far.append(go.start(row, row, me.core()))
    for copy in far:
        copy.wait_recv()
    far_tgt = line(lambda r: tl[1, 0, r])

    def head_rows(n):
        at = tile(n)
        states = vf[...].reshape(1024, 1024)
        logits = lax.dot_general(vh[at], states, lanes, preferred_element_type=F32)
        vocab = lax.broadcasted_iota(jnp.int32, (128, 1024), 0) + (base + n * 128)
        hit = jnp.where(vocab == far_tgt, 1.0, 0.0)
        lse_far = line(lambda r: lse[8 + r : 9 + r])
        tw_far = line(lambda r: tw[8 + r : 9 + r])
        d = (tw_far * (jnp.exp(logits - lse_far) - hit)).astype(BF16)
        grad = jnp.dot(d, states, preferred_element_type=F32)
        grad += jnp.dot(vd[at], fin[...].reshape(1024, 1024), preferred_element_type=F32)
        grad_head[at] = grad.astype(BF16)

    pl.loop(0, 2)(head_rows)
    collect.turn(acc.at[b], d_units)
    pl.loop(2, 4)(head_rows)
    d_give[...] = collect.total(d_units).astype(BF16)
    swap = go.start(d_give, d_rp, me.partner())
    pl.loop(4, 6)(head_rows)
    swap.wait_recv()
    d_final = d_give[...].astype(F32) + d_rp[...].astype(F32)
    middle = mid[...]
    inv = lax.rsqrt(jnp.mean(middle * middle, axis=1, keepdims=True) + EPSILON)
    scaled = d_final * gain_out[...]
    inner = jnp.mean(middle * scaled, axis=1, keepdims=True)
    d_mid = (inv * scaled - middle * inv * inv * inv * inner).astype(BF16)
    dmid[b, a] = d_mid.reshape(2, 16, 1024)
    d2 = Spread(go, me, lambda bb, aa: dmid.at[bb, aa])
    pl.loop(6, 8)(head_rows)
    d2.hand_on()
    h = pre[...].reshape(512, 256)
    g, u = h[:, :128], h[:, 128:]
    s = jax.nn.sigmoid(g)
    act = (g * s * u).astype(BF16)
    gate_slope = u * s * (1.0 + g * (1.0 - s))
    up_slope = g * s
    for k in (1, 3, 2):
        d2.row(k)
    dm = dmid[...].reshape(512, 1024)
    states_in = normed[...].reshape(512, 1024)
    d_act = lax.dot_general(dm, dnw[...], lanes, preferred_element_type=F32)
    for n, (left, right) in enumerate(
        (
            ((d_act * gate_slope).astype(BF16), states_in),
            ((d_act * up_slope).astype(BF16), states_in),
            (act, dm),
        )
    ):
        grad = lax.dot_general(left, right, rows, preferred_element_type=F32).astype(BF16)
        for j in range(8):
            comb[j % 2, j // 2 % 2, j // 4, 128 * n : 128 * (n + 1)] = grad[
                :, 128 * j : 128 * (j + 1)
            ]
    swap = go.start(comb.at[1 - c], oc, me.core())
    swap.wait_recv()
    sc[...] = (comb[c].astype(F32) + oc[...].astype(F32)).astype(BF16)
    swap = go.start(sc.at[1 - me.dp], ox, me.neighbour())
    swap.wait_recv()
    sx[...] = (sc[me.dp].astype(F32) + ox[...].astype(F32)).astype(BF16)
    half, odd = lax.div(me.y, 2), lax.rem(me.y, 2)

    def homeward(e, side, src):
        h = lax.rem(half + e, 2)
        return pltpu.make_async_remote_copy(
            src_ref=sx.at[h],
            dst_ref=rg.at[src],
            send_sem=hsend.at[2 * e + side],
            recv_sem=hrecv.at[src],
            device_id=me.at(dp=1 - me.dp if side else me.dp, y=2 * h + me.dp),
            device_id_type=MESH,
        )

    stays = odd == me.dp
    for e, side in ((1, 1), (1, 0), (0, 1)):
        homeward(e, side, me.y).start()

    @pl.when(jnp.logical_not(stays))
    def _():
        homeward(0, 0, me.y).start()

    @pl.when(stays)
    def _():
        rg[me.y] = sx[half]

    for j in range(4):

        @pl.when(jnp.logical_or(me.y != j, jnp.logical_not(stays)))
        def _(j=j):
            homeward(1, 1, j).wait_recv()

        at = slice(128 * j, 128 * (j + 1))
        got = rg[j].astype(F32)
        g_gate[:, at] = got[0:128].T.astype(BF16)
        g_up[:, at] = got[128:256].T.astype(BF16)
        g_down[at] = rg[j, 256:384]
    for e, side in ((1, 1), (1, 0), (0, 1)):
        homeward(e, side, me.y).wait_send()

    @pl.when(jnp.logical_not(stays))
    def _():
        homeward(0, 0, me.y).wait_send()

    go.drain()


def step(*arrays):
    vmem = pl.BlockSpec(memory_space=pltpu.VMEM)
    hbm = pl.BlockSpec(memory_space=pl.ANY)
    shape = jax.ShapeDtypeStruct
    half = lambda *s: pltpu.VMEM(s, BF16)
    full = lambda *s: pltpu.VMEM(s, F32)
    ints = lambda *s: pltpu.VMEM(s, jnp.int32)
    return pl.pallas_call(
        step_body,
        out_shape=[
            shape((1, LANGS), F32),
            shape((1024, 1024), BF16),
            shape((128, 512), BF16),
            shape((128, 512), BF16),
            shape((512, 128), BF16),
        ],
        in_specs=[vmem] * 11 + [hbm] * 2,
        out_specs=[vmem] * 5,
        scratch_shapes=[
            half(4, 4, 2, 16, 1024),
            full(4, 128, 256),
            half(2, 4, 4, 2, 16, 1024),
            half(2, 16, 1024),
            full(32, 1024),
            full(3, 8, 1, 128),
            ints(2, 2, 8, 1, 128),
            half(128, 1024),
            ints(4, 4, 8, 128),
            half(8, 128, 256),
            half(2, 4, 4, 2, 16, 4096),
            half(1024, 4096),
            half(256, 4096),
            full(1024, 256),
            half(4, 4, 32, 1024),
            half(4, 4, 32, 1024),
            half(4, 32, 1024),
            half(4, 32, 1024),
            half(32, 1024),
            half(32, 1024),
            half(2, 4, 4, 2, 16, 1024),
            half(1024, 1024),
            full(1024, 1024),
            full(2, 24, 128),
            full(2, 24, 128),
            full(16, 24, 128),
            full(2, 2, 24, 128),
            full(2, 2, 24, 128),
            full(16, 128),
            full(16, 128),
            full(LANGS, 128),
            full(LANGS, 128),
            half(2, 4, 128, 1024),
            half(4, 128, 1024),
            half(4, 4, 32, 1024),
            half(4, 4, 32, 1024),
            half(4, 32, 1024),
            half(4, 32, 1024),
            half(32, 1024),
            half(32, 1024),
            half(4, 4, 2, 16, 1024),
            half(2, 2, 2, 384, 128),
            half(2, 2, 384, 128),
            half(2, 2, 384, 128),
            half(2, 384, 128),
            half(2, 384, 128),
            half(4, 384, 128),
            pltpu.SemaphoreType.DMA((200,)),
            pltpu.SemaphoreType.DMA((200,)),
            pltpu.SemaphoreType.DMA((4,)),
            pltpu.SemaphoreType.DMA((4,)),
            pltpu.SemaphoreType.DMA((2,)),
        ],
        compiler_params=pltpu.CompilerParams(
            collective_id=1, has_side_effects=True, vmem_limit_bytes=VMEM_LIMIT * 2**20
        ),
        name="step",
    )(*arrays)


def local(
    ref_hidden,
    proxy_hidden,
    targets,
    languages,
    ref_gain,
    ref_head,
    proxy_gain_in,
    proxy_gain_out,
    gate_weight,
    up_weight,
    down_weight,
    proxy_head,
    domain_weights,
):
    log_weights, grad_head, grad_gate, grad_up, grad_down = step(
        targets[None],
        languages[None],
        proxy_hidden,
        proxy_gain_in[None],
        proxy_gain_out[None],
        ref_hidden,
        ref_gain[None],
        gate_weight,
        up_weight,
        down_weight,
        domain_weights[None],
        ref_head,
        proxy_head,
    )
    grads = [g.astype(F32) for g in (grad_gate, grad_up, grad_down, grad_head)]
    return (log_weights[0], *grads)


def solution(mesh):
    in_specs = (
        P(("dp", "fsdp", "tp"), None),
        P(("dp", "fsdp"), None),
        P(("dp", "fsdp")),
        P(("dp", "fsdp")),
        P(),
        P(("fsdp", "tp"), None),
        P(),
        P(),
        P("fsdp", "tp"),
        P("fsdp", "tp"),
        P("tp", "fsdp"),
        P(("fsdp", "tp"), None),
        P(),
    )
    out_specs = (P(), P("fsdp", "tp"), P("fsdp", "tp"), P("tp", "fsdp"), P(("fsdp", "tp"), None))
    return jax.shard_map(local, mesh=mesh, in_specs=in_specs, out_specs=out_specs, check_vma=False)
```

```python
import functools

import jax
import jax.numpy as jnp
from jax import lax
from jax.experimental import pallas as pl
from jax.experimental.pallas import tpu as pltpu
from jax.sharding import PartitionSpec as P

EPSILON = 1e-05
STEP_SIZE = 1.0
SMOOTHING = 0.001
LANGS = 64
VMEM_LIMIT = 60
MESH = pl.DeviceIdType.MESH
F32, BF16 = jnp.float32, jnp.bfloat16


class Place:
    def __init__(self):
        self.dp = lax.axis_index("dp")
        f, t = lax.axis_index("fsdp"), lax.axis_index("tp")
        self.f, self.t = f, t
        self.y, self.c = lax.div(f, 2), lax.rem(f, 2)
        self.z, self.xh = lax.div(t, 2), lax.rem(t, 2)
        self.p = self.xh
        c = self.c
        self.a = (1 - c) * self.y + c * self.z
        self.b = (1 - c) * self.z + c * self.y

    def at(self, dp=None, y=None, z=None, xh=None, c=None):
        pick = lambda new, old: old if new is None else new
        dp, y, z = pick(dp, self.dp), pick(y, self.y), pick(z, self.z)
        xh, c = pick(xh, self.xh), pick(c, self.c)
        return {"dp": dp, "fsdp": y * 2 + c, "tp": z * 2 + xh}

    def on_a(self, a):
        c = self.c
        return self.at(y=(1 - c) * a + c * self.y, z=(1 - c) * self.z + c * a)

    def on_b(self, b):
        c = self.c
        return self.at(y=(1 - c) * self.y + c * b, z=(1 - c) * b + c * self.z)

    def on_ab(self, a, b):
        c = self.c
        return self.at(y=(1 - c) * a + c * b, z=(1 - c) * b + c * a)

    def core(self):
        return self.at(c=1 - self.c)

    def partner(self):
        return self.at(xh=1 - self.xh)

    def neighbour(self):
        return self.at(dp=1 - self.dp)

    def opposite(self):
        return self.at(dp=1 - self.dp, xh=1 - self.xh)


class Copies:
    def __init__(self, send, recv):
        self.send, self.recv, self.n, self.all = send, recv, 0, []

    def start(self, src, dst, to):
        copy = pltpu.make_async_remote_copy(
            src_ref=src,
            dst_ref=dst,
            send_sem=self.send.at[self.n],
            recv_sem=self.recv.at[self.n],
            device_id=to,
            device_id_type=MESH,
        )
        copy.start()
        self.n += 1
        self.all.append(copy)
        return copy

    def drain(self):
        for copy in self.all:
            copy.wait_send()


def greet(peers):
    barrier = pltpu.get_barrier_semaphore()
    for peer in peers:
        pl.semaphore_signal(barrier, inc=1, device_id=peer, device_id_type=MESH)
    pl.semaphore_wait(barrier, len(peers))


def ring(i, k):
    return lax.rem(i + k, 4)


OFFSETS = [(k, i) for k in (2, 1, 3, 0) for i in range(4) if k or i]
ROWS = (2, 3, 1, 0)


def rms_rows(values, gain):
    values = values.astype(F32)
    return values * lax.rsqrt(jnp.mean(values * values, axis=-1, keepdims=True) + EPSILON) * gain


def to_plane(go, me, view):
    sent = {}
    for k, i in OFFSETS:
        to = me.on_ab(ring(me.a, i), ring(me.b, k))
        sent[k, i] = go.start(view, view, to)
    return sent


class Spread:
    def __init__(self, go, me, view):
        self.go, self.me, self.view = go, me, view
        own = view(me.b, me.a)
        self.near = {i: go.start(own, own, me.on_a(ring(me.a, i))) for i in (2, 1, 3)}
        self.along = {(k, 0): go.start(own, own, me.on_b(ring(me.b, k))) for k in (2, 1, 3)}

    def hand_on(self):
        me = self.me
        for i in (1, 3, 2):
            self.near[i].wait_recv()
            unit = self.view(me.b, ring(me.a, 4 - i))
            for k in (2, 1, 3):
                self.along[k, i] = self.go.start(unit, unit, me.on_b(ring(me.b, k)))

    def row(self, k):
        if k:
            for i in range(4):
                self.along[k, i].wait_recv()
        return ring(self.me.b, (4 - k) % 4)


class Collect:
    def __init__(self, go, me, rb, ra):
        self.go, self.me, self.rb, self.ra, self.sent = go, me, rb, ra, []

    def row(self, m, view):
        if m:
            self.sent.append(self.go.start(view, self.rb.at[m], self.me.on_b(ring(self.me.b, m))))

    def turn(self, own, units):
        go, me = self.go, self.me
        for copy in self.sent:
            copy.wait_recv()
        row = own[...].astype(F32)
        for m in (1, 2, 3):
            row = row + self.rb[m].astype(F32)
        units[...] = row.astype(BF16)
        self.swaps = [
            go.start(units.at[ring(me.a, i)], self.ra.at[i], me.on_a(ring(me.a, i))) for i in (2, 1, 3)
        ]

    def total(self, units):
        for copy in self.swaps:
            copy.wait_recv()
        total = units[self.me.a].astype(F32)
        for i in (1, 2, 3):
            total = total + self.ra[i].astype(F32)
        return total


def join_all(pieces):
    out = []
    for base in (0, 12):
        high = functools.reduce(jnp.maximum, [s[base : base + 4] for s in pieces])
        total = pick = None
        for s in pieces:
            t = s[base + 4 : base + 8] * jnp.exp(s[base : base + 4] - high)
            k = s[base + 8 : base + 12]
            total, pick = (t, k) if total is None else (total + t, pick + k)
        out += [high, total, pick]
    return jnp.concatenate(out, axis=0)


def step_body(
    targets, languages, hid, gain_in, gain_out, refh, ref_gain, gate, up, down, dw, head, proxy_head,
    logw, grad_head, g_gate, g_up, g_down,
    normed, pre, fin, fin_x, mid, ref_st, tl, dnw,
    idsg, guw, ref_all, headv, rhs, logit, x, rb, ra, units, give, rp,
    vf, vh, lg, st, slot_c, slot_yz, slot_x, both, lse, tw, ls, lc,
    d_x, r0, acc, d_rb, d_ra, d_units, d_give, d_rp, dmid, comb, oc, sc, ox, sx, rg,
    send, recv, hsend, hrecv, local,
):
    me = Place()
    a, b, c, p, f = me.a, me.b, me.c, me.p, me.f
    go = Copies(send, recv)
    plane = [me.on_ab(ring(a, i), ring(b, k)) for k, i in OFFSETS]
    x_peers = [me.partner(), me.neighbour(), me.opposite()]
    across_dp = [me.at(dp=1 - me.dp, y=ring(me.y, k)) for k in (1, 2, 3)]
    vd = headv.at[:, pl.ds(0, 1024)]
    take_proxy = pltpu.make_async_copy(proxy_head, vh, local.at[1])
    greet(plane + x_peers + [me.core()] + across_dp)
    take_head = pltpu.make_async_copy(head, headv, local.at[0])
    take_head.start()
    take_proxy.start()
    own_hid = pl.ds(pl.multiple_of(me.z * 32, 32), 32)
    normed[b, a] = rms_rows(hid[own_hid], gain_in[...]).astype(BF16).reshape(2, 16, 1024)
    s2 = Spread(go, me, lambda bb, aa: normed.at[bb, aa])
    both_ids = jnp.concatenate([targets[...], languages[...]] * 4, axis=0)
    turn = lax.rem(a - me.z + 4, 4)
    turned = both_ids
    for n in (1, 2, 3):
        turned = jnp.where(turn == n, pltpu.roll(both_ids, 32 * n, 1), turned)
    lane_unit = lax.div(lax.broadcasted_iota(jnp.int32, (8, 128), 1), 32)
    idsg[b, a] = jnp.where(lane_unit == a, turned, 0)
    s2_ids = Spread(go, me, lambda bb, aa: idsg.at[bb, aa])
    here = pl.ds(pl.multiple_of(f * 128, 128), 128)

    def weights(ff, to, y=None):
        lanes = pl.ds(pl.multiple_of(ff * 128, 128), 128)
        pieces = [guw.at[ff], dnw.at[:, lanes]]
        if y is None:
            return [go.start(v, v, to) for v in pieces]
        part = pl.ds(pl.multiple_of(y * 128, 128), 128)
        return [
            go.start(gate.at[:, part], guw.at[ff, :, pl.ds(0, 128)], to),
            go.start(up.at[:, part], guw.at[ff, :, pl.ds(128, 128)], to),
            go.start(down.at[part], pieces[1], to),
        ]

    w_sent = {k: weights(f, me.at(y=ring(me.y, k)), ring(me.y, k)) for k in (2, 1, 3)}
    w_core = weights(f, me.core(), me.y)
    part = pl.ds(pl.multiple_of(me.y * 128, 128), 128)
    guw[f, :, 0:128] = gate[:, part]
    guw[f, :, 128:256] = up[:, part]
    dnw[:, here] = down[part]
    ref_all[c, b, a, p] = rms_rows(refh[...], ref_gain[...]).astype(BF16)
    r1 = go.start(ref_all.at[c, b, a, p], ref_all.at[c, b, a, p], me.partner())
    s2.hand_on()
    s2_ids.hand_on()
    r1.wait_recv()
    unit = ref_all.at[c, b, a]
    r2 = [go.start(unit, unit, me.on_a(ring(a, k))) for k in (1, 3, 2)]
    for k in (1, 3, 2):
        for copy in w_sent[k]:
            copy.wait_recv()
        w_core += weights(2 * ring(me.y, 4 - k) + c, me.core())
    for copy in w_core:
        copy.wait_recv()
    collect = Collect(go, me, rb, ra)
    for k in (1, 3, 2, 0):
        bb = s2.row(k)
        h = jnp.dot(
            normed[bb].reshape(128, 1024), guw[...].reshape(1024, 256),
            preferred_element_type=F32,
        )
        pre[bb] = h
        g = h[:, :128]
        h = (g * jax.nn.sigmoid(g) * h[:, 128:]).astype(BF16)
        h = jnp.dot(h, dnw[...], preferred_element_type=F32).astype(BF16)
        x[bb] = h.reshape(4, 32, 1024)
        collect.row((4 - k) % 4, x.at[bb])
    for copy in r2:
        copy.wait_recv()
    right_b, left_b = me.on_b(ring(b, 1)), me.on_b(ring(b, 3))
    unit = ref_all.at[c, b]
    cross = {0: go.start(unit, unit, me.core())}
    r3 = [go.start(unit, unit, right_b), go.start(unit, unit, left_b)]
    for k in (1, 2, 3):
        s2_ids.row(k)
    for bb in range(4):
        row = idsg[bb, 0] + idsg[bb, 1] + idsg[bb, 2] + idsg[bb, 3]
        tl[0, 0, 4 * c + bb] = row[0:1]
        tl[0, 1, 4 * c + bb] = row[1:2]
    mine = pl.ds(4 * c, 4)
    ids_across = [
        go.start(tl.at[0, n, mine], tl.at[0, n, mine], me.core()) for n in range(2)
    ]
    for copy in ids_across:
        copy.wait_recv()
    ids_far = go.start(tl.at[0], tl.at[1], me.neighbour())
    vocab = lax.broadcasted_iota(jnp.int32, (1024, 256), 0) + (f * 8 + me.t) * 1024

    def ref_rows(*pair):
        for n, at in enumerate(pair):
            rhs[128 * n : 128 * (n + 1)] = ref_all[at].reshape(128, 4096)

        @pl.loop(0, 4)
        def _(n):
            at = pl.ds(pl.multiple_of(n * 256, 256), 256)
            logit[at] = lax.dot_general(
                headv[at], rhs[...], (((1,), (1,)), ((), ())), preferred_element_type=F32
            )

        value = logit[...]
        high = jnp.max(value, axis=0, keepdims=True)
        want = jnp.concatenate([tl[0, 0, 4 * cc + bb] for cc, bb in pair], axis=1)
        picked = jnp.sum(jnp.where(vocab == want, value, 0.0), axis=0, keepdims=True)
        total = jnp.sum(jnp.exp(value - high), axis=0, keepdims=True)
        for s, got in enumerate((high, total, picked)):
            for n, (cc, bb) in enumerate(pair):
                ref_st[s, 4 * cc + bb] = got[:, 128 * n : 128 * (n + 1)]

    take_head.wait()
    cross[0].wait_recv()
    ref_rows((c, b), (1 - c, a))
    collect.turn(x.at[b], units)
    give[...] = collect.total(units).astype(BF16)
    swap = go.start(give, rp, me.partner())
    swap.wait_recv()
    middle = hid[own_hid].astype(F32) + (give[...].astype(F32) + rp[...].astype(F32))
    mid[...] = middle
    fin[c, b, a] = rms_rows(middle, gain_out[...]).astype(BF16).reshape(2, 16, 1024)
    f2 = Spread(go, me, lambda bb, aa: fin.at[c, bb, aa])
    f_x = go.start(fin.at[c, b, a], fin_x, me.neighbour())
    f2.hand_on()
    r3[0].wait_recv()
    half = ref_all.at[c, ring(b, 3), pl.ds(0, 2)]
    r4 = [go.start(half, half, right_b)]
    r3[1].wait_recv()
    half = ref_all.at[c, ring(b, 1), pl.ds(2, 2)]
    r4.append(go.start(half, half, left_b))
    for m in (3, 1):
        unit = ref_all.at[c, ring(b, m)]
        cross[m] = go.start(unit, unit, me.core())
    ref_rows((c, ring(b, 3)), (c, ring(b, 1)))
    f3 = []
    for k in (0, 1, 3, 2):
        row = fin.at[c, f2.row(k)]
        f3.append(go.start(row, row, me.core()))
    take_proxy.wait()
    lanes = (((1,), (1,)), ((), ()))
    rows = (((0,), (0,)), ((), ()))
    base = (f * 8 + me.t) * 1024
    tile = lambda n: pl.ds(pl.multiple_of(n * 128, 128), 128)

    def line(v):
        return jnp.concatenate([v(r) for r in range(8)], axis=1)

    def half_rows(cc):
        at = pl.ds(pl.multiple_of(cc * 512, 512), 512)

        def some(n, high):
            states = fin[cc].reshape(512, 1024)
            logits = lax.dot_general(vh[tile(n)], states, lanes, preferred_element_type=F32)
            lg[tile(n), at] = logits
            return jnp.maximum(high, jnp.max(logits, axis=0, keepdims=True))

        return lax.fori_loop(0, 8, some, jnp.full((1, 512), -jnp.inf, F32))

    high_own = half_rows(c)
    for copy in r4:
        copy.wait_recv()
    unit = ref_all.at[c, ring(b, 2)]
    cross[2] = go.start(unit, unit, me.core())
    for copy in f3 + [f_x, ids_far]:
        copy.wait_recv()
    high_far = half_rows(1 - c)
    high = jnp.concatenate(
        [jnp.where(c == 0, high_own, high_far), jnp.where(c == 0, high_far, high_own)], axis=1
    )
    own_tgt = line(lambda r: tl[0, 0, r])

    def own_sums(n, carry):
        total, picked = carry
        logits = lg[tile(n)]
        vocab = lax.broadcasted_iota(jnp.int32, (128, 1024), 0) + (base + n * 128)
        total += jnp.sum(jnp.exp(logits - high), axis=0, keepdims=True)
        picked += jnp.sum(jnp.where(vocab == own_tgt, logits, 0.0), axis=0, keepdims=True)
        return total, picked

    zero = jnp.zeros((1, 1024), F32)
    total, picked = lax.fori_loop(0, 8, own_sums, (zero, zero))
    cross[3].wait_recv()
    cross[1].wait_recv()
    ref_rows((1 - c, ring(a, 3)), (1 - c, ring(a, 1)))
    cross[2].wait_recv()
    ref_rows((c, ring(b, 2)), (1 - c, ring(a, 2)))
    for r in range(8):
        h, q = r // 4, r % 4
        for s in range(3):
            st[h, 4 * s + q : 4 * s + q + 1] = ref_st[s, r]
        for s, v in enumerate((high, total, picked)):
            st[h, 12 + 4 * s + q : 13 + 4 * s + q] = v[:, 128 * r : 128 * (r + 1)]
    slot_c[c] = st[c]
    half = go.start(st.at[1 - c], slot_c.at[c], me.core())
    half.wait_recv()
    yz = me.y * 4 + me.z
    slot_yz[yz] = join_all([slot_c[0], slot_c[1]])
    sent = to_plane(go, me, slot_yz.at[yz])
    vf[c, b, a] = fin_x[...]
    for copy in sent.values():
        copy.wait_recv()
    slot_x[0, p] = join_all([slot_yz[j] for j in range(16)])
    spread = [
        go.start(slot_x.at[0, p], slot_x.at[g, p], to) for g, to in zip((0, 1, 1), x_peers)
    ]
    beside = Spread(go, me, lambda bb, aa: vf.at[c, bb, aa])
    for copy in spread:
        copy.wait_recv()
    both[c, 0] = join_all([slot_x[0, 0], slot_x[0, 1]])
    both[c, 1] = join_all([slot_x[1, 0], slot_x[1, 1]])
    share = go.start(both.at[c], both.at[c], me.core())
    share.wait_recv()
    beside.hand_on()
    excess = [None, None]
    for g in range(2):
        now = [
            jnp.concatenate([both[0, g, 4 * i : 4 * i + 4], both[1, g, 4 * i : 4 * i + 4]])
            for i in range(6)
        ]
        ref_loss = now[0] + jnp.log(now[1]) - now[2]
        proxy_lse = now[3] + jnp.log(now[4])
        lse[8 * g : 8 * g + 8] = proxy_lse
        excess[g] = jnp.maximum(proxy_lse - now[5] - ref_loss, 0.0)
    every = jnp.concatenate([tl[g, 1, r] for g in range(2) for r in range(8)], axis=0)
    for l in range(LANGS):
        here = every == l
        e = jnp.where(here[:8], excess[0], 0.0) + jnp.where(here[8:], excess[1], 0.0)
        n = jnp.where(here[:8], 1.0, 0.0) + jnp.where(here[8:], 1.0, 0.0)
        ls[l : l + 1] = jnp.sum(e, axis=0, keepdims=True)
        lc[l : l + 1] = jnp.sum(n, axis=0, keepdims=True)
    wide = lambda v: jnp.broadcast_to(jnp.sum(v[...], axis=1, keepdims=True), (LANGS, 128))
    count = jnp.maximum(wide(lc), 1.0)
    prior = jnp.broadcast_to(jnp.log(dw[...]), (128, LANGS)).T
    score = prior + STEP_SIZE * (wide(ls) / count)
    score = jnp.exp(score - jnp.max(score, axis=0, keepdims=True))
    mixture = score / jnp.sum(score, axis=0, keepdims=True)
    new = (1.0 - SMOOTHING) * mixture + SMOOTHING / LANGS
    logw[...] = jnp.log(new).T[0:1]
    per_token = new / count * 2048.0
    weight = jnp.zeros(every.shape, F32)
    for l in range(LANGS):
        weight = jnp.where(every == l, per_token[l : l + 1], weight)
    tw[...] = weight
    lse_own, tw_own = line(lambda r: lse[r : r + 1]), line(lambda r: tw[r : r + 1])

    @pl.loop(0, 8)
    def _(n):
        vocab = lax.broadcasted_iota(jnp.int32, (128, 1024), 0) + (base + n * 128)
        hit = jnp.where(vocab == own_tgt, 1.0, 0.0)
        vd[tile(n)] = (tw_own * (jnp.exp(lg[tile(n)] - lse_own) - hit)).astype(BF16)

    def d_rows(cc):
        at = pl.ds(pl.multiple_of(cc * 512, 512), 512)
        part = lax.dot_general(vd[:, at], vh[...], rows, preferred_element_type=F32)
        d_x[cc] = part.astype(BF16).reshape(4, 128, 1024)

    d_rows(1 - c)
    across = {}
    for m in ROWS:
        bb = ring(a, m)
        across[m] = go.start(d_x.at[1 - c, bb], r0.at[bb], me.core())
    d_rows(c)
    collect = Collect(go, me, d_rb, d_ra)
    for m in ROWS:
        bb = ring(b, m)
        across[m].wait_recv()
        joined = d_x[c, bb].astype(F32) + r0[bb].astype(F32)
        acc[bb] = joined.astype(BF16).reshape(acc.shape[1:])
        collect.row(m, acc.at[bb])
    far = []
    for k in (0, 1, 3, 2):
        row = vf.at[c, beside.row(k)]
        far.append(go.start(row, row, me.core()))
    for copy in far:
        copy.wait_recv()
    far_tgt = line(lambda r: tl[1, 0, r])

    def head_rows(n):
        at = tile(n)
        states = vf[...].reshape(1024, 1024)
        logits = lax.dot_general(vh[at], states, lanes, preferred_element_type=F32)
        vocab = lax.broadcasted_iota(jnp.int32, (128, 1024), 0) + (base + n * 128)
        hit = jnp.where(vocab == far_tgt, 1.0, 0.0)
        lse_far = line(lambda r: lse[8 + r : 9 + r])
        tw_far = line(lambda r: tw[8 + r : 9 + r])
        d = (tw_far * (jnp.exp(logits - lse_far) - hit)).astype(BF16)
        grad = jnp.dot(d, states, preferred_element_type=F32)
        grad += jnp.dot(vd[at], fin[...].reshape(1024, 1024), preferred_element_type=F32)
        grad_head[at] = grad.astype(BF16)

    pl.loop(0, 2)(head_rows)
    collect.turn(acc.at[b], d_units)
    pl.loop(2, 4)(head_rows)
    d_give[...] = collect.total(d_units).astype(BF16)
    swap = go.start(d_give, d_rp, me.partner())
    pl.loop(4, 6)(head_rows)
    swap.wait_recv()
    d_final = d_give[...].astype(F32) + d_rp[...].astype(F32)
    middle = mid[...]
    inv = lax.rsqrt(jnp.mean(middle * middle, axis=1, keepdims=True) + EPSILON)
    scaled = d_final * gain_out[...]
    inner = jnp.mean(middle * scaled, axis=1, keepdims=True)
    d_mid = (inv * scaled - middle * inv * inv * inv * inner).astype(BF16)
    dmid[b, a] = d_mid.reshape(2, 16, 1024)
    d2 = Spread(go, me, lambda bb, aa: dmid.at[bb, aa])
    pl.loop(6, 8)(head_rows)
    d2.hand_on()
    h = pre[...].reshape(512, 256)
    g, u = h[:, :128], h[:, 128:]
    s = jax.nn.sigmoid(g)
    act = (g * s * u).astype(BF16)
    gate_slope = u * s * (1.0 + g * (1.0 - s))
    up_slope = g * s
    for k in (1, 3, 2):
        d2.row(k)
    dm = dmid[...].reshape(512, 1024)
    states_in = normed[...].reshape(512, 1024)
    d_act = lax.dot_general(dm, dnw[...], lanes, preferred_element_type=F32)
    for n, (left, right) in enumerate(
        (
            ((d_act * gate_slope).astype(BF16), states_in),
            ((d_act * up_slope).astype(BF16), states_in),
            (act, dm),
        )
    ):
        grad = lax.dot_general(left, right, rows, preferred_element_type=F32).astype(BF16)
        for j in range(8):
            comb[j % 2, j // 2 % 2, j // 4, 128 * n : 128 * (n + 1)] = grad[
                :, 128 * j : 128 * (j + 1)
            ]
    swap = go.start(comb.at[1 - c], oc, me.core())
    swap.wait_recv()
    sc[...] = (comb[c].astype(F32) + oc[...].astype(F32)).astype(BF16)
    swap = go.start(sc.at[1 - me.dp], ox, me.neighbour())
    swap.wait_recv()
    sx[...] = (sc[me.dp].astype(F32) + ox[...].astype(F32)).astype(BF16)
    half, odd = lax.div(me.y, 2), lax.rem(me.y, 2)

    def homeward(e, side, src):
        h = lax.rem(half + e, 2)
        return pltpu.make_async_remote_copy(
            src_ref=sx.at[h],
            dst_ref=rg.at[src],
            send_sem=hsend.at[2 * e + side],
            recv_sem=hrecv.at[src],
            device_id=me.at(dp=1 - me.dp if side else me.dp, y=2 * h + me.dp),
            device_id_type=MESH,
        )

    stays = odd == me.dp
    for e, side in ((1, 1), (1, 0), (0, 1)):
        homeward(e, side, me.y).start()

    @pl.when(jnp.logical_not(stays))
    def _():
        homeward(0, 0, me.y).start()

    @pl.when(stays)
    def _():
        rg[me.y] = sx[half]

    for j in range(4):

        @pl.when(jnp.logical_or(me.y != j, jnp.logical_not(stays)))
        def _(j=j):
            homeward(1, 1, j).wait_recv()

        at = slice(128 * j, 128 * (j + 1))
        got = rg[j].astype(F32)
        g_gate[:, at] = got[0:128].T.astype(BF16)
        g_up[:, at] = got[128:256].T.astype(BF16)
        g_down[at] = rg[j, 256:384]
    for e, side in ((1, 1), (1, 0), (0, 1)):
        homeward(e, side, me.y).wait_send()

    @pl.when(jnp.logical_not(stays))
    def _():
        homeward(0, 0, me.y).wait_send()

    go.drain()


def step(*arrays):
    vmem = pl.BlockSpec(memory_space=pltpu.VMEM)
    hbm = pl.BlockSpec(memory_space=pl.ANY)
    shape = jax.ShapeDtypeStruct
    half = lambda *s: pltpu.VMEM(s, BF16)
    full = lambda *s: pltpu.VMEM(s, F32)
    ints = lambda *s: pltpu.VMEM(s, jnp.int32)
    return pl.pallas_call(
        step_body,
        out_shape=[
            shape((1, LANGS), F32),
            shape((1024, 1024), BF16),
            shape((128, 512), BF16),
            shape((128, 512), BF16),
            shape((512, 128), BF16),
        ],
        in_specs=[vmem] * 11 + [hbm] * 2,
        out_specs=[vmem] * 5,
        scratch_shapes=[
            half(4, 4, 2, 16, 1024),
            full(4, 128, 256),
            half(2, 4, 4, 2, 16, 1024),
            half(2, 16, 1024),
            full(32, 1024),
            full(3, 8, 1, 128),
            ints(2, 2, 8, 1, 128),
            half(128, 1024),
            ints(4, 4, 8, 128),
            half(8, 128, 256),
            half(2, 4, 4, 2, 16, 4096),
            half(1024, 4096),
            half(256, 4096),
            full(1024, 256),
            half(4, 4, 32, 1024),
            half(4, 4, 32, 1024),
            half(4, 32, 1024),
            half(4, 32, 1024),
            half(32, 1024),
            half(32, 1024),
            half(2, 4, 4, 2, 16, 1024),
            half(1024, 1024),
            full(1024, 1024),
            full(2, 24, 128),
            full(2, 24, 128),
            full(16, 24, 128),
            full(2, 2, 24, 128),
            full(2, 2, 24, 128),
            full(16, 128),
            full(16, 128),
            full(LANGS, 128),
            full(LANGS, 128),
            half(2, 4, 128, 1024),
            half(4, 128, 1024),
            half(4, 4, 32, 1024),
            half(4, 4, 32, 1024),
            half(4, 32, 1024),
            half(4, 32, 1024),
            half(32, 1024),
            half(32, 1024),
            half(4, 4, 2, 16, 1024),
            half(2, 2, 2, 384, 128),
            half(2, 2, 384, 128),
            half(2, 2, 384, 128),
            half(2, 384, 128),
            half(2, 384, 128),
            half(4, 384, 128),
            pltpu.SemaphoreType.DMA((200,)),
            pltpu.SemaphoreType.DMA((200,)),
            pltpu.SemaphoreType.DMA((4,)),
            pltpu.SemaphoreType.DMA((4,)),
            pltpu.SemaphoreType.DMA((2,)),
        ],
        compiler_params=pltpu.CompilerParams(
            collective_id=1, has_side_effects=True, vmem_limit_bytes=VMEM_LIMIT * 2**20
        ),
        name="step",
    )(*arrays)


def results_body(*refs):
    n = len(refs) // 2
    for src, dst in zip(refs[:n], refs[n:]):
        dst[...] = src[...].astype(F32)


def results(grads, log_weights):
    steps = 4
    block = lambda v: pl.BlockSpec((v.shape[0] // steps, v.shape[1]), lambda i: (i, 0))
    whole = pl.BlockSpec(log_weights.shape, lambda i: (0, 0))
    specs = [block(g) for g in grads] + [whole]
    arrays = [*grads, log_weights]
    return pl.pallas_call(
        results_body,
        grid=(steps,),
        out_shape=[jax.ShapeDtypeStruct(v.shape, F32) for v in arrays],
        in_specs=specs,
        out_specs=specs,
        compiler_params=pltpu.CompilerParams(vmem_limit_bytes=VMEM_LIMIT * 2**20),
        name="results",
    )(*arrays)


def local(
    ref_hidden,
    proxy_hidden,
    targets,
    languages,
    ref_gain,
    ref_head,
    proxy_gain_in,
    proxy_gain_out,
    gate_weight,
    up_weight,
    down_weight,
    proxy_head,
    domain_weights,
):
    log_weights, grad_head, grad_gate, grad_up, grad_down = step(
        targets[None],
        languages[None],
        proxy_hidden,
        proxy_gain_in[None],
        proxy_gain_out[None],
        ref_hidden,
        ref_gain[None],
        gate_weight,
        up_weight,
        down_weight,
        domain_weights[None],
        ref_head,
        proxy_head,
    )
    grad_gate, grad_up, grad_down, grad_head, log_weights = results(
        (grad_gate, grad_up, grad_down, grad_head), log_weights
    )
    return (log_weights[0], grad_gate, grad_up, grad_down, grad_head)


def solution(mesh):
    in_specs = (
        P(("dp", "fsdp", "tp"), None),
        P(("dp", "fsdp"), None),
        P(("dp", "fsdp")),
        P(("dp", "fsdp")),
        P(),
        P(("fsdp", "tp"), None),
        P(),
        P(),
        P("fsdp", "tp"),
        P("fsdp", "tp"),
        P("tp", "fsdp"),
        P(("fsdp", "tp"), None),
        P(),
    )
    out_specs = (P(), P("fsdp", "tp"), P("fsdp", "tp"), P("tp", "fsdp"), P(("fsdp", "tp"), None))
    return jax.shard_map(local, mesh=mesh, in_specs=in_specs, out_specs=out_specs, check_vma=False)
```

```python
import functools

import jax
import jax.numpy as jnp
from jax import lax
from jax.experimental import pallas as pl
from jax.experimental.pallas import tpu as pltpu
from jax.sharding import PartitionSpec as P

EPSILON = 1e-05
STEP_SIZE = 1.0
SMOOTHING = 0.001
LANGS = 64
VMEM_LIMIT = 60
MESH = pl.DeviceIdType.MESH
F32, BF16 = jnp.float32, jnp.bfloat16


class Place:
    def __init__(self):
        self.dp = lax.axis_index("dp")
        f, t = lax.axis_index("fsdp"), lax.axis_index("tp")
        self.f, self.t = f, t
        self.y, self.c = lax.div(f, 2), lax.rem(f, 2)
        self.z, self.xh = lax.div(t, 2), lax.rem(t, 2)
        self.p = self.xh
        c = self.c
        self.a = (1 - c) * self.y + c * self.z
        self.b = (1 - c) * self.z + c * self.y

    def at(self, dp=None, y=None, z=None, xh=None, c=None):
        pick = lambda new, old: old if new is None else new
        dp, y, z = pick(dp, self.dp), pick(y, self.y), pick(z, self.z)
        xh, c = pick(xh, self.xh), pick(c, self.c)
        return {"dp": dp, "fsdp": y * 2 + c, "tp": z * 2 + xh}

    def on_a(self, a):
        c = self.c
        return self.at(y=(1 - c) * a + c * self.y, z=(1 - c) * self.z + c * a)

    def on_b(self, b):
        c = self.c
        return self.at(y=(1 - c) * self.y + c * b, z=(1 - c) * b + c * self.z)

    def on_ab(self, a, b):
        c = self.c
        return self.at(y=(1 - c) * a + c * b, z=(1 - c) * b + c * a)

    def core(self):
        return self.at(c=1 - self.c)

    def partner(self):
        return self.at(xh=1 - self.xh)

    def neighbour(self):
        return self.at(dp=1 - self.dp)

    def opposite(self):
        return self.at(dp=1 - self.dp, xh=1 - self.xh)


class Copies:
    def __init__(self, send, recv):
        self.send, self.recv, self.n, self.all = send, recv, 0, []

    def start(self, src, dst, to):
        copy = pltpu.make_async_remote_copy(
            src_ref=src,
            dst_ref=dst,
            send_sem=self.send.at[self.n],
            recv_sem=self.recv.at[self.n],
            device_id=to,
            device_id_type=MESH,
        )
        copy.start()
        self.n += 1
        self.all.append(copy)
        return copy

    def drain(self):
        for copy in self.all:
            copy.wait_send()


def greet(peers):
    barrier = pltpu.get_barrier_semaphore()
    for peer in peers:
        pl.semaphore_signal(barrier, inc=1, device_id=peer, device_id_type=MESH)
    pl.semaphore_wait(barrier, len(peers))


def ring(i, k):
    return lax.rem(i + k, 4)


OFFSETS = [(k, i) for k in (2, 1, 3, 0) for i in range(4) if k or i]
ROWS = (2, 3, 1, 0)


def rms_rows(values, gain):
    values = values.astype(F32)
    return values * lax.rsqrt(jnp.mean(values * values, axis=-1, keepdims=True) + EPSILON) * gain


def to_plane(go, me, view):
    sent = {}
    for k, i in OFFSETS:
        to = me.on_ab(ring(me.a, i), ring(me.b, k))
        sent[k, i] = go.start(view, view, to)
    return sent


class Spread:
    def __init__(self, go, me, view):
        self.go, self.me, self.view = go, me, view
        own = view(me.b, me.a)
        self.near = {i: go.start(own, own, me.on_a(ring(me.a, i))) for i in (2, 1, 3)}
        self.along = {(k, 0): go.start(own, own, me.on_b(ring(me.b, k))) for k in (2, 1, 3)}

    def hand_on(self):
        me = self.me
        for i in (1, 3, 2):
            self.near[i].wait_recv()
            unit = self.view(me.b, ring(me.a, 4 - i))
            for k in (2, 1, 3):
                self.along[k, i] = self.go.start(unit, unit, me.on_b(ring(me.b, k)))

    def row(self, k):
        if k:
            for i in range(4):
                self.along[k, i].wait_recv()
        return ring(self.me.b, (4 - k) % 4)


class Collect:
    def __init__(self, go, me, rb, ra):
        self.go, self.me, self.rb, self.ra, self.sent = go, me, rb, ra, []

    def row(self, m, view):
        if m:
            self.sent.append(self.go.start(view, self.rb.at[m], self.me.on_b(ring(self.me.b, m))))

    def turn(self, own, units):
        go, me = self.go, self.me
        for copy in self.sent:
            copy.wait_recv()
        row = own[...].astype(F32)
        for m in (1, 2, 3):
            row = row + self.rb[m].astype(F32)
        units[...] = row.astype(BF16)
        self.swaps = [
            go.start(units.at[ring(me.a, i)], self.ra.at[i], me.on_a(ring(me.a, i))) for i in (2, 1, 3)
        ]

    def total(self, units):
        for copy in self.swaps:
            copy.wait_recv()
        total = units[self.me.a].astype(F32)
        for i in (1, 2, 3):
            total = total + self.ra[i].astype(F32)
        return total


def join_all(pieces):
    out = []
    for base in (0, 12):
        high = functools.reduce(jnp.maximum, [s[base : base + 4] for s in pieces])
        total = pick = None
        for s in pieces:
            t = s[base + 4 : base + 8] * jnp.exp(s[base : base + 4] - high)
            k = s[base + 8 : base + 12]
            total, pick = (t, k) if total is None else (total + t, pick + k)
        out += [high, total, pick]
    return jnp.concatenate(out, axis=0)


def step_body(
    targets, languages, hid, gain_in, gain_out, refh, ref_gain, gate, up, down, dw, head, proxy_head,
    logw, grad_head, g_gate, g_up, g_down,
    normed, pre, fin, fin_x, mid, ref_st, tl, dnw,
    idsg, guw, ref_all, headv, rhs, logit, x, rb, ra, units, give, rp,
    vf, vh, lg, st, slot_c, slot_yz, slot_x, both, lse, tw, ls, lc,
    d_x, r0, acc, d_rb, d_ra, d_units, d_give, d_rp, dmid, comb, oc, sc, ox, sx, rg,
    send, recv, hsend, hrecv, local,
):
    me = Place()
    a, b, c, p, f = me.a, me.b, me.c, me.p, me.f
    go = Copies(send, recv)
    plane = [me.on_ab(ring(a, i), ring(b, k)) for k, i in OFFSETS]
    x_peers = [me.partner(), me.neighbour(), me.opposite()]
    across_dp = [me.at(dp=1 - me.dp, y=ring(me.y, k)) for k in (1, 2, 3)]
    vd = headv.at[:, pl.ds(0, 1024)]
    take_proxy = pltpu.make_async_copy(proxy_head, vh, local.at[1])
    greet(plane + x_peers + [me.core()] + across_dp)
    take_head = pltpu.make_async_copy(head, headv, local.at[0])
    take_head.start()
    take_proxy.start()
    own_hid = pl.ds(pl.multiple_of(me.z * 32, 32), 32)
    normed[b, a] = rms_rows(hid[own_hid], gain_in[...]).astype(BF16).reshape(2, 16, 1024)
    s2 = Spread(go, me, lambda bb, aa: normed.at[bb, aa])
    both_ids = jnp.concatenate([targets[...], languages[...]] * 4, axis=0)
    turn = lax.rem(a - me.z + 4, 4)
    turned = both_ids
    for n in (1, 2, 3):
        turned = jnp.where(turn == n, pltpu.roll(both_ids, 32 * n, 1), turned)
    lane_unit = lax.div(lax.broadcasted_iota(jnp.int32, (8, 128), 1), 32)
    idsg[b, a] = jnp.where(lane_unit == a, turned, 0)
    s2_ids = Spread(go, me, lambda bb, aa: idsg.at[bb, aa])
    here = pl.ds(pl.multiple_of(f * 128, 128), 128)

    def weights(ff, to, y=None):
        lanes = pl.ds(pl.multiple_of(ff * 128, 128), 128)
        pieces = [guw.at[ff], dnw.at[:, lanes]]
        if y is None:
            return [go.start(v, v, to) for v in pieces]
        part = pl.ds(pl.multiple_of(y * 128, 128), 128)
        return [
            go.start(gate.at[:, part], guw.at[ff, :, pl.ds(0, 128)], to),
            go.start(up.at[:, part], guw.at[ff, :, pl.ds(128, 128)], to),
            go.start(down.at[part], pieces[1], to),
        ]

    w_sent = {k: weights(f, me.at(y=ring(me.y, k)), ring(me.y, k)) for k in (2, 1, 3)}
    w_core = weights(f, me.core(), me.y)
    part = pl.ds(pl.multiple_of(me.y * 128, 128), 128)
    guw[f, :, 0:128] = gate[:, part]
    guw[f, :, 128:256] = up[:, part]
    dnw[:, here] = down[part]
    ref_all[c, b, a, p] = rms_rows(refh[...], ref_gain[...]).astype(BF16)
    r1 = go.start(ref_all.at[c, b, a, p], ref_all.at[c, b, a, p], me.partner())
    s2.hand_on()
    s2_ids.hand_on()
    r1.wait_recv()
    unit = ref_all.at[c, b, a]
    r2 = [go.start(unit, unit, me.on_a(ring(a, k))) for k in (1, 3, 2)]
    for k in (1, 3, 2):
        for copy in w_sent[k]:
            copy.wait_recv()
        w_core += weights(2 * ring(me.y, 4 - k) + c, me.core())
    for copy in w_core:
        copy.wait_recv()
    collect = Collect(go, me, rb, ra)
    for k in (1, 3, 2, 0):
        bb = s2.row(k)
        h = jnp.dot(
            normed[bb].reshape(128, 1024), guw[...].reshape(1024, 256),
            preferred_element_type=F32,
        )
        pre[bb] = h
        g = h[:, :128]
        h = (g * jax.nn.sigmoid(g) * h[:, 128:]).astype(BF16)
        h = jnp.dot(h, dnw[...], preferred_element_type=F32).astype(BF16)
        x[bb] = h.reshape(4, 32, 1024)
        collect.row((4 - k) % 4, x.at[bb])
    for copy in r2:
        copy.wait_recv()
    right_b, left_b = me.on_b(ring(b, 1)), me.on_b(ring(b, 3))
    unit = ref_all.at[c, b]
    cross = {0: go.start(unit, unit, me.core())}
    r3 = [go.start(unit, unit, right_b), go.start(unit, unit, left_b)]
    for k in (1, 2, 3):
        s2_ids.row(k)
    for bb in range(4):
        row = idsg[bb, 0] + idsg[bb, 1] + idsg[bb, 2] + idsg[bb, 3]
        tl[0, 0, 4 * c + bb] = row[0:1]
        tl[0, 1, 4 * c + bb] = row[1:2]
    mine = pl.ds(4 * c, 4)
    ids_across = [
        go.start(tl.at[0, n, mine], tl.at[0, n, mine], me.core()) for n in range(2)
    ]
    for copy in ids_across:
        copy.wait_recv()
    ids_far = go.start(tl.at[0], tl.at[1], me.neighbour())
    vocab = lax.broadcasted_iota(jnp.int32, (1024, 256), 0) + (f * 8 + me.t) * 1024

    def ref_rows(m):
        b_own, b_far = ring(b, m), ring(a, m)
        rhs[0:128] = ref_all[c, b_own].reshape(128, 4096)
        rhs[128:256] = ref_all[1 - c, b_far].reshape(128, 4096)

        @pl.loop(0, 4)
        def _(n):
            at = pl.ds(pl.multiple_of(n * 256, 256), 256)
            logit[at] = lax.dot_general(
                headv[at], rhs[...], (((1,), (1,)), ((), ())), preferred_element_type=F32
            )

        value = logit[...]
        high = jnp.max(value, axis=0, keepdims=True)
        want = jnp.concatenate([tl[0, 0, 4 * c + b_own], tl[0, 0, 4 * (1 - c) + b_far]], axis=1)
        picked = jnp.sum(jnp.where(vocab == want, value, 0.0), axis=0, keepdims=True)
        total = jnp.sum(jnp.exp(value - high), axis=0, keepdims=True)
        for s, got in enumerate((high, total, picked)):
            ref_st[s, 4 * c + b_own] = got[:, :128]
            ref_st[s, 4 * (1 - c) + b_far] = got[:, 128:]

    take_head.wait()
    cross[0].wait_recv()
    ref_rows(0)
    collect.turn(x.at[b], units)
    give[...] = collect.total(units).astype(BF16)
    swap = go.start(give, rp, me.partner())
    swap.wait_recv()
    middle = hid[own_hid].astype(F32) + (give[...].astype(F32) + rp[...].astype(F32))
    mid[...] = middle
    fin[c, b, a] = rms_rows(middle, gain_out[...]).astype(BF16).reshape(2, 16, 1024)
    f2 = Spread(go, me, lambda bb, aa: fin.at[c, bb, aa])
    f_x = go.start(fin.at[c, b, a], fin_x, me.neighbour())
    f2.hand_on()
    r3[0].wait_recv()
    half = ref_all.at[c, ring(b, 3), pl.ds(0, 2)]
    r4 = [go.start(half, half, right_b)]
    r3[1].wait_recv()
    half = ref_all.at[c, ring(b, 1), pl.ds(2, 2)]
    r4.append(go.start(half, half, left_b))
    for m in (3, 1):
        unit = ref_all.at[c, ring(b, m)]
        cross[m] = go.start(unit, unit, me.core())
    cross[3].wait_recv()
    ref_rows(3)
    f3 = []
    for k in (0, 1, 3, 2):
        row = fin.at[c, f2.row(k)]
        f3.append(go.start(row, row, me.core()))
    for copy in f3 + [f_x, ids_far]:
        copy.wait_recv()
    take_proxy.wait()
    lanes = (((1,), (1,)), ((), ()))
    rows = (((0,), (0,)), ((), ()))
    base = (f * 8 + me.t) * 1024
    tile = lambda n: pl.ds(pl.multiple_of(n * 128, 128), 128)

    def line(v):
        return jnp.concatenate([v(r) for r in range(8)], axis=1)

    def own_rows(n, high):
        logits = lax.dot_general(vh[tile(n)], fin[...].reshape(1024, 1024), lanes, preferred_element_type=F32)
        lg[tile(n)] = logits
        return jnp.maximum(high, jnp.max(logits, axis=0, keepdims=True))

    high = lax.fori_loop(0, 8, own_rows, jnp.full((1, 1024), -jnp.inf, F32))
    for copy in r4:
        copy.wait_recv()
    unit = ref_all.at[c, ring(b, 2)]
    cross[2] = go.start(unit, unit, me.core())
    own_tgt = line(lambda r: tl[0, 0, r])

    def own_sums(n, carry):
        total, picked = carry
        logits = lg[tile(n)]
        vocab = lax.broadcasted_iota(jnp.int32, (128, 1024), 0) + (base + n * 128)
        total += jnp.sum(jnp.exp(logits - high), axis=0, keepdims=True)
        picked += jnp.sum(jnp.where(vocab == own_tgt, logits, 0.0), axis=0, keepdims=True)
        return total, picked

    zero = jnp.zeros((1, 1024), F32)
    total, picked = lax.fori_loop(0, 8, own_sums, (zero, zero))
    cross[1].wait_recv()
    ref_rows(1)
    cross[2].wait_recv()
    ref_rows(2)
    for r in range(8):
        h, q = r // 4, r % 4
        for s in range(3):
            st[h, 4 * s + q : 4 * s + q + 1] = ref_st[s, r]
        for s, v in enumerate((high, total, picked)):
            st[h, 12 + 4 * s + q : 13 + 4 * s + q] = v[:, 128 * r : 128 * (r + 1)]
    slot_c[c] = st[c]
    half = go.start(st.at[1 - c], slot_c.at[c], me.core())
    half.wait_recv()
    yz = me.y * 4 + me.z
    slot_yz[yz] = join_all([slot_c[0], slot_c[1]])
    sent = to_plane(go, me, slot_yz.at[yz])
    vf[c, b, a] = fin_x[...]
    for copy in sent.values():
        copy.wait_recv()
    slot_x[0, p] = join_all([slot_yz[j] for j in range(16)])
    spread = [
        go.start(slot_x.at[0, p], slot_x.at[g, p], to) for g, to in zip((0, 1, 1), x_peers)
    ]
    beside = Spread(go, me, lambda bb, aa: vf.at[c, bb, aa])
    for copy in spread:
        copy.wait_recv()
    both[c, 0] = join_all([slot_x[0, 0], slot_x[0, 1]])
    both[c, 1] = join_all([slot_x[1, 0], slot_x[1, 1]])
    share = go.start(both.at[c], both.at[c], me.core())
    share.wait_recv()
    beside.hand_on()
    excess = [None, None]
    for g in range(2):
        now = [
            jnp.concatenate([both[0, g, 4 * i : 4 * i + 4], both[1, g, 4 * i : 4 * i + 4]])
            for i in range(6)
        ]
        ref_loss = now[0] + jnp.log(now[1]) - now[2]
        proxy_lse = now[3] + jnp.log(now[4])
        lse[8 * g : 8 * g + 8] = proxy_lse
        excess[g] = jnp.maximum(proxy_lse - now[5] - ref_loss, 0.0)
    every = jnp.concatenate([tl[g, 1, r] for g in range(2) for r in range(8)], axis=0)
    for l in range(LANGS):
        here = every == l
        e = jnp.where(here[:8], excess[0], 0.0) + jnp.where(here[8:], excess[1], 0.0)
        n = jnp.where(here[:8], 1.0, 0.0) + jnp.where(here[8:], 1.0, 0.0)
        ls[l : l + 1] = jnp.sum(e, axis=0, keepdims=True)
        lc[l : l + 1] = jnp.sum(n, axis=0, keepdims=True)
    wide = lambda v: jnp.broadcast_to(jnp.sum(v[...], axis=1, keepdims=True), (LANGS, 128))
    count = jnp.maximum(wide(lc), 1.0)
    prior = jnp.broadcast_to(jnp.log(dw[...]), (128, LANGS)).T
    score = prior + STEP_SIZE * (wide(ls) / count)
    score = jnp.exp(score - jnp.max(score, axis=0, keepdims=True))
    mixture = score / jnp.sum(score, axis=0, keepdims=True)
    new = (1.0 - SMOOTHING) * mixture + SMOOTHING / LANGS
    logw[...] = jnp.log(new).T[0:1]
    per_token = new / count * 2048.0
    weight = jnp.zeros(every.shape, F32)
    for l in range(LANGS):
        weight = jnp.where(every == l, per_token[l : l + 1], weight)
    tw[...] = weight
    lse_own, tw_own = line(lambda r: lse[r : r + 1]), line(lambda r: tw[r : r + 1])

    @pl.loop(0, 8)
    def _(n):
        vocab = lax.broadcasted_iota(jnp.int32, (128, 1024), 0) + (base + n * 128)
        hit = jnp.where(vocab == own_tgt, 1.0, 0.0)
        vd[tile(n)] = (tw_own * (jnp.exp(lg[tile(n)] - lse_own) - hit)).astype(BF16)

    def d_rows(cc):
        at = pl.ds(pl.multiple_of(cc * 512, 512), 512)
        part = lax.dot_general(vd[:, at], vh[...], rows, preferred_element_type=F32)
        d_x[cc] = part.astype(BF16).reshape(4, 128, 1024)

    d_rows(1 - c)
    across = {}
    for m in ROWS:
        bb = ring(a, m)
        across[m] = go.start(d_x.at[1 - c, bb], r0.at[bb], me.core())
    d_rows(c)
    collect = Collect(go, me, d_rb, d_ra)
    for m in ROWS:
        bb = ring(b, m)
        across[m].wait_recv()
        joined = d_x[c, bb].astype(F32) + r0[bb].astype(F32)
        acc[bb] = joined.astype(BF16).reshape(acc.shape[1:])
        collect.row(m, acc.at[bb])
    far = []
    for k in (0, 1, 3, 2):
        row = vf.at[c, beside.row(k)]
        far.append(go.start(row, row, me.core()))
    for copy in far:
        copy.wait_recv()
    far_tgt = line(lambda r: tl[1, 0, r])

    def head_rows(n):
        at = tile(n)
        states = vf[...].reshape(1024, 1024)
        logits = lax.dot_general(vh[at], states, lanes, preferred_element_type=F32)
        vocab = lax.broadcasted_iota(jnp.int32, (128, 1024), 0) + (base + n * 128)
        hit = jnp.where(vocab == far_tgt, 1.0, 0.0)
        lse_far = line(lambda r: lse[8 + r : 9 + r])
        tw_far = line(lambda r: tw[8 + r : 9 + r])
        d = (tw_far * (jnp.exp(logits - lse_far) - hit)).astype(BF16)
        grad = jnp.dot(d, states, preferred_element_type=F32)
        grad += jnp.dot(vd[at], fin[...].reshape(1024, 1024), preferred_element_type=F32)
        grad_head[at] = grad.astype(BF16)

    pl.loop(0, 2)(head_rows)
    collect.turn(acc.at[b], d_units)
    pl.loop(2, 4)(head_rows)
    d_give[...] = collect.total(d_units).astype(BF16)
    swap = go.start(d_give, d_rp, me.partner())
    pl.loop(4, 6)(head_rows)
    swap.wait_recv()
    d_final = d_give[...].astype(F32) + d_rp[...].astype(F32)
    middle = mid[...]
    inv = lax.rsqrt(jnp.mean(middle * middle, axis=1, keepdims=True) + EPSILON)
    scaled = d_final * gain_out[...]
    inner = jnp.mean(middle * scaled, axis=1, keepdims=True)
    d_mid = (inv * scaled - middle * inv * inv * inv * inner).astype(BF16)
    dmid[b, a] = d_mid.reshape(2, 16, 1024)
    d2 = Spread(go, me, lambda bb, aa: dmid.at[bb, aa])
    pl.loop(6, 8)(head_rows)
    d2.hand_on()
    h = pre[...].reshape(512, 256)
    g, u = h[:, :128], h[:, 128:]
    s = jax.nn.sigmoid(g)
    act = (g * s * u).astype(BF16)
    gate_slope = u * s * (1.0 + g * (1.0 - s))
    up_slope = g * s
    for k in (1, 3, 2):
        d2.row(k)
    dm = dmid[...].reshape(512, 1024)
    states_in = normed[...].reshape(512, 1024)
    d_act = lax.dot_general(dm, dnw[...], lanes, preferred_element_type=F32)
    for n, (left, right) in enumerate(
        (
            ((d_act * gate_slope).astype(BF16), states_in),
            ((d_act * up_slope).astype(BF16), states_in),
            (act, dm),
        )
    ):
        grad = lax.dot_general(left, right, rows, preferred_element_type=F32).astype(BF16)
        for j in range(8):
            comb[j % 2, j // 2 % 2, j // 4, 128 * n : 128 * (n + 1)] = grad[
                :, 128 * j : 128 * (j + 1)
            ]
    swap = go.start(comb.at[1 - c], oc, me.core())
    swap.wait_recv()
    sc[...] = (comb[c].astype(F32) + oc[...].astype(F32)).astype(BF16)
    swap = go.start(sc.at[1 - me.dp], ox, me.neighbour())
    swap.wait_recv()
    sx[...] = (sc[me.dp].astype(F32) + ox[...].astype(F32)).astype(BF16)
    half, odd = lax.div(me.y, 2), lax.rem(me.y, 2)

    def homeward(e, side, src):
        h = lax.rem(half + e, 2)
        return pltpu.make_async_remote_copy(
            src_ref=sx.at[h],
            dst_ref=rg.at[src],
            send_sem=hsend.at[2 * e + side],
            recv_sem=hrecv.at[src],
            device_id=me.at(dp=1 - me.dp if side else me.dp, y=2 * h + me.dp),
            device_id_type=MESH,
        )

    stays = odd == me.dp
    for e, side in ((1, 1), (1, 0), (0, 1)):
        homeward(e, side, me.y).start()

    @pl.when(jnp.logical_not(stays))
    def _():
        homeward(0, 0, me.y).start()

    @pl.when(stays)
    def _():
        rg[me.y] = sx[half]

    for j in range(4):

        @pl.when(jnp.logical_or(me.y != j, jnp.logical_not(stays)))
        def _(j=j):
            homeward(1, 1, j).wait_recv()

        at = slice(128 * j, 128 * (j + 1))
        got = rg[j].astype(F32)
        g_gate[:, at] = got[0:128].T.astype(BF16)
        g_up[:, at] = got[128:256].T.astype(BF16)
        g_down[at] = rg[j, 256:384]
    for e, side in ((1, 1), (1, 0), (0, 1)):
        homeward(e, side, me.y).wait_send()

    @pl.when(jnp.logical_not(stays))
    def _():
        homeward(0, 0, me.y).wait_send()

    go.drain()


def step(*arrays):
    vmem = pl.BlockSpec(memory_space=pltpu.VMEM)
    hbm = pl.BlockSpec(memory_space=pl.ANY)
    shape = jax.ShapeDtypeStruct
    half = lambda *s: pltpu.VMEM(s, BF16)
    full = lambda *s: pltpu.VMEM(s, F32)
    ints = lambda *s: pltpu.VMEM(s, jnp.int32)
    return pl.pallas_call(
        step_body,
        out_shape=[
            shape((1, LANGS), F32),
            shape((1024, 1024), BF16),
            shape((128, 512), BF16),
            shape((128, 512), BF16),
            shape((512, 128), BF16),
        ],
        in_specs=[vmem] * 11 + [hbm] * 2,
        out_specs=[vmem] * 5,
        scratch_shapes=[
            half(4, 4, 2, 16, 1024),
            full(4, 128, 256),
            half(2, 4, 4, 2, 16, 1024),
            half(2, 16, 1024),
            full(32, 1024),
            full(3, 8, 1, 128),
            ints(2, 2, 8, 1, 128),
            half(128, 1024),
            ints(4, 4, 8, 128),
            half(8, 128, 256),
            half(2, 4, 4, 2, 16, 4096),
            half(1024, 4096),
            half(256, 4096),
            full(1024, 256),
            half(4, 4, 32, 1024),
            half(4, 4, 32, 1024),
            half(4, 32, 1024),
            half(4, 32, 1024),
            half(32, 1024),
            half(32, 1024),
            half(2, 4, 4, 2, 16, 1024),
            half(1024, 1024),
            full(1024, 1024),
            full(2, 24, 128),
            full(2, 24, 128),
            full(16, 24, 128),
            full(2, 2, 24, 128),
            full(2, 2, 24, 128),
            full(16, 128),
            full(16, 128),
            full(LANGS, 128),
            full(LANGS, 128),
            half(2, 4, 128, 1024),
            half(4, 128, 1024),
            half(4, 4, 32, 1024),
            half(4, 4, 32, 1024),
            half(4, 32, 1024),
            half(4, 32, 1024),
            half(32, 1024),
            half(32, 1024),
            half(4, 4, 2, 16, 1024),
            half(2, 2, 2, 384, 128),
            half(2, 2, 384, 128),
            half(2, 2, 384, 128),
            half(2, 384, 128),
            half(2, 384, 128),
            half(4, 384, 128),
            pltpu.SemaphoreType.DMA((200,)),
            pltpu.SemaphoreType.DMA((200,)),
            pltpu.SemaphoreType.DMA((4,)),
            pltpu.SemaphoreType.DMA((4,)),
            pltpu.SemaphoreType.DMA((2,)),
        ],
        compiler_params=pltpu.CompilerParams(
            collective_id=1, has_side_effects=True, vmem_limit_bytes=VMEM_LIMIT * 2**20
        ),
        name="step",
    )(*arrays)


def results_body(*refs):
    n = len(refs) // 2
    for src, dst in zip(refs[:n], refs[n:]):
        dst[...] = src[...].astype(F32)


def results(grads, log_weights):
    steps = 4
    block = lambda v: pl.BlockSpec((v.shape[0] // steps, v.shape[1]), lambda i: (i, 0))
    whole = pl.BlockSpec(log_weights.shape, lambda i: (0, 0))
    specs = [block(g) for g in grads] + [whole]
    arrays = [*grads, log_weights]
    return pl.pallas_call(
        results_body,
        grid=(steps,),
        out_shape=[jax.ShapeDtypeStruct(v.shape, F32) for v in arrays],
        in_specs=specs,
        out_specs=specs,
        compiler_params=pltpu.CompilerParams(vmem_limit_bytes=VMEM_LIMIT * 2**20),
        name="results",
    )(*arrays)


def local(
    ref_hidden,
    proxy_hidden,
    targets,
    languages,
    ref_gain,
    ref_head,
    proxy_gain_in,
    proxy_gain_out,
    gate_weight,
    up_weight,
    down_weight,
    proxy_head,
    domain_weights,
):
    log_weights, grad_head, grad_gate, grad_up, grad_down = step(
        targets[None],
        languages[None],
        proxy_hidden,
        proxy_gain_in[None],
        proxy_gain_out[None],
        ref_hidden,
        ref_gain[None],
        gate_weight,
        up_weight,
        down_weight,
        domain_weights[None],
        ref_head,
        proxy_head,
    )
    grad_gate, grad_up, grad_down, grad_head, log_weights = results(
        (grad_gate, grad_up, grad_down, grad_head), log_weights
    )
    return (log_weights[0], grad_gate, grad_up, grad_down, grad_head)


def solution(mesh):
    in_specs = (
        P(("dp", "fsdp", "tp"), None),
        P(("dp", "fsdp"), None),
        P(("dp", "fsdp")),
        P(("dp", "fsdp")),
        P(),
        P(("fsdp", "tp"), None),
        P(),
        P(),
        P("fsdp", "tp"),
        P("fsdp", "tp"),
        P("tp", "fsdp"),
        P(("fsdp", "tp"), None),
        P(),
    )
    out_specs = (P(), P("fsdp", "tp"), P("fsdp", "tp"), P("tp", "fsdp"), P(("fsdp", "tp"), None))
    return jax.shard_map(local, mesh=mesh, in_specs=in_specs, out_specs=out_specs, check_vma=False)
```
